512 devices in a mesh: dp: 128 (over z, x, core), frame: 4 (over y).
Axes of the slice: x: 4, y: 4, z: 16, core: 2. Of those that a mesh axis runs over, the one named last changes fastest.
Arguments:
- enc_rows: bfloat16 [65536, 512], P(('dp', 'frame')), may hold values from -6 to 6
- dest: int32 [128, 4, 128], P(None, 'frame'), may hold values from 0 to 16383, as said below
- pred_rows: bfloat16 [16384, 512], P(('dp', 'frame')), may hold values from -6 to 6
- label_ids: int32 [128, 128], P('dp'), may hold values from 1 to 499
- block_off: int32 [1024], P(('dp', 'frame')), may hold values from 0 to 64
- band_start: int32 [65536], P(('dp', 'frame')), may hold values from 0 to 61
- w_enc: bfloat16 [512, 512], replicated, may hold values from -0.25 to 0.25
- w_dec: bfloat16 [512, 512], replicated, may hold values from -0.25 to 0.25
- w_out: bfloat16 [512, 500], replicated
- bias_out: float32 [500], replicated, may hold values from -4 to 4
- grad_blank: float32 [65536, 3], P(('dp', 'frame')), may hold values from -6 to 6
- grad_label: float32 [65536, 3], P(('dp', 'frame')), may hold values from -6 to 6
Outputs:
- logprobs: float32 [65536, 6], P(('dp', 'frame'))
- grad_enc: bfloat16 [65536, 512], P(('dp', 'frame'))
- grad_pred: float32 [16384, 512], P(('dp', 'frame'))
- grad_w_out: float32 [512, 500], P(('dp', 'frame'))
The draws below stay inside these ranges and needn't reach their ends.
Inputs may be any that keep to these rules, and one draw needn't show every extreme that they name: For each frame shard f, dest[:, f, :] holds every value 0 to 16383 once; at most 2 rows of one loader shard go to one owner, exactly 2 for some pairs; the rows one loader shard sends one owner take consecutive owner rows, in increasing order of the sending shard.
All inputs are finite; a program needn't handle non-finite values.
Results may differ from the reference program's by a relative error of at most 0.01.
Values may be sent and summed in bfloat16 or wider, within the bound.
No kernel may reach another device: no remote copies, remote signals or barrier semaphores. Data moves between devices by JAX's collectives and lax.ppermute only.
A program may use at most 64 MiB of HBM per device.

```python
import jax
import jax.numpy as jnp
from jax import lax

D = 512
DJ = 512
V = 500
PRUNE = 3
BLOCK = 64
ROWS_DEV = 128
OWNERS = 128
SHARDS = 4
CAP = 2
LABELS = 128
TOTAL_ROWS = 65536
LAB_ALL = 16384
BLOCKS_ALL = 1024


def dest_column(key):
    key_pairs, key_perm, key_order = jax.random.split(key, 3)
    halves = OWNERS // 2
    first_half = jax.random.randint(key_pairs, (halves,), 0, CAP + 1).astype(jnp.int32)
    first_half = first_half.at[0].set(CAP)
    pattern = jnp.concatenate([first_half, CAP - first_half])
    pattern = pattern[jax.random.permutation(key_perm, OWNERS)]
    source_ids = jnp.arange(OWNERS, dtype=jnp.int32)
    pair_counts = pattern[(source_ids[None, :] - source_ids[:, None]) % OWNERS]
    owner_offsets = jnp.cumsum(pair_counts, axis=0) - pair_counts
    group_ends = jnp.cumsum(pair_counts, axis=1)
    group_starts = group_ends - pair_counts
    positions = jnp.arange(ROWS_DEV, dtype=jnp.int32)
    owner_of = jnp.sum((positions[None, :, None] >= group_ends[:, None, :]).astype(jnp.int32), axis=2)
    start_of = jnp.take_along_axis(group_starts, owner_of, axis=1)
    offset_of = jnp.take_along_axis(owner_offsets, owner_of, axis=1)
    ordered = owner_of * ROWS_DEV + offset_of + (positions[None, :] - start_of)
    scores = jax.random.randint(key_order, (OWNERS, ROWS_DEV), 0, 1 << 16).astype(jnp.int32) * ROWS_DEV + positions[None, :]
    shuffle = jnp.argsort(scores, axis=1)
    return jnp.take_along_axis(ordered, shuffle, axis=1)


def draw_dest(key, part):
    column_keys = jax.random.split(jax.random.fold_in(key, 11), SHARDS)
    columns = jax.vmap(dest_column)(column_keys)
    return columns.transpose(1, 0, 2).astype(jnp.int32)


def draw_w_out(key, part):
    key_main = jax.random.fold_in(jax.random.fold_in(key, 23), 0)
    weights = jax.random.normal(key_main, (DJ, V), jnp.float32) * DJ ** (-0.5)
    return weights.astype(jnp.bfloat16)


def plant(values, key, smallest, largest):
    shape = values.shape
    index_at = [jax.random.randint(jax.random.fold_in(key, axis), (), 0, shape[axis]) for axis in range(len(shape))]
    values = values.at[tuple(index_at)].set(smallest)
    longest = shape.index(max(shape))
    index_at[longest] = (index_at[longest] + 1) % shape[longest]
    return values.at[tuple(index_at)].set(largest)


def steps_of(own_key, dims, cuts, low, largest):
    gain, own = 1.0, jax.random.fold_in(own_key, 6)
    for axis_at, shards_of in cuts:
        draws = jnp.exp(jax.random.uniform(jax.random.fold_in(own, axis_at), (shards_of,), jnp.float32, low / len(cuts), largest / len(cuts)))
        gain = gain * jnp.repeat(draws, dims[axis_at] // shards_of).reshape([-1 if axis == axis_at else 1 for axis in range(len(dims))])
    return gain


def centred(rng, extent, deviation, bound, cuts=(), held_as=jnp.bfloat16):
    entries = deviation * jax.random.normal(rng, extent, jnp.float32)
    if cuts:
        entries = entries * steps_of(rng, extent, cuts, -0.22, 0.18)
    return jnp.clip(entries, -bound, bound).astype(held_as)


def setup_inputs(seed: int = 0) -> dict:
    arg_keys = jax.random.split(jax.random.key(seed), 13)
    enc_rows = centred(arg_keys[0], (TOTAL_ROWS, D), 1.0, 6.0, ((0, 512),))
    dest = draw_dest(jax.random.fold_in(arg_keys[12], 71), 0)
    pred_rows = centred(arg_keys[2], (LAB_ALL, D), 1.0, 6.0, ((0, 512),))
    label_ids = plant(jax.random.randint(arg_keys[3], (OWNERS, LABELS), 1, V), jax.random.fold_in(arg_keys[3], 1), 1, V - 1).astype(jnp.int32)
    block_off = plant(jax.random.randint(arg_keys[4], (BLOCKS_ALL,), 0, LABELS - BLOCK + 1), jax.random.fold_in(arg_keys[4], 1), 0, LABELS - BLOCK).astype(jnp.int32)
    band_start = plant(jax.random.randint(arg_keys[5], (TOTAL_ROWS,), 0, BLOCK - PRUNE + 1), jax.random.fold_in(arg_keys[5], 1), 0, BLOCK - PRUNE).astype(jnp.int32)
    w_enc = centred(arg_keys[6], (D, DJ), D ** -0.5, 0.25)
    w_dec = centred(arg_keys[7], (D, DJ), D ** -0.5, 0.25)
    w_out = draw_w_out(jax.random.fold_in(arg_keys[12], 71), 0)
    bias_out = centred(arg_keys[9], (V,), 1.0, 4.0, (), jnp.float32)
    grad_blank = centred(arg_keys[10], (TOTAL_ROWS, PRUNE), 1.0, 6.0, ((0, 512),), jnp.float32)
    grad_label = centred(arg_keys[11], (TOTAL_ROWS, PRUNE), 1.0, 6.0, ((0, 512),), jnp.float32)
    return {"enc_rows": enc_rows, "dest": dest, "pred_rows": pred_rows, "label_ids": label_ids, "block_off": block_off, "band_start": band_start, "w_enc": w_enc, "w_dec": w_dec, "w_out": w_out, "bias_out": bias_out, "grad_blank": grad_blank, "grad_label": grad_label}


def to_columns(array):
    return array.reshape(OWNERS, SHARDS, ROWS_DEV, -1).transpose(1, 0, 2, 3).reshape(SHARDS, OWNERS * ROWS_DEV, -1)


def from_columns(array):
    return array.reshape(SHARDS, OWNERS, ROWS_DEV, -1).transpose(1, 0, 2, 3).reshape(TOTAL_ROWS, -1)


def reference(enc_rows, dest, pred_rows, label_ids, block_off, band_start, w_enc, w_dec, w_out, bias_out, grad_blank, grad_label):
    dest_index = dest.transpose(1, 0, 2).reshape(SHARDS, OWNERS * ROWS_DEV).astype(jnp.int32)
    placed = jax.vmap(lambda values, where_to: jnp.zeros_like(values).at[where_to].set(values))(to_columns(enc_rows), dest_index)
    enc_owned = from_columns(placed)
    enc_joint = jnp.dot(enc_owned, w_enc, preferred_element_type=jnp.float32)
    dec_joint = jnp.dot(pred_rows, w_dec, preferred_element_type=jnp.float32).astype(jnp.bfloat16)
    flat_index = jnp.arange(TOTAL_ROWS, dtype=jnp.int32)
    owner_ids = flat_index // (SHARDS * ROWS_DEV)
    band_base = block_off[flat_index // BLOCK].astype(jnp.int32) + band_start
    label_flat = label_ids.reshape(-1)
    vocab_ids = jnp.arange(V, dtype=jnp.int32)
    enc_grad_j = jnp.zeros((TOTAL_ROWS, DJ), jnp.float32)
    dec_grad_j = jnp.zeros((LAB_ALL, DJ), jnp.float32)
    grad_w_out = jnp.zeros((DJ, V), jnp.float32)
    blank_cols = []
    label_cols = []
    for column in range(PRUNE):
        label_row = (owner_ids * LABELS + band_base + column).astype(jnp.int32)
        emitted = label_flat[label_row]
        hidden = jnp.tanh(enc_joint + dec_joint[label_row].astype(jnp.float32)).astype(jnp.bfloat16)
        logits = jnp.dot(hidden, w_out, preferred_element_type=jnp.float32) + bias_out
        logp = jax.nn.log_softmax(logits, axis=-1)
        blank_cols.append(logp[:, 0])
        label_cols.append(jnp.take_along_axis(logp, emitted[:, None], axis=1)[:, 0])
        cot_blank = grad_blank[:, column][:, None]
        cot_label = grad_label[:, column][:, None]
        dlogit = (cot_blank * (vocab_ids[None, :] == 0) + cot_label * (vocab_ids[None, :] == emitted[:, None])
                  - jnp.exp(logp) * (cot_blank + cot_label)).astype(jnp.bfloat16)
        grad_w_out = grad_w_out + lax.dot_general(hidden, dlogit, (((0,), (0,)), ((), ())), preferred_element_type=jnp.float32)
        back_hidden = lax.dot_general(dlogit, w_out, (((1,), (1,)), ((), ())), preferred_element_type=jnp.float32)
        hidden_f = hidden.astype(jnp.float32)
        dz_term = back_hidden * (1.0 - hidden_f * hidden_f)
        enc_grad_j = enc_grad_j + dz_term
        dec_grad_j = dec_grad_j.at[label_row].add(dz_term)
    logprobs = jnp.stack(blank_cols + label_cols, axis=1)
    owned_grad = lax.dot_general(enc_grad_j.astype(jnp.bfloat16), w_enc, (((1,), (1,)), ((), ())),
                                 preferred_element_type=jnp.float32).astype(jnp.bfloat16)
    taken = jax.vmap(lambda values, where_from: values[where_from])(to_columns(owned_grad), dest_index)
    grad_enc = from_columns(taken)
    grad_pred = jnp.dot(dec_grad_j, w_dec.astype(jnp.float32).T, precision=lax.Precision.HIGHEST)
    return logprobs, grad_enc, grad_pred, grad_w_out
```

```python
import jax
import jax.numpy as jnp
from jax import lax
from jax.experimental import pallas as pl
from jax.experimental.pallas import tpu as pltpu
from jax.sharding import Mesh
from jax.sharding import PartitionSpec as P

F32 = jnp.float32
BF16 = jnp.bfloat16
I32 = jnp.int32

ROWS = 128
PACK = 4
SLOTS = 2
WIRE = ROWS * SLOTS * PACK
KEPT = 3
BLOCK = 64
VPAD = 512
GROUP = 8
CHIPS = 64


def iota(shape, dim):
    return lax.broadcasted_iota(I32, shape, dim)


def mm(a, b):
    return jnp.dot(a, b, preferred_element_type=F32)


def mm_nt(a, b):
    return lax.dot_general(a, b, (((1,), (1,)), ((), ())), preferred_element_type=F32)


def mm_tn(a, b):
    return lax.dot_general(a, b, (((0,), (0,)), ((), ())), preferred_element_type=F32)


def to_bf(mask):
    return jnp.where(mask, 1.0, 0.0).astype(BF16)


def as_column(row):
    square = iota((ROWS, ROWS), 0) == iota((ROWS, ROWS), 1)
    return jnp.sum(jnp.where(square, jnp.broadcast_to(row, (ROWS, ROWS)), 0.0), axis=1, keepdims=True)


def spread(select, rows):
    full = mm(select, rows)
    quarter = iota((WIRE, ROWS), 0) % PACK
    out = full[:, 0:128]
    for c in range(1, PACK):
        out = jnp.where(quarter == c, full[:, c * 128 : (c + 1) * 128], out)
    return out.astype(BF16)


def collapse(select, wire):
    quarter = iota((WIRE, ROWS), 0) % PACK
    parts = [mm(select, wire * to_bf(quarter == c)) for c in range(PACK)]
    return jnp.concatenate(parts, axis=1)


def slot_of(dest_row):
    dest_f = dest_row.astype(F32)
    column = as_column(dest_f)
    follows = (jnp.broadcast_to(column, (ROWS, ROWS)) + 1.0) == jnp.broadcast_to(dest_f, (ROWS, ROWS))
    rank = jnp.sum(jnp.where(follows, 1.0, 0.0), axis=0, keepdims=True)
    rank = jnp.where(dest_row % ROWS == 0, 0.0, rank)
    return (dest_row // ROWS * SLOTS).astype(F32) + rank


def pack_kernel(me_ref, dest_ref, enc_ref, out_ref):
    slot = slot_of(dest_ref[pl.ds(me_ref[0], 1), :])
    wire = (iota((WIRE, ROWS), 0) // PACK).astype(F32)
    out_ref[...] = spread(to_bf(wire == jnp.broadcast_to(slot, (WIRE, ROWS))), enc_ref[...])


def unpack_kernel(me_ref, dest_ref, wire_ref, out_ref):
    slot = as_column(slot_of(dest_ref[pl.ds(me_ref[0], 1), :]))
    wire = (iota((ROWS, WIRE), 1) // PACK).astype(F32)
    out_ref[...] = collapse(to_bf(wire == jnp.broadcast_to(slot, (ROWS, WIRE))), wire_ref[...]).astype(BF16)


def arrival_rows(dest, me):
    mine = to_bf(dest // ROWS == me)
    count = mm_nt(jnp.ones((8, ROWS), BF16), mine).astype(BF16)
    offset = mm(count, to_bf(iota((ROWS, ROWS), 0) < iota((ROWS, ROWS), 1))).astype(BF16)
    expand = to_bf(iota((ROWS, WIRE), 0) == iota((ROWS, WIRE), 1) // (SLOTS * PACK))
    count_j = mm(count, expand)[0:1]
    offset_j = mm(offset, expand)[0:1]
    rank = ((iota((1, WIRE), 1) // PACK) % SLOTS).astype(F32)
    where_to = jnp.where(rank < count_j, offset_j + rank, -1.0)
    return to_bf(jnp.broadcast_to(where_to, (ROWS, WIRE)) == iota((ROWS, WIRE), 0).astype(F32))


def departure_rows(dest, me):
    mine = to_bf(dest // ROWS == me)
    count = mm(mine, jnp.ones((ROWS, ROWS), BF16)).astype(BF16)
    offset = mm(to_bf(iota((ROWS, ROWS), 1) < iota((ROWS, ROWS), 0)), count).astype(BF16)
    expand = to_bf(iota((WIRE, ROWS), 1) == iota((WIRE, ROWS), 0) // (SLOTS * PACK))
    count_j = mm(expand, count)
    offset_j = mm(expand, offset)
    rank = ((iota((WIRE, ROWS), 0) // PACK) % SLOTS).astype(F32)
    where_to = jnp.where(rank < count_j, offset_j + rank, -1.0)
    return to_bf(where_to == iota((WIRE, ROWS), 1).astype(F32))


def base_row(off_ref, start_ref):
    lane = iota((1, ROWS), 1)
    return (start_ref[...] + jnp.where(lane < BLOCK, off_ref[0], off_ref[1])).astype(F32)


def dec_kernel(pred_ref, w_ref, out_ref):
    out_ref[...] = mm(pred_ref[...], w_ref[...]).astype(BF16)


def joint_kernel(
    me_ref, off_ref, dest_ref, wire_ref, dec_ref, label_ref, start_ref, w_enc_ref, w_out_ref, bias_ref,
    cot_blank_ref, cot_label_ref, logprob_ref, hidden_ref, dlogit_ref, grad_ref, wide_ref, bias_wide_ref, term_ref,
):
    vocab = w_out_ref.shape[1]
    wide_ref[...] = jnp.zeros_like(wide_ref)
    wide_ref[:, 0:vocab] = w_out_ref[...]
    bias_wide_ref[...] = jnp.full_like(bias_wide_ref, -1e30)
    bias_wide_ref[:, 0:vocab] = bias_ref[...]
    owned = collapse(arrival_rows(dest_ref[...], me_ref[0]), wire_ref[...]).astype(BF16)
    enc_joint = mm(owned, w_enc_ref[...])
    base = as_column(base_row(off_ref, start_ref))
    position = iota((ROWS, ROWS), 1).astype(F32)
    labels = label_ref[...].astype(F32)
    lane = iota((ROWS, VPAD), 1)
    for k in range(KEPT):
        here = position == base + float(k)
        emitted = jnp.sum(jnp.where(here, labels, 0.0), axis=1, keepdims=True).astype(I32)
        hidden = jnp.tanh(enc_joint + mm(to_bf(here), dec_ref[...])).astype(BF16)
        hidden_ref[k * ROWS : (k + 1) * ROWS, :] = hidden
        logits = mm(hidden, wide_ref[...]) + bias_wide_ref[...]
        shifted = logits - jnp.max(logits, axis=1, keepdims=True)
        power = jnp.exp(shifted)
        total = jnp.sum(power, axis=1, keepdims=True)
        log_total = jnp.log(total)
        is_label = lane == emitted
        at_label = jnp.sum(jnp.where(is_label, shifted, 0.0), axis=1, keepdims=True)
        logprob_ref[:, k : k + 1] = shifted[:, 0:1] - log_total
        logprob_ref[:, KEPT + k : KEPT + k + 1] = at_label - log_total
        cot_blank = cot_blank_ref[:, k : k + 1]
        cot_label = cot_label_ref[:, k : k + 1]
        scale = (cot_blank + cot_label) / total
        direct = jnp.where(is_label, cot_label, 0.0) + jnp.where(lane == 0, cot_blank, 0.0)
        dlogit_ref[k * ROWS : (k + 1) * ROWS, :] = (direct - power * scale).astype(BF16)
    term = mm_tn(hidden_ref[...], dlogit_ref[...])
    for c in range(PACK):
        term_ref[c] = term[:, c * 128 : (c + 1) * 128]
    for b in range(GROUP):
        for c in range(PACK):
            picked = term_ref.at[c][pl.ds(b, CHIPS, stride=GROUP), :]
            grad_ref[b * CHIPS : (b + 1) * CHIPS, c * 128 : (c + 1) * 128] = picked.astype(BF16)


def back_kernel(
    me_ref, off_ref, dest_ref, start_ref, hidden_ref, dlogit_ref, w_enc_ref, w_out_ref, wire_ref, dec_grad_ref, wide_ref
):
    vocab = w_out_ref.shape[1]
    wide_ref[...] = jnp.zeros_like(wide_ref)
    wide_ref[:, 0:vocab] = w_out_ref[...]
    base = base_row(off_ref, start_ref)
    position = iota((ROWS, ROWS), 0).astype(F32)
    enc_grad = jnp.zeros((ROWS, 512), F32)
    dec_grad = jnp.zeros((ROWS, 512), F32)
    for k in range(KEPT):
        rows = slice(k * ROWS, (k + 1) * ROWS)
        hidden = hidden_ref[rows, :].astype(F32)
        dz = mm_nt(dlogit_ref[rows, :], wide_ref[...]) * (1.0 - hidden * hidden)
        enc_grad = enc_grad + dz
        here = to_bf(position == base + float(k))
        high = dz.astype(BF16)
        low = (dz - high.astype(F32)).astype(BF16)
        dec_grad = dec_grad + mm(here, high) + mm(here, low)
    dec_grad_ref[...] = dec_grad.astype(BF16)
    owned = mm_nt(enc_grad.astype(BF16), w_enc_ref[...]).astype(BF16)
    wire_ref[...] = spread(departure_rows(dest_ref[...], me_ref[0]), owned)


def pred_kernel(parts_ref, w_ref, out_ref):
    rows = out_ref.shape[0]
    total = parts_ref[0:rows, :].astype(F32)
    for f in range(1, 4):
        total = total + parts_ref[f * rows : (f + 1) * rows, :].astype(F32)
    high = total.astype(BF16)
    low = (total - high.astype(F32)).astype(BF16)
    out_ref[...] = mm_nt(high, w_ref[...]) + mm_nt(low, w_ref[...])


def chip_sum_kernel(parts_ref, out_ref):
    total = parts_ref[0:CHIPS, :].astype(F32)
    for b in range(1, GROUP):
        total = total + parts_ref[b * CHIPS : (b + 1) * CHIPS, :].astype(F32)
    for c in range(PACK):
        out_ref[pl.ds(c, CHIPS, stride=PACK), :] = total[:, c * 128 : (c + 1) * 128]


def last_sum_kernel(parts_ref, out_ref):
    total = parts_ref[0:8, :]
    for i in range(1, CHIPS * PACK // 8):
        total = total + parts_ref[i * 8 : (i + 1) * 8, :]
    total = total[0:PACK] + total[PACK : 2 * PACK]
    row = jnp.concatenate([total[c : c + 1] for c in range(PACK)], axis=1)
    out_ref[...] = row[:, 0 : out_ref.shape[1]]


VM = pl.BlockSpec(memory_space=pltpu.VMEM)
SM = pl.BlockSpec(memory_space=pltpu.SMEM)


def call(kernel, name, outs, specs, scratch=(), flops=0, bytes_accessed=0):
    return pl.pallas_call(
        kernel,
        name=name,
        out_shape=outs,
        in_specs=list(specs),
        out_specs=jax.tree.map(lambda _: VM, outs),
        scratch_shapes=list(scratch),
        cost_estimate=pl.CostEstimate(flops=flops, bytes_accessed=bytes_accessed, transcendentals=0),
    )


def out(shape, dtype):
    return jax.ShapeDtypeStruct(shape, dtype)


DP = ("z", "x", "core")


def shards(
    enc_rows, dest, pred_rows, label_ids, block_off, band_start, w_enc, w_dec, w_out, bias_out, grad_blank, grad_label
):
    me = lax.axis_index(DP).astype(I32).reshape(1)
    dest = dest.reshape(ROWS, ROWS)
    start = band_start.reshape(1, ROWS)
    bias = bias_out.reshape(1, -1)

    wire = call(pack_kernel, "pack", out((WIRE, ROWS), BF16), [SM, VM, VM], flops=300000000, bytes_accessed=400000)(
        me, dest, enc_rows
    )
    wire = lax.all_to_all(wire, DP, 0, 0, tiled=True)
    dec_own = call(dec_kernel, "dec", out((32, 512), BF16), [VM, VM], flops=20000000, bytes_accessed=600000)(pred_rows, w_dec)
    dec_joint = lax.all_to_all(
        jnp.broadcast_to(dec_own[None], (4, 32, 512)).reshape(ROWS, 512), "frame", 0, 0, tiled=True
    )
    logprobs, hidden, dlogit, term = call(
        joint_kernel,
        "joint",
        (
            out((ROWS, 2 * KEPT), F32),
            out((KEPT * ROWS, 512), BF16),
            out((KEPT * ROWS, VPAD), BF16),
            out((512, VPAD), BF16),
        ),
        [SM, SM] + [VM] * 10,
        [pltpu.VMEM((512, VPAD), BF16), pltpu.VMEM((1, VPAD), F32), pltpu.VMEM((PACK, 512, 128), F32)],
        flops=800000000,
        bytes_accessed=3000000,
    )(me, block_off, dest, wire, dec_joint, label_ids, start, w_enc, w_out, bias, grad_blank, grad_label)
    term = lax.all_to_all(term, ("core", "frame"), 0, 0, tiled=True)
    back, dec_grad = call(
        back_kernel,
        "back",
        (out((WIRE, ROWS), BF16), out((ROWS, 512), BF16)),
        [SM, SM] + [VM] * 6,
        [pltpu.VMEM((512, VPAD), BF16)],
        flops=600000000,
        bytes_accessed=3000000,
    )(me, block_off, dest, start, hidden, dlogit, w_enc, w_out)
    back = lax.all_to_all(back, DP, 0, 0, tiled=True)
    dec_grad = lax.all_to_all(dec_grad, "frame", 0, 0, tiled=True)
    chip_term = call(chip_sum_kernel, "chip_sum", out((CHIPS * PACK, 128), F32), [VM], flops=300000, bytes_accessed=700000)(
        term
    )
    chip_term = lax.all_to_all(chip_term, ("z", "x"), 0, 0, tiled=True)
    grad_pred = call(pred_kernel, "pred", out((32, 512), F32), [VM, VM], flops=40000000, bytes_accessed=700000)(dec_grad, w_dec)
    grad_enc = call(unpack_kernel, "unpack", out((ROWS, 512), BF16), [SM, VM, VM], flops=300000000, bytes_accessed=400000)(
        me, dest, back
    )
    grad_w_out = call(last_sum_kernel, "last_sum", out((1, w_out.shape[1]), F32), [VM], flops=40000, bytes_accessed=140000)(
        chip_term
    )
    return (logprobs, grad_enc, grad_pred, grad_w_out)


def solution(mesh):
    fine = Mesh(mesh.devices.reshape(16, 4, 2, 4), ("z", "x", "core", "frame"))
    every = ("z", "x", "core", "frame")
    return jax.shard_map(
        shards,
        mesh=fine,
        in_specs=(
            P(every, None),
            P(None, "frame", None),
            P(every, None),
            P(DP, None),
            P(every),
            P(every),
            P(),
            P(),
            P(),
            P(),
            P(every, None),
            P(every, None),
        ),
        out_specs=(P(every, None), P(every, None), P(every, None), P(every, None)),
        check_vma=False,
    )
```

```python
import jax
import jax.numpy as jnp
from jax import lax
from jax.experimental import pallas as pl
from jax.experimental.pallas import tpu as pltpu
from jax.sharding import Mesh
from jax.sharding import PartitionSpec as P

F32 = jnp.float32
BF16 = jnp.bfloat16
I32 = jnp.int32

ROWS = 128
PACK = 4
SLOTS = 2
WIDTH = PACK * ROWS
KEPT = 3
BLOCK = 64
FRAMES = 4
PART = ROWS // FRAMES
OUT_ROWS = SLOTS * PACK
BACK_ROWS = OUT_ROWS + PACK


def iota(dim, shape=(ROWS, ROWS)):
    return lax.broadcasted_iota(I32, shape, dim)


def mm(a, b):
    return jnp.dot(a, b, preferred_element_type=F32)


def mm_nt(a, b):
    return lax.dot_general(a, b, (((1,), (1,)), ((), ())), preferred_element_type=F32)


def mm_tn(a, b):
    return lax.dot_general(a, b, (((0,), (0,)), ((), ())), preferred_element_type=F32)


def to_bf(mask):
    return jnp.where(mask, 1.0, 0.0).astype(BF16)


def chunk(c):
    return slice(c * ROWS, (c + 1) * ROWS)


def as_column(row):
    return jnp.sum(jnp.where(iota(0) == iota(1), jnp.broadcast_to(row, (ROWS, ROWS)), 0.0), axis=1, keepdims=True)


def owner_and_rank(dest_row):
    dest_f = dest_row.astype(F32)
    follows = (as_column(dest_f) + 1.0) == jnp.broadcast_to(dest_f, (ROWS, ROWS))
    rank = jnp.sum(jnp.where(follows, 1.0, 0.0), axis=0, keepdims=True)
    return (dest_row // ROWS).astype(F32), jnp.where(dest_row % ROWS == 0, 0.0, rank)


def pack_kernel(id_ref, dest_ref, enc_ref, out_ref, wire_ref):
    owner, rank = owner_and_rank(dest_ref[pl.ds(id_ref[0] // FRAMES, 1), :])
    for k in range(SLOTS):
        picked = mm(to_bf((iota(0).astype(F32) == owner) & (rank == float(k))), enc_ref[...])
        for c in range(PACK):
            wire_ref[pl.ds(k * PACK + c, ROWS, stride=OUT_ROWS), :] = picked[:, chunk(c)]
    out_ref[...] = wire_ref[...].astype(BF16)


def base_row(off_ref, start_ref):
    lane = iota(1, (1, ROWS))
    return (start_ref[...] + jnp.where(lane < BLOCK, off_ref[0], off_ref[1])).astype(F32)


def dec_kernel(pred_ref, w_ref, out_ref):
    out_ref[...] = mm(pred_ref[...], w_ref[...]).astype(BF16)


def prep_kernel(
    id_ref, off_ref, dest_ref, start_ref, label_ref, dec0_ref, dec1_ref, dec2_ref, dec3_ref, w_ref, bias_ref,
    route_ref, dec_ref, label_out_ref, wide_ref, bias_out_ref,
):
    frame = id_ref[0] % FRAMES
    dest = dest_ref[...]
    mine = to_bf(dest // ROWS == id_ref[0] // FRAMES)
    ones = jnp.ones((ROWS, ROWS), BF16)
    count_row = mm_nt(ones, mine)
    count_col = mm(mine, ones)
    offset_row = mm(count_row.astype(BF16), to_bf(iota(0) < iota(1)))
    offset_col = mm(to_bf(iota(1) < iota(0)), count_col.astype(BF16))
    owner, rank = owner_and_rank(dest_ref[pl.ds(id_ref[0] // FRAMES, 1), :])
    owner = as_column(owner)
    rank = as_column(rank)
    down = iota(0).astype(F32)
    along = iota(1).astype(F32)
    for k in range(SLOTS):
        route_ref[k] = to_bf((offset_row + float(k) == down) & (count_row > float(k)))
        route_ref[SLOTS + k] = to_bf((offset_col + float(k) == along) & (count_col > float(k)))
        route_ref[2 * SLOTS + k] = to_bf((owner == along) & (rank == float(k)))
    base = as_column(base_row(off_ref, start_ref))
    labels = label_ref[...].astype(F32)
    dec = jnp.concatenate([dec0_ref[...], dec1_ref[...], dec2_ref[...], dec3_ref[...]], axis=0)
    held = (((frame + FRAMES - iota(1) // PART) % FRAMES) * PART + iota(1) % PART).astype(F32)
    for k in range(KEPT):
        position = base + float(k)
        emitted = jnp.sum(jnp.where(along == position, labels, 0.0), axis=1, keepdims=True)
        label_out_ref[k] = jnp.broadcast_to(emitted, (ROWS, ROWS)).astype(I32)
        dec_ref[k * ROWS : (k + 1) * ROWS, :] = mm(to_bf(held == position), dec).astype(BF16)
    vocab = w_ref.shape[1]
    wide_ref[...] = jnp.zeros_like(wide_ref)
    wide_ref[:, 0:vocab] = w_ref[...]
    bias_out_ref[...] = jnp.full_like(bias_out_ref, -1e30)
    bias_out_ref[:, 0:vocab] = bias_ref[...]


def take_slot(wire_ref, slot, rows):
    return jnp.concatenate([wire_ref[pl.ds(slot * PACK + c, ROWS, stride=rows), :] for c in range(PACK)], axis=1)


def joint_kernel(
    wire_ref, route_ref, dec_ref, label_ref, w_enc_ref, w_out_ref, bias_ref, cot_blank_ref, cot_label_ref,
    logprob_ref, hidden_ref, dlogit_ref, grad_ref, float_ref, term_ref,
):
    float_ref[...] = wire_ref[...].astype(F32)
    owned = jnp.zeros((ROWS, WIDTH), F32)
    for k in range(SLOTS):
        owned = owned + mm(route_ref[k], take_slot(float_ref, k, OUT_ROWS).astype(BF16))
    enc_joint = mm(owned.astype(BF16), w_enc_ref[...])
    lane = iota(1, (ROWS, WIDTH))
    for k in range(KEPT):
        rows = slice(k * ROWS, (k + 1) * ROWS)
        hidden = jnp.tanh(enc_joint + dec_ref[rows, :].astype(F32)).astype(BF16)
        hidden_ref[rows, :] = hidden
        logits = mm(hidden, w_out_ref[...]) + bias_ref[...]
        shifted = logits - jnp.max(logits, axis=1, keepdims=True)
        power = jnp.exp(shifted)
        total = jnp.sum(power, axis=1, keepdims=True)
        log_total = jnp.log(total)
        is_label = lane == label_ref[k][:, 0:1]
        at_label = jnp.sum(jnp.where(is_label, shifted, 0.0), axis=1, keepdims=True)
        logprob_ref[:, k : k + 1] = shifted[:, 0:1] - log_total
        logprob_ref[:, KEPT + k : KEPT + k + 1] = at_label - log_total
        cot_blank = cot_blank_ref[:, k : k + 1]
        cot_label = cot_label_ref[:, k : k + 1]
        scale = (cot_blank + cot_label) / total
        direct = jnp.where(is_label, cot_label, 0.0) + jnp.where(lane == 0, cot_blank, 0.0)
        dlogit_ref[rows, :] = (direct - power * scale).astype(BF16)
    term = mm_tn(hidden_ref[...], dlogit_ref[...])
    for c in range(PACK):
        term_ref[c] = term[:, chunk(c)]
    for f in range(FRAMES):
        for c in range(PACK):
            grad_ref[chunk(f), chunk(c)] = term_ref.at[c][pl.ds(f, ROWS, stride=FRAMES), :].astype(BF16)


def back_kernel(
    id_ref, off_ref, start_ref, route_ref, hidden_ref, dlogit_ref, w_enc_ref, w_out_ref,
    wire_ref, dec0_ref, dec1_ref, dec2_ref, dec3_ref,
):
    base = base_row(off_ref, start_ref)
    frame = id_ref[0] % FRAMES
    sent = (((frame + iota(0) // PART) % FRAMES) * PART + iota(0) % PART).astype(F32)
    enc_grad = jnp.zeros((ROWS, WIDTH), F32)
    dec_grad = jnp.zeros((ROWS, WIDTH), F32)
    for k in range(KEPT):
        rows = slice(k * ROWS, (k + 1) * ROWS)
        hidden = hidden_ref[rows, :].astype(F32)
        dz = mm_nt(dlogit_ref[rows, :], w_out_ref[...]) * (1.0 - hidden * hidden)
        enc_grad = enc_grad + dz
        here = to_bf(sent == base + float(k))
        high = dz.astype(BF16)
        low = (dz - high.astype(F32)).astype(BF16)
        dec_grad = dec_grad + mm(here, high) + mm(here, low)
    dec_grad = dec_grad.astype(BF16)
    for f, ref in enumerate((dec0_ref, dec1_ref, dec2_ref, dec3_ref)):
        ref[...] = dec_grad[f * PART : (f + 1) * PART, :]
    owned = mm_nt(enc_grad.astype(BF16), w_enc_ref[...]).astype(BF16)
    wire_ref[...] = jnp.zeros_like(wire_ref)
    for k in range(SLOTS):
        picked = mm(route_ref[SLOTS + k], owned)
        for c in range(PACK):
            wire_ref[pl.ds(k * PACK + c, ROWS, stride=BACK_ROWS), :] = picked[:, chunk(c)]


def merge_kernel(parts_ref, wire_ref, out_ref, float_ref):
    float_ref[...] = wire_ref[...]
    total = parts_ref[chunk(0), :].astype(F32)
    for f in range(1, FRAMES):
        total = total + parts_ref[chunk(f), :].astype(F32)
    for c in range(PACK):
        float_ref[pl.ds(OUT_ROWS + c, ROWS, stride=BACK_ROWS), :] = total[:, chunk(c)]
    out_ref[...] = float_ref[...].astype(BF16)


def pred_kernel(part0_ref, part1_ref, part2_ref, part3_ref, w_ref, out_ref):
    total = part0_ref[...].astype(F32) + part1_ref[...].astype(F32)
    total = total + (part2_ref[...].astype(F32) + part3_ref[...].astype(F32))
    high = total.astype(BF16)
    low = (total - high.astype(F32)).astype(BF16)
    out_ref[...] = mm_nt(high, w_ref[...]) + mm_nt(low, w_ref[...])


def unpack_kernel(route_ref, wire_ref, enc_ref, grad_ref, float_ref):
    float_ref[...] = wire_ref[...].astype(F32)
    rows = jnp.zeros((ROWS, WIDTH), F32)
    for k in range(SLOTS):
        rows = rows + mm(route_ref[2 * SLOTS + k], take_slot(float_ref, k, BACK_ROWS).astype(BF16))
    enc_ref[...] = rows.astype(BF16)
    term = jnp.sum(take_slot(float_ref, SLOTS, BACK_ROWS), axis=0, keepdims=True)
    grad_ref[...] = term[:, 0 : grad_ref.shape[1]]


VM = pl.BlockSpec(memory_space=pltpu.VMEM)
SM = pl.BlockSpec(memory_space=pltpu.SMEM)


def call(kernel, name, outs, specs, scratch=(), flops=0, bytes_accessed=0):
    return pl.pallas_call(
        kernel,
        name=name,
        out_shape=outs,
        in_specs=list(specs),
        out_specs=jax.tree.map(lambda _: VM, outs),
        scratch_shapes=list(scratch),
        compiler_params=pltpu.CompilerParams(vmem_limit_bytes=24 << 20),
        cost_estimate=pl.CostEstimate(flops=flops, bytes_accessed=bytes_accessed, transcendentals=0),
    )


def out(shape, dtype):
    return jax.ShapeDtypeStruct(shape, dtype)


DP = ("z", "x", "core")
EVERY = DP + ("frame",)


def to_frame(array, ahead):
    return lax.ppermute(array, "frame", [(f, (f + ahead) % FRAMES) for f in range(FRAMES)])


def shards(
    enc_rows, dest, pred_rows, label_ids, block_off, band_start, w_enc, w_dec, w_out, bias_out, grad_blank, grad_label
):
    me = lax.axis_index(EVERY).astype(I32).reshape(1)
    dest = dest.reshape(ROWS, ROWS)
    start = band_start.reshape(1, ROWS)
    bias = bias_out.reshape(1, -1)
    part = out((PART, WIDTH), BF16)

    wire = call(
        pack_kernel,
        "pack",
        out((ROWS * OUT_ROWS, ROWS), BF16),
        [SM, VM, VM],
        [pltpu.VMEM((ROWS * OUT_ROWS, ROWS), F32)],
        flops=40000000,
        bytes_accessed=400000,
    )(me, dest, enc_rows)
    wire, pred_rows = lax.optimization_barrier((wire, pred_rows))
    wire = lax.all_to_all(wire, DP, 0, 0, tiled=True)
    dec = call(dec_kernel, "dec", part, [VM, VM], flops=20000000, bytes_accessed=600000)(pred_rows, w_dec)
    route, dec_rows, emitted, wide, wide_bias = call(
        prep_kernel,
        "prep",
        (
            out((3 * SLOTS, ROWS, ROWS), BF16),
            out((KEPT * ROWS, WIDTH), BF16),
            out((KEPT, ROWS, ROWS), I32),
            out((WIDTH, WIDTH), BF16),
            out((1, WIDTH), F32),
        ),
        [SM, SM] + [VM] * 9,
        flops=100000000,
        bytes_accessed=2000000,
    )(me, block_off, dest, start, label_ids, dec, to_frame(dec, 1), to_frame(dec, 2), to_frame(dec, 3), w_out, bias)
    logprobs, hidden, dlogit, term = call(
        joint_kernel,
        "joint",
        (
            out((ROWS, 2 * KEPT), F32),
            out((KEPT * ROWS, WIDTH), BF16),
            out((KEPT * ROWS, WIDTH), BF16),
            out((WIDTH, WIDTH), BF16),
        ),
        [VM] * 9,
        [pltpu.VMEM((ROWS * OUT_ROWS, ROWS), F32), pltpu.VMEM((PACK, WIDTH, ROWS), F32)],
        flops=500000000,
        bytes_accessed=3000000,
    )(wire, route, dec_rows, emitted, w_enc, wide, wide_bias, grad_blank, grad_label)
    term = lax.all_to_all(term, "frame", 0, 0, tiled=True)
    back, dec0, dec1, dec2, dec3 = call(
        back_kernel,
        "back",
        (out((ROWS * BACK_ROWS, ROWS), F32), part, part, part, part),
        [SM, SM] + [VM] * 6,
        flops=500000000,
        bytes_accessed=3000000,
    )(me, block_off, start, route, hidden, dlogit, w_enc, wide)
    back = call(
        merge_kernel,
        "merge",
        out((ROWS * BACK_ROWS, ROWS), BF16),
        [VM, VM],
        [pltpu.VMEM((ROWS * BACK_ROWS, ROWS), F32)],
        flops=300000,
        bytes_accessed=1700000,
    )(term, back)
    back, dec1, dec2, dec3 = lax.optimization_barrier((back, dec1, dec2, dec3))
    back = lax.all_to_all(back.reshape(ROWS * BACK_ROWS // PACK, PACK, ROWS), DP, 0, 0, tiled=True)
    back = back.reshape(ROWS * BACK_ROWS, ROWS)
    grad_pred = call(pred_kernel, "pred", out((PART, WIDTH), F32), [VM] * 5, flops=40000000, bytes_accessed=700000)(
        dec0, to_frame(dec1, 1), to_frame(dec2, 2), to_frame(dec3, 3), w_dec
    )
    grad_enc, grad_w_out = call(
        unpack_kernel,
        "unpack",
        (out((ROWS, WIDTH), BF16), out((1, w_out.shape[1]), F32)),
        [VM, VM],
        [pltpu.VMEM((ROWS * BACK_ROWS, ROWS), F32)],
        flops=40000000,
        bytes_accessed=600000,
    )(route, back)
    return (logprobs, grad_enc, grad_pred, grad_w_out)


def solution(mesh):
    fine = Mesh(mesh.devices.reshape(16, 4, 2, 4), EVERY)
    return jax.shard_map(
        shards,
        mesh=fine,
        in_specs=(
            P(EVERY, None),
            P(None, "frame", None),
            P(EVERY, None),
            P(DP, None),
            P(EVERY),
            P(EVERY),
            P(),
            P(),
            P(),
            P(),
            P(EVERY, None),
            P(EVERY, None),
        ),
        out_specs=(P(EVERY, None), P(EVERY, None), P(EVERY, None), P(EVERY, None)),
        check_vma=False,
    )
```

```python
import jax
import jax.numpy as jnp
from jax import lax
from jax.experimental import pallas as pl
from jax.experimental.pallas import tpu as pltpu
from jax.sharding import Mesh
from jax.sharding import PartitionSpec as P

F32 = jnp.float32
BF16 = jnp.bfloat16
I32 = jnp.int32

ROWS = 128
PACK = 4
SLOTS = 2
WIDTH = PACK * ROWS
KEPT = 3
BLOCK = 64
FRAMES = 4
PART = ROWS // FRAMES
OUT_ROWS = SLOTS * PACK
HALF = PACK // 2
BACK_ROWS = OUT_ROWS + HALF
CORES = 2


def iota(dim, shape=(ROWS, ROWS)):
    return lax.broadcasted_iota(I32, shape, dim)


def mm(a, b):
    return jnp.dot(a, b, preferred_element_type=F32)


def mm_nt(a, b):
    return lax.dot_general(a, b, (((1,), (1,)), ((), ())), preferred_element_type=F32)


def mm_tn(a, b):
    return lax.dot_general(a, b, (((0,), (0,)), ((), ())), preferred_element_type=F32)


def to_bf(mask):
    return jnp.where(mask, 1.0, 0.0).astype(BF16)


def chunk(c):
    return slice(c * ROWS, (c + 1) * ROWS)


def as_column(row):
    return jnp.sum(jnp.where(iota(0) == iota(1), jnp.broadcast_to(row, (ROWS, ROWS)), 0.0), axis=1, keepdims=True)


def owner_and_rank(dest_row):
    dest_f = dest_row.astype(F32)
    follows = (as_column(dest_f) + 1.0) == jnp.broadcast_to(dest_f, (ROWS, ROWS))
    rank = jnp.sum(jnp.where(follows, 1.0, 0.0), axis=0, keepdims=True)
    return (dest_row // ROWS).astype(F32), jnp.where(dest_row % ROWS == 0, 0.0, rank)


def pack_kernel(id_ref, dest_hbm, enc_hbm, out_ref, dest_ref, enc_ref, wire_ref, sems):
    dest_copy = pltpu.make_async_copy(dest_hbm.at[id_ref[0] // FRAMES], dest_ref, sems.at[0])
    enc_copy = pltpu.make_async_copy(enc_hbm, enc_ref, sems.at[1])
    dest_copy.start()
    enc_copy.start()
    dest_copy.wait()
    owner, rank = owner_and_rank(dest_ref[...])
    down = iota(0).astype(F32)
    picks = [to_bf((down == owner) & (rank == float(k))) for k in range(SLOTS)]
    enc_copy.wait()
    for k in range(SLOTS):
        picked = mm(picks[k], enc_ref[...])
        for c in range(PACK):
            wire_ref[pl.ds(k * PACK + c, ROWS, stride=OUT_ROWS), :] = picked[:, chunk(c)]
    out_ref[...] = wire_ref[...].astype(BF16)


def base_row(off_ref, start_ref):
    lane = iota(1, (1, ROWS))
    return (start_ref[...] + jnp.where(lane < BLOCK, off_ref[0], off_ref[1])).astype(F32)


def dec_kernel(pred_ref, w_ref, out_ref):
    out_ref[...] = mm(pred_ref[...], w_ref[...]).astype(BF16)


def prep_kernel(
    id_ref, off_ref, dest_ref, start_ref, label_ref, w_ref, bias_ref,
    into_ref, from_ref, home_ref, table_ref, wide_ref, bias_out_ref,
):
    dest = dest_ref[...]
    mine = to_bf(dest // ROWS == id_ref[0] // FRAMES)
    ones = jnp.ones((ROWS, ROWS), BF16)
    count_row = mm_nt(ones, mine)
    count_col = mm(mine, ones)
    offset_row = mm(count_row.astype(BF16), to_bf(iota(0) < iota(1)))
    offset_col = mm(to_bf(iota(1) < iota(0)), count_col.astype(BF16))
    owner, rank = owner_and_rank(dest_ref[pl.ds(id_ref[0] // FRAMES, 1), :])
    owner = as_column(owner)
    rank = as_column(rank)
    down = iota(0).astype(F32)
    along = iota(1).astype(F32)
    for k in range(SLOTS):
        into_ref[k] = to_bf((offset_row + float(k) == down) & (count_row > float(k)))
        from_ref[k] = to_bf((offset_col + float(k) == along) & (count_col > float(k)))
        home_ref[k] = to_bf((owner == along) & (rank == float(k)))
    base = as_column(base_row(off_ref, start_ref))
    labels = label_ref[...].astype(F32)
    table = jnp.broadcast_to(base, (ROWS, ROWS))
    for k in range(KEPT):
        emitted = jnp.sum(jnp.where(along == base + float(k), labels, 0.0), axis=1, keepdims=True)
        table = jnp.where(iota(1) == k, emitted, table)
    table_ref[...] = table
    vocab = w_ref.shape[1]
    wide_ref[...] = jnp.zeros_like(wide_ref)
    wide_ref[:, 0:vocab] = w_ref[...]
    bias_out_ref[...] = jnp.full_like(bias_out_ref, -1e30)
    bias_out_ref[:, 0:vocab] = bias_ref[...]


def take_slot(wire_ref, slot, rows):
    return jnp.concatenate([wire_ref[pl.ds(slot * PACK + c, ROWS, stride=rows), :] for c in range(PACK)], axis=1)


def joint_kernel(
    id_ref, wire_ref, into_ref, near_ref, far_ref, table_ref, w_enc_ref, w_out_ref, bias_ref, cot_blank_ref,
    cot_label_ref, logprob_ref, hidden_ref, dlogit_ref, grad_ref, float_ref, term_ref,
):
    float_ref[...] = wire_ref[...].astype(F32)
    owned = jnp.zeros((ROWS, WIDTH), F32)
    for k in range(SLOTS):
        owned = owned + mm(into_ref[k], take_slot(float_ref, k, OUT_ROWS).astype(BF16))
    enc_joint = mm(owned.astype(BF16), w_enc_ref[...])
    frame = id_ref[0] % FRAMES
    held = (((frame + FRAMES - iota(1) // PART) % FRAMES) * PART + iota(1) % PART).astype(F32)
    dec = jnp.concatenate([near_ref[...], far_ref[...]], axis=0)
    base = table_ref[:, KEPT : KEPT + 1]
    lane = iota(1, (ROWS, WIDTH))
    for k in range(KEPT):
        rows = slice(k * ROWS, (k + 1) * ROWS)
        dec_rows = mm(to_bf(held == base + float(k)), dec)
        hidden = jnp.tanh(enc_joint + dec_rows).astype(BF16)
        hidden_ref[rows, :] = hidden
        logits = mm(hidden, w_out_ref[...]) + bias_ref[...]
        shifted = logits - jnp.max(logits, axis=1, keepdims=True)
        power = jnp.exp(shifted)
        total = jnp.sum(power, axis=1, keepdims=True)
        log_total = jnp.log(total)
        is_label = lane == table_ref[:, k : k + 1].astype(I32)
        at_label = jnp.sum(jnp.where(is_label, shifted, 0.0), axis=1, keepdims=True)
        logprob_ref[:, k : k + 1] = shifted[:, 0:1] - log_total
        logprob_ref[:, KEPT + k : KEPT + k + 1] = at_label - log_total
        cot_blank = cot_blank_ref[:, k : k + 1]
        cot_label = cot_label_ref[:, k : k + 1]
        scale = (cot_blank + cot_label) / total
        direct = jnp.where(is_label, cot_label, 0.0) + jnp.where(lane == 0, cot_blank, 0.0)
        dlogit_ref[rows, :] = (direct - power * scale).astype(BF16)
    term = mm_tn(hidden_ref[...], dlogit_ref[...])
    for c in range(PACK):
        term_ref[c] = term[:, chunk(c)]
    for core in range(CORES):
        for f in range(FRAMES):
            for h in range(HALF):
                picked = term_ref.at[core * HALF + h][pl.ds(f, ROWS, stride=FRAMES), :]
                grad_ref[chunk(core * FRAMES + f), chunk(h)] = picked.astype(BF16)


def back_kernel(
    id_ref, off_ref, start_ref, from_ref, hidden_ref, dlogit_ref, w_enc_ref, w_out_ref,
    plane_ref, dec0_ref, dec1_ref, dec2_ref, dec3_ref,
):
    base = base_row(off_ref, start_ref)
    frame = id_ref[0] % FRAMES
    sent = (((frame + iota(0) // PART) % FRAMES) * PART + iota(0) % PART).astype(F32)
    enc_grad = jnp.zeros((ROWS, WIDTH), F32)
    dec_grad = jnp.zeros((ROWS, WIDTH), F32)
    for k in range(KEPT):
        rows = slice(k * ROWS, (k + 1) * ROWS)
        hidden = hidden_ref[rows, :].astype(F32)
        dz = mm_nt(dlogit_ref[rows, :], w_out_ref[...]) * (1.0 - hidden * hidden)
        enc_grad = enc_grad + dz
        here = to_bf(sent == base + float(k))
        high = dz.astype(BF16)
        low = (dz - high.astype(F32)).astype(BF16)
        dec_grad = dec_grad + mm(here, high) + mm(here, low)
    dec_grad = dec_grad.astype(BF16)
    for f, ref in enumerate((dec0_ref, dec1_ref, dec2_ref, dec3_ref)):
        ref[...] = dec_grad[f * PART : (f + 1) * PART, :]
    owned = mm_nt(enc_grad.astype(BF16), w_enc_ref[...]).astype(BF16)
    for k in range(SLOTS):
        plane_ref[chunk(k), :] = mm(from_ref[k], owned).astype(BF16)


def merge_kernel(parts_ref, plane_ref, out_ref, float_ref):
    for k in range(SLOTS):
        for c in range(PACK):
            plane = plane_ref[chunk(k), chunk(c)].astype(F32)
            float_ref[pl.ds(k * PACK + c, ROWS, stride=BACK_ROWS), :] = plane
    for h in range(HALF):
        total = parts_ref[chunk(0), chunk(h)].astype(F32)
        for i in range(1, CORES * FRAMES):
            total = total + parts_ref[chunk(i), chunk(h)].astype(F32)
        float_ref[pl.ds(OUT_ROWS + h, ROWS, stride=BACK_ROWS), :] = total
    out_ref[...] = float_ref[...].astype(BF16)


def pred_kernel(part0_ref, part1_ref, part2_ref, part3_ref, w_ref, out_ref):
    total = part0_ref[...].astype(F32) + part1_ref[...].astype(F32)
    total = total + (part2_ref[...].astype(F32) + part3_ref[...].astype(F32))
    high = total.astype(BF16)
    low = (total - high.astype(F32)).astype(BF16)
    out_ref[...] = mm_nt(high, w_ref[...]) + mm_nt(low, w_ref[...])


def unpack_kernel(home_ref, wire_ref, enc_ref, grad_ref, float_ref):
    float_ref[...] = wire_ref[...].astype(F32)
    rows = jnp.zeros((ROWS, WIDTH), F32)
    for k in range(SLOTS):
        rows = rows + mm(home_ref[k], take_slot(float_ref, k, BACK_ROWS).astype(BF16))
    enc_ref[...] = rows.astype(BF16)
    quarters = []
    for core in range(CORES):
        for h in range(HALF):
            first = core * BACK_ROWS + OUT_ROWS + h
            from_core = float_ref[pl.ds(first, ROWS // CORES, stride=CORES * BACK_ROWS), :]
            quarters.append(jnp.sum(from_core, axis=0, keepdims=True))
    term = jnp.concatenate(quarters, axis=1)
    grad_ref[...] = term[:, 0 : grad_ref.shape[1]]


VM = pl.BlockSpec(memory_space=pltpu.VMEM)
SM = pl.BlockSpec(memory_space=pltpu.SMEM)
HBM = pl.BlockSpec(memory_space=pltpu.HBM)


def call(kernel, name, outs, specs, scratch=(), flops=0, bytes_accessed=0, limit=24 << 20):
    return pl.pallas_call(
        kernel,
        name=name,
        out_shape=outs,
        in_specs=list(specs),
        out_specs=jax.tree.map(lambda _: VM, outs),
        scratch_shapes=list(scratch),
        compiler_params=pltpu.CompilerParams(vmem_limit_bytes=limit),
        cost_estimate=pl.CostEstimate(flops=flops, bytes_accessed=bytes_accessed, transcendentals=0),
    )


def out(shape, dtype):
    return jax.ShapeDtypeStruct(shape, dtype)


DP = ("z", "x", "core")
EVERY = DP + ("frame",)


def to_frame(array, ahead):
    return lax.ppermute(array, "frame", [(f, (f + ahead) % FRAMES) for f in range(FRAMES)])


def shards(
    enc_rows, dest, pred_rows, label_ids, block_off, band_start, w_enc, w_dec, w_out, bias_out, grad_blank, grad_label
):
    me = lax.axis_index(EVERY).astype(I32).reshape(1)
    flat_dest = dest.reshape(ROWS, ROWS)
    start = band_start.reshape(1, ROWS)
    bias = bias_out.reshape(1, -1)
    part = out((PART, WIDTH), BF16)
    pick = out((SLOTS, ROWS, ROWS), BF16)

    wire = call(
        pack_kernel,
        "pack",
        out((ROWS * OUT_ROWS, ROWS), BF16),
        [SM, HBM, HBM],
        [
            pltpu.VMEM((1, ROWS), I32),
            pltpu.VMEM((ROWS, WIDTH), BF16),
            pltpu.VMEM((ROWS * OUT_ROWS, ROWS), F32),
            pltpu.SemaphoreType.DMA((2,)),
        ],
        flops=40000000,
        bytes_accessed=400000,
        limit=None,
    )(me, dest, enc_rows)
    wire, pred_rows = lax.optimization_barrier((wire, pred_rows))
    wire = lax.all_to_all(wire, DP, 0, 0, tiled=True)
    dec = call(dec_kernel, "dec", part, [VM, VM], flops=20000000, bytes_accessed=600000, limit=None)(pred_rows, w_dec)
    near = jnp.concatenate([dec, to_frame(dec, 1)], axis=0)
    far = to_frame(near, 2)
    into, out_of, home, table, wide, wide_bias = call(
        prep_kernel,
        "prep",
        (pick, pick, pick, out((ROWS, ROWS), F32), out((WIDTH, WIDTH), BF16), out((1, WIDTH), F32)),
        [SM, SM] + [VM] * 5,
        flops=100000000,
        bytes_accessed=2000000,
    )(me, block_off, flat_dest, start, label_ids, w_out, bias)
    logprobs, hidden, dlogit, term = call(
        joint_kernel,
        "joint",
        (
            out((ROWS, 2 * KEPT), F32),
            out((KEPT * ROWS, WIDTH), BF16),
            out((KEPT * ROWS, WIDTH), BF16),
            out((CORES * WIDTH, WIDTH // CORES), BF16),
        ),
        [SM] + [VM] * 10,
        [pltpu.VMEM((ROWS * OUT_ROWS, ROWS), F32), pltpu.VMEM((PACK, WIDTH, ROWS), F32)],
        flops=500000000,
        bytes_accessed=3000000,
    )(me, wire, into, near, far, table, w_enc, wide, wide_bias, grad_blank, grad_label)
    term = lax.all_to_all(term, ("core", "frame"), 0, 0, tiled=True)
    planes, dec0, dec1, dec2, dec3 = call(
        back_kernel,
        "back",
        (out((SLOTS * ROWS, WIDTH), BF16), part, part, part, part),
        [SM, SM] + [VM] * 6,
        flops=500000000,
        bytes_accessed=3000000,
    )(me, block_off, start, out_of, hidden, dlogit, w_enc, wide)
    back = call(
        merge_kernel,
        "merge",
        out((ROWS * BACK_ROWS, ROWS), BF16),
        [VM, VM],
        [pltpu.VMEM((ROWS * BACK_ROWS, ROWS), F32)],
        flops=300000,
        bytes_accessed=1700000,
    )(term, planes)
    back, dec1, dec2, dec3 = lax.optimization_barrier((back, dec1, dec2, dec3))
    back = lax.all_to_all(back.reshape(ROWS * BACK_ROWS // 2, 2, ROWS), DP, 0, 0, tiled=True)
    back = back.reshape(ROWS * BACK_ROWS, ROWS)
    grad_pred = call(
        pred_kernel,
        "pred",
        out((PART, WIDTH), F32),
        [VM] * 5,
        flops=40000000,
        bytes_accessed=700000,
    )(dec0, to_frame(dec1, 1), to_frame(dec2, 2), to_frame(dec3, 3), w_dec)
    grad_enc, grad_w_out = call(
        unpack_kernel,
        "unpack",
        (out((ROWS, WIDTH), BF16), out((1, w_out.shape[1]), F32)),
        [VM, VM],
        [pltpu.VMEM((ROWS * BACK_ROWS, ROWS), F32)],
        flops=40000000,
        bytes_accessed=600000,
    )(home, back)
    return (logprobs, grad_enc, grad_pred, grad_w_out)


def solution(mesh):
    fine = Mesh(mesh.devices.reshape(16, 4, 2, 4), EVERY)
    return jax.shard_map(
        shards,
        mesh=fine,
        in_specs=(
            P(EVERY, None),
            P(None, "frame", None),
            P(EVERY, None),
            P(DP, None),
            P(EVERY),
            P(EVERY),
            P(),
            P(),
            P(),
            P(),
            P(EVERY, None),
            P(EVERY, None),
        ),
        out_specs=(P(EVERY, None), P(EVERY, None), P(EVERY, None), P(EVERY, None)),
        check_vma=False,
    )
```

```python
import jax
import jax.numpy as jnp
from jax import lax
from jax.experimental import pallas as pl
from jax.experimental.pallas import tpu as pltpu
from jax.sharding import Mesh
from jax.sharding import PartitionSpec as P

F32 = jnp.float32
BF16 = jnp.bfloat16
I32 = jnp.int32

ROWS = 128
PACK = 4
SLOTS = 2
WIDTH = PACK * ROWS
KEPT = 3
BLOCK = 64
FRAMES = 4
PART = ROWS // FRAMES
OUT_ROWS = SLOTS * PACK
HALF = PACK // 2
BACK_ROWS = OUT_ROWS + HALF
CORES = 2


def iota(dim, shape=(ROWS, ROWS)):
    return lax.broadcasted_iota(I32, shape, dim)


def mm(a, b):
    return jnp.dot(a, b, preferred_element_type=F32)


def mm_nt(a, b):
    return lax.dot_general(a, b, (((1,), (1,)), ((), ())), preferred_element_type=F32)


def mm_tn(a, b):
    return lax.dot_general(a, b, (((0,), (0,)), ((), ())), preferred_element_type=F32)


def to_bf(mask):
    return jnp.where(mask, 1.0, 0.0).astype(BF16)


def chunk(c):
    return slice(c * ROWS, (c + 1) * ROWS)


def as_column(row):
    return jnp.sum(jnp.where(iota(0) == iota(1), jnp.broadcast_to(row, (ROWS, ROWS)), 0.0), axis=1, keepdims=True)


def as_row(column):
    return jnp.sum(jnp.where(iota(0) == iota(1), jnp.broadcast_to(column, (ROWS, ROWS)), 0.0), axis=0, keepdims=True)


def owner_and_rank(dest_row):
    dest_f = dest_row.astype(F32)
    follows = (as_column(dest_f) + 1.0) == jnp.broadcast_to(dest_f, (ROWS, ROWS))
    rank = jnp.sum(jnp.where(follows, 1.0, 0.0), axis=0, keepdims=True)
    return (dest_row // ROWS).astype(F32), jnp.where(dest_row % ROWS == 0, 0.0, rank)


def pack_kernel(id_ref, dest_hbm, enc_hbm, pred_hbm, w_hbm, out_ref, dec_ref, dest_ref, enc_ref, pred_ref, w_ref, wire_ref, sems):
    pairs = ((dest_hbm.at[id_ref[0] // FRAMES], dest_ref), (enc_hbm, enc_ref), (pred_hbm, pred_ref), (w_hbm, w_ref))
    copies = [pltpu.make_async_copy(src, dst, sems.at[i]) for i, (src, dst) in enumerate(pairs)]
    for copy in copies:
        copy.start()
    copies[0].wait()
    owner, rank = owner_and_rank(dest_ref[...])
    down = iota(0).astype(F32)
    picks = [to_bf((down == owner) & (rank == float(k))) for k in range(SLOTS)]
    copies[1].wait()
    for k in range(SLOTS):
        picked = mm(picks[k], enc_ref[...])
        for c in range(PACK):
            wire_ref[pl.ds(k * PACK + c, ROWS, stride=OUT_ROWS), :] = picked[:, chunk(c)]
    out_ref[...] = wire_ref[...].astype(BF16)
    copies[2].wait()
    copies[3].wait()
    dec_ref[...] = mm(pred_ref[...], w_ref[...]).astype(BF16)


def base_row(off_ref, start_ref):
    lane = iota(1, (1, ROWS))
    return (start_ref[...] + jnp.where(lane < BLOCK, off_ref[0], off_ref[1])).astype(F32)


def prep_kernel(
    id_ref, off_ref, dest_ref, start_ref, label_ref, w_ref, bias_ref,
    into_ref, from_ref, home_ref, table_ref, wide_ref, bias_out_ref,
):
    dest = dest_ref[...]
    mine = to_bf(dest // ROWS == id_ref[0] // FRAMES)
    ones = jnp.ones((ROWS, ROWS), BF16)
    count_row = mm_nt(ones, mine)
    count_col = mm(mine, ones)
    offset_row = mm(count_row.astype(BF16), to_bf(iota(0) < iota(1)))
    offset_col = mm(to_bf(iota(1) < iota(0)), count_col.astype(BF16))
    owner, rank = owner_and_rank(dest_ref[pl.ds(id_ref[0] // FRAMES, 1), :])
    owner = as_column(owner)
    rank = as_column(rank)
    down = iota(0).astype(F32)
    along = iota(1).astype(F32)
    for k in range(SLOTS):
        into_ref[k] = to_bf((offset_row + float(k) == down) & (count_row > float(k)))
        from_ref[k] = to_bf((offset_col + float(k) == along) & (count_col > float(k)))
        home_ref[k] = to_bf((owner == along) & (rank == float(k)))
    base = as_column(base_row(off_ref, start_ref))
    labels = label_ref[...].astype(F32)
    table = jnp.broadcast_to(base, (ROWS, ROWS))
    for k in range(KEPT):
        emitted = jnp.sum(jnp.where(along == base + float(k), labels, 0.0), axis=1, keepdims=True)
        table = jnp.where(iota(1) == k, emitted, table)
    table_ref[...] = table
    vocab = w_ref.shape[1]
    wide_ref[...] = jnp.zeros_like(wide_ref)
    wide_ref[:, 0:vocab] = w_ref[...]
    bias_out_ref[...] = jnp.full_like(bias_out_ref, -1e30)
    bias_out_ref[:, 0:vocab] = bias_ref[...]


def take_slot(wire_ref, slot, rows):
    return jnp.concatenate([wire_ref[pl.ds(slot * PACK + c, ROWS, stride=rows), :] for c in range(PACK)], axis=1)


def joint_kernel(
    id_ref, wire_ref, into_ref, dec0_ref, dec1_ref, dec2_ref, dec3_ref, table_ref, w_enc_ref, w_out_ref, bias_ref, cot_blank_ref,
    cot_label_ref, logprob_ref, hidden_ref, dlogit_ref, grad_ref, float_ref, term_ref,
):
    float_ref[...] = wire_ref[...].astype(F32)
    owned = jnp.zeros((ROWS, WIDTH), F32)
    for k in range(SLOTS):
        owned = owned + mm(into_ref[k], take_slot(float_ref, k, OUT_ROWS).astype(BF16))
    enc_joint = mm(owned.astype(BF16), w_enc_ref[...])
    frame = id_ref[0] % FRAMES
    held = (((frame + FRAMES - iota(1) // PART) % FRAMES) * PART + iota(1) % PART).astype(F32)
    dec = jnp.concatenate([dec0_ref[...], dec1_ref[...], dec2_ref[...], dec3_ref[...]], axis=0)
    base = table_ref[:, KEPT : KEPT + 1]
    lane = iota(1, (ROWS, WIDTH))
    for k in range(KEPT):
        rows = slice(k * ROWS, (k + 1) * ROWS)
        dec_rows = mm(to_bf(held == base + float(k)), dec)
        hidden = jnp.tanh(enc_joint + dec_rows).astype(BF16)
        hidden_ref[rows, :] = hidden
        logits = mm(hidden, w_out_ref[...]) + bias_ref[...]
        shifted = logits - jnp.max(logits, axis=1, keepdims=True)
        power = jnp.exp(shifted)
        total = jnp.sum(power, axis=1, keepdims=True)
        log_total = jnp.log(total)
        is_label = lane == table_ref[:, k : k + 1].astype(I32)
        at_label = jnp.sum(jnp.where(is_label, shifted, 0.0), axis=1, keepdims=True)
        logprob_ref[:, k : k + 1] = shifted[:, 0:1] - log_total
        logprob_ref[:, KEPT + k : KEPT + k + 1] = at_label - log_total
        cot_blank = cot_blank_ref[:, k : k + 1]
        cot_label = cot_label_ref[:, k : k + 1]
        scale = (cot_blank + cot_label) / total
        direct = jnp.where(is_label, cot_label, 0.0) + jnp.where(lane == 0, cot_blank, 0.0)
        dlogit_ref[rows, :] = (direct - power * scale).astype(BF16)
    term = mm_tn(hidden_ref[...], dlogit_ref[...])
    for c in range(PACK):
        term_ref[c] = term[:, chunk(c)]
    for core in range(CORES):
        for f in range(FRAMES):
            for h in range(HALF):
                picked = term_ref.at[core * HALF + h][pl.ds(f, ROWS, stride=FRAMES), :]
                grad_ref[chunk(core * FRAMES + f), chunk(h)] = picked.astype(BF16)


def back_kernel(
    id_ref, off_ref, start_ref, from_ref, hidden_ref, dlogit_ref, w_enc_ref, w_out_ref, logprob_ref,
    row_ref, plane_ref, dec0_ref, dec1_ref, dec2_ref, dec3_ref,
):
    for i in range(2 * KEPT):
        row_ref[i : i + 1, :] = as_row(logprob_ref[:, i : i + 1])
    base = base_row(off_ref, start_ref)
    frame = id_ref[0] % FRAMES
    sent = (((frame + iota(0) // PART) % FRAMES) * PART + iota(0) % PART).astype(F32)
    enc_grad = jnp.zeros((ROWS, WIDTH), F32)
    dec_grad = jnp.zeros((ROWS, WIDTH), F32)
    for k in range(KEPT):
        rows = slice(k * ROWS, (k + 1) * ROWS)
        hidden = hidden_ref[rows, :].astype(F32)
        dz = mm_nt(dlogit_ref[rows, :], w_out_ref[...]) * (1.0 - hidden * hidden)
        enc_grad = enc_grad + dz
        here = to_bf(sent == base + float(k))
        high = dz.astype(BF16)
        low = (dz - high.astype(F32)).astype(BF16)
        dec_grad = dec_grad + mm(here, high) + mm(here, low)
    dec_grad = dec_grad.astype(BF16)
    for f, ref in enumerate((dec0_ref, dec1_ref, dec2_ref, dec3_ref)):
        ref[...] = dec_grad[f * PART : (f + 1) * PART, :]
    owned = mm_nt(enc_grad.astype(BF16), w_enc_ref[...]).astype(BF16)
    for k in range(SLOTS):
        plane_ref[chunk(k), :] = mm(from_ref[k], owned).astype(BF16)


def merge_kernel(parts_ref, plane_ref, out_ref, float_ref):
    for k in range(SLOTS):
        for c in range(PACK):
            plane = plane_ref[chunk(k), chunk(c)].astype(F32)
            float_ref[pl.ds(k * PACK + c, ROWS, stride=BACK_ROWS), :] = plane
    for h in range(HALF):
        total = parts_ref[chunk(0), chunk(h)].astype(F32)
        for i in range(1, CORES * FRAMES):
            total = total + parts_ref[chunk(i), chunk(h)].astype(F32)
        float_ref[pl.ds(OUT_ROWS + h, ROWS, stride=BACK_ROWS), :] = total
    out_ref[...] = float_ref[...].astype(BF16)


def pred_kernel(part0_ref, part1_ref, part2_ref, part3_ref, w_ref, out_ref):
    total = part0_ref[...].astype(F32) + part1_ref[...].astype(F32)
    total = total + (part2_ref[...].astype(F32) + part3_ref[...].astype(F32))
    high = total.astype(BF16)
    low = (total - high.astype(F32)).astype(BF16)
    out_ref[...] = mm_nt(high, w_ref[...]) + mm_nt(low, w_ref[...])


def unpack_kernel(home_ref, wire_ref, enc_ref, grad_ref, float_ref):
    float_ref[...] = wire_ref[...].astype(F32)
    rows = jnp.zeros((ROWS, WIDTH), F32)
    for k in range(SLOTS):
        rows = rows + mm(home_ref[k], take_slot(float_ref, k, BACK_ROWS).astype(BF16))
    enc_ref[...] = rows.astype(BF16)
    quarters = []
    for core in range(CORES):
        for h in range(HALF):
            first = core * BACK_ROWS + OUT_ROWS + h
            from_core = float_ref[pl.ds(first, ROWS // CORES, stride=CORES * BACK_ROWS), :]
            quarters.append(jnp.sum(from_core, axis=0, keepdims=True))
    term = jnp.concatenate(quarters, axis=1)
    grad_ref[...] = term[:, 0 : grad_ref.shape[1]]


VM = pl.BlockSpec(memory_space=pltpu.VMEM)
SM = pl.BlockSpec(memory_space=pltpu.SMEM)
HBM = pl.BlockSpec(memory_space=pltpu.HBM)


def call(kernel, name, outs, specs, scratch=(), flops=0, bytes_accessed=0, limit=24 << 20):
    return pl.pallas_call(
        kernel,
        name=name,
        out_shape=outs,
        in_specs=list(specs),
        out_specs=jax.tree.map(lambda _: VM, outs),
        scratch_shapes=list(scratch),
        compiler_params=pltpu.CompilerParams(vmem_limit_bytes=limit),
        cost_estimate=pl.CostEstimate(flops=flops, bytes_accessed=bytes_accessed, transcendentals=0),
    )


def out(shape, dtype):
    return jax.ShapeDtypeStruct(shape, dtype)


DP = ("z", "x", "core")
EVERY = DP + ("frame",)


def to_frame(array, ahead):
    return lax.ppermute(array, "frame", [(f, (f + ahead) % FRAMES) for f in range(FRAMES)])


def shards(
    enc_rows, dest, pred_rows, label_ids, block_off, band_start, w_enc, w_dec, w_out, bias_out, grad_blank, grad_label
):
    me = lax.axis_index(EVERY).astype(I32).reshape(1)
    flat_dest = dest.reshape(ROWS, ROWS)
    start = band_start.reshape(1, ROWS)
    bias = bias_out.reshape(1, -1)
    part = out((PART, WIDTH), BF16)
    pick = out((SLOTS, ROWS, ROWS), BF16)

    wire, dec = call(
        pack_kernel,
        "pack",
        (out((ROWS * OUT_ROWS, ROWS), BF16), part),
        [SM, HBM, HBM, HBM, HBM],
        [
            pltpu.VMEM((1, ROWS), I32),
            pltpu.VMEM((ROWS, WIDTH), BF16),
            pltpu.VMEM((PART, WIDTH), BF16),
            pltpu.VMEM((WIDTH, WIDTH), BF16),
            pltpu.VMEM((ROWS * OUT_ROWS, ROWS), F32),
            pltpu.SemaphoreType.DMA((4,)),
        ],
        flops=40000000,
        bytes_accessed=400000,
        limit=None,
    )(me, dest, enc_rows, pred_rows, w_dec)
    wire = lax.all_to_all(wire, DP, 0, 0, tiled=True)
    into, out_of, home, table, wide, wide_bias = call(
        prep_kernel,
        "prep",
        (pick, pick, pick, out((ROWS, ROWS), F32), out((WIDTH, WIDTH), BF16), out((1, WIDTH), F32)),
        [SM, SM] + [VM] * 5,
        flops=100000000,
        bytes_accessed=2000000,
    )(me, block_off, flat_dest, start, label_ids, w_out, bias)
    logprobs, hidden, dlogit, term = call(
        joint_kernel,
        "joint",
        (
            out((ROWS, 2 * KEPT), F32),
            out((KEPT * ROWS, WIDTH), BF16),
            out((KEPT * ROWS, WIDTH), BF16),
            out((CORES * WIDTH, WIDTH // CORES), BF16),
        ),
        [SM] + [VM] * 12,
        [pltpu.VMEM((ROWS * OUT_ROWS, ROWS), F32), pltpu.VMEM((PACK, WIDTH, ROWS), F32)],
        flops=500000000,
        bytes_accessed=3000000,
    )(me, wire, into, dec, to_frame(dec, 1), to_frame(dec, 2), to_frame(dec, 3), table, w_enc, wide, wide_bias, grad_blank, grad_label)
    term = lax.all_to_all(term, ("core", "frame"), 0, 0, tiled=True)
    rows, planes, dec0, dec1, dec2, dec3 = call(
        back_kernel,
        "back",
        (out((2 * KEPT, ROWS), F32), out((SLOTS * ROWS, WIDTH), BF16), part, part, part, part),
        [SM, SM] + [VM] * 7,
        flops=500000000,
        bytes_accessed=3000000,
    )(me, block_off, start, out_of, hidden, dlogit, w_enc, wide, logprobs)
    back = call(
        merge_kernel,
        "merge",
        out((ROWS * BACK_ROWS, ROWS), BF16),
        [VM, VM],
        [pltpu.VMEM((ROWS * BACK_ROWS, ROWS), F32)],
        flops=300000,
        bytes_accessed=1700000,
    )(term, planes)
    back, dec1, dec2 = lax.optimization_barrier((back, dec1, dec2))
    back = lax.all_to_all(back.reshape(ROWS * BACK_ROWS // 2, 2, ROWS), DP, 0, 0, tiled=True)
    back = back.reshape(ROWS * BACK_ROWS, ROWS)
    grad_pred = call(
        pred_kernel,
        "pred",
        out((PART, WIDTH), F32),
        [VM] * 5,
        flops=40000000,
        bytes_accessed=700000,
    )(dec0, to_frame(dec1, 1), to_frame(dec2, 2), to_frame(dec3, 3), w_dec)
    grad_enc, grad_w_out = call(
        unpack_kernel,
        "unpack",
        (out((ROWS, WIDTH), BF16), out((1, w_out.shape[1]), F32)),
        [VM, VM],
        [pltpu.VMEM((ROWS * BACK_ROWS, ROWS), F32)],
        flops=40000000,
        bytes_accessed=600000,
    )(home, back)
    return (rows.T, grad_enc, grad_pred, grad_w_out)


def solution(mesh):
    fine = Mesh(mesh.devices.reshape(16, 4, 2, 4), EVERY)
    return jax.shard_map(
        shards,
        mesh=fine,
        in_specs=(
            P(EVERY, None),
            P(None, "frame", None),
            P(EVERY, None),
            P(DP, None),
            P(EVERY),
            P(EVERY),
            P(),
            P(),
            P(),
            P(),
            P(EVERY, None),
            P(EVERY, None),
        ),
        out_specs=(P(EVERY, None), P(EVERY, None), P(EVERY, None), P(EVERY, None)),
        check_vma=False,
    )
```

```python
import jax
import jax.numpy as jnp
from jax import lax
from jax.experimental import pallas as pl
from jax.experimental.pallas import tpu as pltpu
from jax.sharding import Mesh
from jax.sharding import PartitionSpec as P

F32 = jnp.float32
BF16 = jnp.bfloat16
I32 = jnp.int32

ROWS = 128
PACK = 4
SLOTS = 2
WIDTH = PACK * ROWS
KEPT = 3
BLOCK = 64
FRAMES = 4
PART = ROWS // FRAMES
OUT_ROWS = SLOTS * PACK
HALF = PACK // 2
BACK_ROWS = OUT_ROWS + HALF
CORES = 2


def iota(dim, shape=(ROWS, ROWS)):
    return lax.broadcasted_iota(I32, shape, dim)


def mm(a, b):
    return jnp.dot(a, b, preferred_element_type=F32)


def mm_nt(a, b):
    return lax.dot_general(a, b, (((1,), (1,)), ((), ())), preferred_element_type=F32)


def mm_tn(a, b):
    return lax.dot_general(a, b, (((0,), (0,)), ((), ())), preferred_element_type=F32)


def to_bf(mask):
    return jnp.where(mask, 1.0, 0.0).astype(BF16)


def chunk(c):
    return slice(c * ROWS, (c + 1) * ROWS)


def as_column(row):
    return jnp.sum(jnp.where(iota(0) == iota(1), jnp.broadcast_to(row, (ROWS, ROWS)), 0.0), axis=1, keepdims=True)


def as_row(column):
    return jnp.sum(jnp.where(iota(0) == iota(1), jnp.broadcast_to(column, (ROWS, ROWS)), 0.0), axis=0, keepdims=True)


def owner_and_rank(dest_row):
    dest_f = dest_row.astype(F32)
    follows = (as_column(dest_f) + 1.0) == jnp.broadcast_to(dest_f, (ROWS, ROWS))
    rank = jnp.sum(jnp.where(follows, 1.0, 0.0), axis=0, keepdims=True)
    return (dest_row // ROWS).astype(F32), jnp.where(dest_row % ROWS == 0, 0.0, rank)


def pack_kernel(id_ref, dest_hbm, enc_hbm, pred_hbm, w_hbm, out_ref, dec_ref, dest_ref, enc_ref, pred_ref, w_ref, wire_ref, sems):
    pairs = ((dest_hbm.at[id_ref[0] // FRAMES], dest_ref), (enc_hbm, enc_ref), (pred_hbm, pred_ref), (w_hbm, w_ref))
    copies = [pltpu.make_async_copy(src, dst, sems.at[i]) for i, (src, dst) in enumerate(pairs)]
    for copy in copies:
        copy.start()
    copies[0].wait()
    owner, rank = owner_and_rank(dest_ref[...])
    down = iota(0).astype(F32)
    picks = [to_bf((down == owner) & (rank == float(k))) for k in range(SLOTS)]
    copies[1].wait()
    for k in range(SLOTS):
        picked = mm(picks[k], enc_ref[...])
        for c in range(PACK):
            wire_ref[pl.ds(k * PACK + c, ROWS, stride=OUT_ROWS), :] = picked[:, chunk(c)]
    out_ref[...] = wire_ref[...].astype(BF16)
    copies[2].wait()
    copies[3].wait()
    dec_ref[...] = mm(pred_ref[...], w_ref[...]).astype(BF16)


def base_row(off_ref, start_ref):
    lane = iota(1, (1, ROWS))
    return (start_ref[...] + jnp.where(lane < BLOCK, off_ref[0], off_ref[1])).astype(F32)


def prep_kernel(
    id_ref, off_ref, dest_ref, start_ref, label_ref, w_ref, bias_ref,
    into_ref, from_ref, home_ref, table_ref, wide_ref, bias_out_ref,
):
    dest = dest_ref[...]
    mine = to_bf(dest // ROWS == id_ref[0] // FRAMES)
    ones = jnp.ones((ROWS, ROWS), BF16)
    count_row = mm_nt(ones, mine)
    count_col = mm(mine, ones)
    offset_row = mm(count_row.astype(BF16), to_bf(iota(0) < iota(1)))
    offset_col = mm(to_bf(iota(1) < iota(0)), count_col.astype(BF16))
    owner, rank = owner_and_rank(dest_ref[pl.ds(id_ref[0] // FRAMES, 1), :])
    owner = as_column(owner)
    rank = as_column(rank)
    down = iota(0).astype(F32)
    along = iota(1).astype(F32)
    for k in range(SLOTS):
        into_ref[k] = to_bf((offset_row + float(k) == down) & (count_row > float(k)))
        from_ref[k] = to_bf((offset_col + float(k) == along) & (count_col > float(k)))
        home_ref[k] = to_bf((owner == along) & (rank == float(k)))
    base = as_column(base_row(off_ref, start_ref))
    labels = label_ref[...].astype(F32)
    table = jnp.broadcast_to(base, (ROWS, ROWS))
    for k in range(KEPT):
        emitted = jnp.sum(jnp.where(along == base + float(k), labels, 0.0), axis=1, keepdims=True)
        table = jnp.where(iota(1) == k, emitted, table)
    table_ref[...] = table
    vocab = w_ref.shape[1]
    wide_ref[...] = jnp.zeros_like(wide_ref)
    wide_ref[:, 0:vocab] = w_ref[...]
    bias_out_ref[...] = jnp.full_like(bias_out_ref, -1e30)
    bias_out_ref[:, 0:vocab] = bias_ref[...]


def take_slot(wire_ref, slot, rows):
    return jnp.concatenate([wire_ref[pl.ds(slot * PACK + c, ROWS, stride=rows), :] for c in range(PACK)], axis=1)


def joint_kernel(
    wire_ref, into_ref, dec_ref, table_ref, w_enc_ref, w_out_ref, bias_ref, cot_blank_ref,
    cot_label_ref, logprob_ref, hidden_ref, dlogit_ref, grad_ref, float_ref, term_ref,
):
    float_ref[...] = wire_ref[...].astype(F32)
    owned = jnp.zeros((ROWS, WIDTH), F32)
    for k in range(SLOTS):
        owned = owned + mm(into_ref[k], take_slot(float_ref, k, OUT_ROWS).astype(BF16))
    enc_joint = mm(owned.astype(BF16), w_enc_ref[...])
    held = iota(1).astype(F32)
    dec = dec_ref[...]
    base = table_ref[:, KEPT : KEPT + 1]
    lane = iota(1, (ROWS, WIDTH))
    for k in range(KEPT):
        rows = slice(k * ROWS, (k + 1) * ROWS)
        dec_rows = mm(to_bf(held == base + float(k)), dec)
        hidden = jnp.tanh(enc_joint + dec_rows).astype(BF16)
        hidden_ref[rows, :] = hidden
        logits = mm(hidden, w_out_ref[...]) + bias_ref[...]
        shifted = logits - jnp.max(logits, axis=1, keepdims=True)
        power = jnp.exp(shifted)
        total = jnp.sum(power, axis=1, keepdims=True)
        log_total = jnp.log(total)
        is_label = lane == table_ref[:, k : k + 1].astype(I32)
        at_label = jnp.sum(jnp.where(is_label, shifted, 0.0), axis=1, keepdims=True)
        logprob_ref[:, k : k + 1] = shifted[:, 0:1] - log_total
        logprob_ref[:, KEPT + k : KEPT + k + 1] = at_label - log_total
        cot_blank = cot_blank_ref[:, k : k + 1]
        cot_label = cot_label_ref[:, k : k + 1]
        scale = (cot_blank + cot_label) / total
        direct = jnp.where(is_label, cot_label, 0.0) + jnp.where(lane == 0, cot_blank, 0.0)
        dlogit_ref[rows, :] = (direct - power * scale).astype(BF16)
    term = mm_tn(hidden_ref[...], dlogit_ref[...])
    for c in range(PACK):
        term_ref[c] = term[:, chunk(c)]
    for core in range(CORES):
        for f in range(FRAMES):
            for h in range(HALF):
                picked = term_ref.at[core * HALF + h][pl.ds(f, ROWS, stride=FRAMES), :]
                grad_ref[chunk(core * FRAMES + f), chunk(h)] = picked.astype(BF16)


def back_kernel(
    id_ref, off_ref, start_ref, from_ref, hidden_ref, dlogit_ref, w_enc_ref, w_out_ref, logprob_ref,
    row_ref, plane_ref, dec0_ref, dec1_ref, dec2_ref, dec3_ref,
):
    for i in range(2 * KEPT):
        row_ref[i : i + 1, :] = as_row(logprob_ref[:, i : i + 1])
    base = base_row(off_ref, start_ref)
    frame = id_ref[0] % FRAMES
    sent = (((frame + iota(0) // PART) % FRAMES) * PART + iota(0) % PART).astype(F32)
    enc_grad = jnp.zeros((ROWS, WIDTH), F32)
    dec_grad = jnp.zeros((ROWS, WIDTH), F32)
    for k in range(KEPT):
        rows = slice(k * ROWS, (k + 1) * ROWS)
        hidden = hidden_ref[rows, :].astype(F32)
        dz = mm_nt(dlogit_ref[rows, :], w_out_ref[...]) * (1.0 - hidden * hidden)
        enc_grad = enc_grad + dz
        here = to_bf(sent == base + float(k))
        high = dz.astype(BF16)
        low = (dz - high.astype(F32)).astype(BF16)
        dec_grad = dec_grad + mm(here, high) + mm(here, low)
    dec_grad = dec_grad.astype(BF16)
    for f, ref in enumerate((dec0_ref, dec1_ref, dec2_ref, dec3_ref)):
        ref[...] = dec_grad[f * PART : (f + 1) * PART, :]
    owned = mm_nt(enc_grad.astype(BF16), w_enc_ref[...]).astype(BF16)
    for k in range(SLOTS):
        plane_ref[chunk(k), :] = mm(from_ref[k], owned).astype(BF16)


def merge_kernel(parts_ref, plane_ref, out_ref, float_ref):
    for k in range(SLOTS):
        for c in range(PACK):
            plane = plane_ref[chunk(k), chunk(c)].astype(F32)
            float_ref[pl.ds(k * PACK + c, ROWS, stride=BACK_ROWS), :] = plane
    for h in range(HALF):
        total = parts_ref[chunk(0), chunk(h)].astype(F32)
        for i in range(1, CORES * FRAMES):
            total = total + parts_ref[chunk(i), chunk(h)].astype(F32)
        float_ref[pl.ds(OUT_ROWS + h, ROWS, stride=BACK_ROWS), :] = total
    out_ref[...] = float_ref[...].astype(BF16)


def pred_kernel(part0_ref, part1_ref, part2_ref, part3_ref, w_ref, out_ref):
    total = part0_ref[...].astype(F32) + part1_ref[...].astype(F32)
    total = total + (part2_ref[...].astype(F32) + part3_ref[...].astype(F32))
    high = total.astype(BF16)
    low = (total - high.astype(F32)).astype(BF16)
    out_ref[...] = mm_nt(high, w_ref[...]) + mm_nt(low, w_ref[...])


def unpack_kernel(home_ref, wire_ref, enc_ref, grad_ref, float_ref):
    float_ref[...] = wire_ref[...].astype(F32)
    rows = jnp.zeros((ROWS, WIDTH), F32)
    for k in range(SLOTS):
        rows = rows + mm(home_ref[k], take_slot(float_ref, k, BACK_ROWS).astype(BF16))
    enc_ref[...] = rows.astype(BF16)
    quarters = []
    for core in range(CORES):
        for h in range(HALF):
            first = core * BACK_ROWS + OUT_ROWS + h
            from_core = float_ref[pl.ds(first, ROWS // CORES, stride=CORES * BACK_ROWS), :]
            quarters.append(jnp.sum(from_core, axis=0, keepdims=True))
    term = jnp.concatenate(quarters, axis=1)
    grad_ref[...] = term[:, 0 : grad_ref.shape[1]]


VM = pl.BlockSpec(memory_space=pltpu.VMEM)
SM = pl.BlockSpec(memory_space=pltpu.SMEM)
HBM = pl.BlockSpec(memory_space=pltpu.HBM)


def call(kernel, name, outs, specs, scratch=(), flops=0, bytes_accessed=0, limit=24 << 20):
    return pl.pallas_call(
        kernel,
        name=name,
        out_shape=outs,
        in_specs=list(specs),
        out_specs=jax.tree.map(lambda _: VM, outs),
        scratch_shapes=list(scratch),
        compiler_params=pltpu.CompilerParams(vmem_limit_bytes=limit),
        cost_estimate=pl.CostEstimate(flops=flops, bytes_accessed=bytes_accessed, transcendentals=0),
    )


def out(shape, dtype):
    return jax.ShapeDtypeStruct(shape, dtype)


DP = ("z", "x", "core")
EVERY = DP + ("frame",)


def to_frame(array, ahead):
    return lax.ppermute(array, "frame", [(f, (f + ahead) % FRAMES) for f in range(FRAMES)])


def shards(
    enc_rows, dest, pred_rows, label_ids, block_off, band_start, w_enc, w_dec, w_out, bias_out, grad_blank, grad_label
):
    me = lax.axis_index(EVERY).astype(I32).reshape(1)
    flat_dest = dest.reshape(ROWS, ROWS)
    start = band_start.reshape(1, ROWS)
    bias = bias_out.reshape(1, -1)
    part = out((PART, WIDTH), BF16)
    pick = out((SLOTS, ROWS, ROWS), BF16)

    wire, dec = call(
        pack_kernel,
        "pack",
        (out((ROWS * OUT_ROWS, ROWS), BF16), part),
        [SM, HBM, HBM, HBM, HBM],
        [
            pltpu.VMEM((1, ROWS), I32),
            pltpu.VMEM((ROWS, WIDTH), BF16),
            pltpu.VMEM((PART, WIDTH), BF16),
            pltpu.VMEM((WIDTH, WIDTH), BF16),
            pltpu.VMEM((ROWS * OUT_ROWS, ROWS), F32),
            pltpu.SemaphoreType.DMA((4,)),
        ],
        flops=40000000,
        bytes_accessed=400000,
        limit=None,
    )(me, dest, enc_rows, pred_rows, w_dec)
    wire = lax.all_to_all(wire, DP, 0, 0, tiled=True)
    dec = lax.all_gather(dec, "frame", axis=0, tiled=True)
    into, out_of, home, table, wide, wide_bias = call(
        prep_kernel,
        "prep",
        (pick, pick, pick, out((ROWS, ROWS), F32), out((WIDTH, WIDTH), BF16), out((1, WIDTH), F32)),
        [SM, SM] + [VM] * 5,
        flops=100000000,
        bytes_accessed=2000000,
    )(me, block_off, flat_dest, start, label_ids, w_out, bias)
    logprobs, hidden, dlogit, term = call(
        joint_kernel,
        "joint",
        (
            out((ROWS, 2 * KEPT), F32),
            out((KEPT * ROWS, WIDTH), BF16),
            out((KEPT * ROWS, WIDTH), BF16),
            out((CORES * WIDTH, WIDTH // CORES), BF16),
        ),
        [VM] * 9,
        [pltpu.VMEM((ROWS * OUT_ROWS, ROWS), F32), pltpu.VMEM((PACK, WIDTH, ROWS), F32)],
        flops=500000000,
        bytes_accessed=3000000,
    )(wire, into, dec, table, w_enc, wide, wide_bias, grad_blank, grad_label)
    term = lax.all_to_all(term, ("core", "frame"), 0, 0, tiled=True)
    rows, planes, dec0, dec1, dec2, dec3 = call(
        back_kernel,
        "back",
        (out((2 * KEPT, ROWS), F32), out((SLOTS * ROWS, WIDTH), BF16), part, part, part, part),
        [SM, SM] + [VM] * 7,
        flops=500000000,
        bytes_accessed=3000000,
    )(me, block_off, start, out_of, hidden, dlogit, w_enc, wide, logprobs)
    back = call(
        merge_kernel,
        "merge",
        out((ROWS * BACK_ROWS, ROWS), BF16),
        [VM, VM],
        [pltpu.VMEM((ROWS * BACK_ROWS, ROWS), F32)],
        flops=300000,
        bytes_accessed=1700000,
    )(term, planes)
    back, dec1, dec2 = lax.optimization_barrier((back, dec1, dec2))
    back = lax.all_to_all(back.reshape(ROWS * BACK_ROWS // 2, 2, ROWS), DP, 0, 0, tiled=True)
    back = back.reshape(ROWS * BACK_ROWS, ROWS)
    grad_pred = call(
        pred_kernel,
        "pred",
        out((PART, WIDTH), F32),
        [VM] * 5,
        flops=40000000,
        bytes_accessed=700000,
    )(dec0, to_frame(dec1, 1), to_frame(dec2, 2), to_frame(dec3, 3), w_dec)
    grad_enc, grad_w_out = call(
        unpack_kernel,
        "unpack",
        (out((ROWS, WIDTH), BF16), out((1, w_out.shape[1]), F32)),
        [VM, VM],
        [pltpu.VMEM((ROWS * BACK_ROWS, ROWS), F32)],
        flops=40000000,
        bytes_accessed=600000,
    )(home, back)
    return (rows.T, grad_enc, grad_pred, grad_w_out)


def solution(mesh):
    fine = Mesh(mesh.devices.reshape(16, 4, 2, 4), EVERY)
    return jax.shard_map(
        shards,
        mesh=fine,
        in_specs=(
            P(EVERY, None),
            P(None, "frame", None),
            P(EVERY, None),
            P(DP, None),
            P(EVERY),
            P(EVERY),
            P(),
            P(),
            P(),
            P(),
            P(EVERY, None),
            P(EVERY, None),
        ),
        out_specs=(P(EVERY, None), P(EVERY, None), P(EVERY, None), P(EVERY, None)),
        check_vma=False,
    )
```

```python
import jax
import jax.numpy as jnp
from jax import lax
from jax.experimental import pallas as pl
from jax.experimental.pallas import tpu as pltpu
from jax.sharding import Mesh
from jax.sharding import PartitionSpec as P

F32 = jnp.float32
BF16 = jnp.bfloat16
I32 = jnp.int32

ROWS = 128
PACK = 4
SLOTS = 2
WIDTH = PACK * ROWS
KEPT = 3
BLOCK = 64
FRAMES = 4
PART = ROWS // FRAMES
OUT_ROWS = SLOTS * PACK
HALF = PACK // 2
BACK_ROWS = OUT_ROWS + HALF
CORES = 2
STEP = 32


def iota(dim, shape=(ROWS, ROWS)):
    return lax.broadcasted_iota(I32, shape, dim)


def mm(a, b):
    return jnp.dot(a, b, preferred_element_type=F32)


def mm_nt(a, b):
    return lax.dot_general(a, b, (((1,), (1,)), ((), ())), preferred_element_type=F32)


def mm_tn(a, b):
    return lax.dot_general(a, b, (((0,), (0,)), ((), ())), preferred_element_type=F32)


def to_bf(mask):
    return jnp.where(mask, 1.0, 0.0).astype(BF16)


def chunk(c):
    return slice(c * ROWS, (c + 1) * ROWS)


def as_column(row):
    return jnp.sum(jnp.where(iota(0) == iota(1), jnp.broadcast_to(row, (ROWS, ROWS)), 0.0), axis=1, keepdims=True)


def as_row(column):
    return jnp.sum(jnp.where(iota(0) == iota(1), jnp.broadcast_to(column, (ROWS, ROWS)), 0.0), axis=0, keepdims=True)


def owner_and_rank(dest_row):
    dest_f = dest_row.astype(F32)
    follows = (as_column(dest_f) + 1.0) == jnp.broadcast_to(dest_f, (ROWS, ROWS))
    rank = jnp.sum(jnp.where(follows, 1.0, 0.0), axis=0, keepdims=True)
    return (dest_row // ROWS).astype(F32), jnp.where(dest_row % ROWS == 0, 0.0, rank)


def pack_kernel(id_ref, dest_hbm, enc_hbm, pred_hbm, w_hbm, out_ref, dec_ref, dest_ref, enc_ref, pred_ref, w_ref, wire_ref, sems):
    pairs = ((dest_hbm.at[id_ref[0] // FRAMES], dest_ref), (enc_hbm, enc_ref), (pred_hbm, pred_ref), (w_hbm, w_ref))
    copies = [pltpu.make_async_copy(src, dst, sems.at[i]) for i, (src, dst) in enumerate(pairs)]
    for copy in copies:
        copy.start()
    copies[0].wait()
    owner, rank = owner_and_rank(dest_ref[...])
    down = iota(0).astype(F32)
    picks = [to_bf((down == owner) & (rank == float(k))) for k in range(SLOTS)]
    copies[1].wait()
    for k in range(SLOTS):
        picked = mm(picks[k], enc_ref[...])
        for c in range(PACK):
            wire_ref[pl.ds(k * PACK + c, ROWS, stride=OUT_ROWS), :] = picked[:, chunk(c)]
    out_ref[...] = wire_ref[...].astype(BF16)
    copies[2].wait()
    copies[3].wait()
    dec_ref[...] = mm(pred_ref[...], w_ref[...]).astype(BF16)


def base_row(off_ref, start_ref):
    lane = iota(1, (1, ROWS))
    return (start_ref[...] + jnp.where(lane < BLOCK, off_ref[0], off_ref[1])).astype(F32)


def prep_kernel(
    id_ref, off_ref, dest_ref, start_ref, label_ref, w_ref, bias_ref,
    into_ref, from_ref, home_ref, here_ref, table_ref, wide_ref, bias_out_ref,
):
    dest = dest_ref[...]
    mine = to_bf(dest // ROWS == id_ref[0] // FRAMES)
    ones = jnp.ones((ROWS, ROWS), BF16)
    count_row = mm_nt(ones, mine)
    count_col = mm(mine, ones)
    offset_row = mm(count_row.astype(BF16), to_bf(iota(0) < iota(1)))
    offset_col = mm(to_bf(iota(1) < iota(0)), count_col.astype(BF16))
    owner, rank = owner_and_rank(dest_ref[pl.ds(id_ref[0] // FRAMES, 1), :])
    owner = as_column(owner)
    rank = as_column(rank)
    down = iota(0).astype(F32)
    along = iota(1).astype(F32)
    for k in range(SLOTS):
        into_ref[k] = to_bf((offset_row + float(k) == down) & (count_row > float(k)))
        from_ref[k] = to_bf((offset_col + float(k) == along) & (count_col > float(k)))
        home_ref[k] = to_bf((owner == along) & (rank == float(k)))
    base = as_column(base_row(off_ref, start_ref))
    labels = label_ref[...].astype(F32)
    table = jnp.zeros((ROWS, ROWS), F32)
    frame = id_ref[0] % FRAMES
    held = (((frame + FRAMES - iota(1) // PART) % FRAMES) * PART + iota(1) % PART).astype(F32)
    for k in range(KEPT):
        here_ref[k * ROWS : (k + 1) * ROWS, :] = to_bf(held == base + float(k))
        emitted = jnp.sum(jnp.where(along == base + float(k), labels, 0.0), axis=1, keepdims=True)
        table = jnp.where(iota(1) == k, emitted, table)
    table_ref[...] = table
    vocab = w_ref.shape[1]
    wide_ref[...] = jnp.zeros_like(wide_ref)
    wide_ref[:, 0:vocab] = w_ref[...]
    bias_out_ref[...] = jnp.full_like(bias_out_ref, -1e30)
    bias_out_ref[:, 0:vocab] = bias_ref[...]


def take_slot(wire_ref, slot, rows):
    return jnp.concatenate([wire_ref[pl.ds(slot * PACK + c, ROWS, stride=rows), :] for c in range(PACK)], axis=1)


def enter_kernel(wire_ref, into_ref, w_enc_ref, out_ref, float_ref):
    float_ref[...] = wire_ref[...].astype(F32)
    owned = jnp.zeros((ROWS, WIDTH), F32)
    for k in range(SLOTS):
        owned = owned + mm(into_ref[k], take_slot(float_ref, k, OUT_ROWS).astype(BF16))
    out_ref[...] = mm(owned.astype(BF16), w_enc_ref[...])


def joint_kernel(
    enc_ref, here_ref, dec0_ref, dec1_ref, dec2_ref, dec3_ref, table_ref, w_out_ref, bias_ref,
    cot_blank_ref, cot_label_ref, logprob_ref, hidden_ref, dlogit_ref, grad_ref, term_ref, logit_ref,
):
    enc_joint = enc_ref[...]
    dec = jnp.concatenate([dec0_ref[...], dec1_ref[...], dec2_ref[...], dec3_ref[...]], axis=0)
    dec_rows = mm(here_ref[...], dec)
    for k in range(KEPT):
        rows = slice(k * ROWS, (k + 1) * ROWS)
        hidden_ref[rows, :] = jnp.tanh(enc_joint + dec_rows[rows, :]).astype(BF16)
    logit_ref[...] = mm(hidden_ref[...], w_out_ref[...])
    lane = iota(1, (STEP, WIDTH))
    for k in range(KEPT):
        for r in range(0, ROWS, STEP):
            rows = slice(k * ROWS + r, k * ROWS + r + STEP)
            part = slice(r, r + STEP)
            logits = logit_ref[rows, :] + bias_ref[...]
            shifted = logits - jnp.max(logits, axis=1, keepdims=True)
            power = jnp.exp(shifted)
            total = jnp.sum(power, axis=1, keepdims=True)
            log_total = jnp.log(total)
            is_label = lane == table_ref[part, k : k + 1].astype(I32)
            at_label = jnp.sum(jnp.where(is_label, shifted, 0.0), axis=1, keepdims=True)
            logprob_ref[part, k : k + 1] = shifted[:, 0:1] - log_total
            logprob_ref[part, KEPT + k : KEPT + k + 1] = at_label - log_total
            cot_blank = cot_blank_ref[part, k : k + 1]
            cot_label = cot_label_ref[part, k : k + 1]
            scale = (cot_blank + cot_label) / total
            direct = jnp.where(is_label, cot_label, jnp.where(lane == 0, cot_blank, 0.0))
            dlogit_ref[rows, :] = (direct - power * scale).astype(BF16)
    for core in range(CORES):
        half = HALF * ROWS
        term = mm_tn(hidden_ref[...], dlogit_ref[:, core * half : (core + 1) * half])
        for h in range(HALF):
            term_ref[core * HALF + h] = term[:, chunk(h)]
            for f in range(FRAMES):
                picked = term_ref.at[core * HALF + h][pl.ds(f, ROWS, stride=FRAMES), :]
                grad_ref[chunk(core * FRAMES + f), chunk(h)] = picked.astype(BF16)


def back_kernel(
    id_ref, off_ref, start_ref, from_ref, hidden_ref, dlogit_ref, w_enc_ref, w_out_ref, logprob_ref,
    row_ref, plane_ref, dec0_ref, dec1_ref, dec2_ref, dec3_ref,
):
    for i in range(2 * KEPT):
        row_ref[i : i + 1, :] = as_row(logprob_ref[:, i : i + 1])
    base = base_row(off_ref, start_ref)
    frame = id_ref[0] % FRAMES
    sent = (((frame + iota(0) // PART) % FRAMES) * PART + iota(0) % PART).astype(F32)
    enc_grad = jnp.zeros((ROWS, WIDTH), F32)
    dec_grad = jnp.zeros((ROWS, WIDTH), F32)
    for k in range(KEPT):
        rows = slice(k * ROWS, (k + 1) * ROWS)
        hidden = hidden_ref[rows, :].astype(F32)
        dz = mm_nt(dlogit_ref[rows, :], w_out_ref[...]) * (1.0 - hidden * hidden)
        enc_grad = enc_grad + dz
        here = to_bf(sent == base + float(k))
        high = dz.astype(BF16)
        low = (dz - high.astype(F32)).astype(BF16)
        dec_grad = dec_grad + mm(here, high) + mm(here, low)
    dec_grad = dec_grad.astype(BF16)
    for f, ref in enumerate((dec0_ref, dec1_ref, dec2_ref, dec3_ref)):
        ref[...] = dec_grad[f * PART : (f + 1) * PART, :]
    owned = mm_nt(enc_grad.astype(BF16), w_enc_ref[...]).astype(BF16)
    for k in range(SLOTS):
        plane_ref[chunk(k), :] = mm(from_ref[k], owned).astype(BF16)


def merge_kernel(parts_ref, plane_ref, out_ref, float_ref):
    for k in range(SLOTS):
        for c in range(PACK):
            plane = plane_ref[chunk(k), chunk(c)].astype(F32)
            float_ref[pl.ds(k * PACK + c, ROWS, stride=BACK_ROWS), :] = plane
    for h in range(HALF):
        total = parts_ref[chunk(0), chunk(h)].astype(F32)
        for i in range(1, CORES * FRAMES):
            total = total + parts_ref[chunk(i), chunk(h)].astype(F32)
        float_ref[pl.ds(OUT_ROWS + h, ROWS, stride=BACK_ROWS), :] = total
    out_ref[...] = float_ref[...].astype(BF16)


def pred_kernel(part0_ref, part1_ref, part2_ref, part3_ref, w_ref, out_ref):
    total = part0_ref[...].astype(F32) + part1_ref[...].astype(F32)
    total = total + (part2_ref[...].astype(F32) + part3_ref[...].astype(F32))
    high = total.astype(BF16)
    low = (total - high.astype(F32)).astype(BF16)
    out_ref[...] = mm_nt(high, w_ref[...]) + mm_nt(low, w_ref[...])


def unpack_kernel(home_ref, wire_ref, enc_ref, grad_ref, float_ref):
    float_ref[...] = wire_ref[...].astype(F32)
    rows = jnp.zeros((ROWS, WIDTH), F32)
    for k in range(SLOTS):
        rows = rows + mm(home_ref[k], take_slot(float_ref, k, BACK_ROWS).astype(BF16))
    enc_ref[...] = rows.astype(BF16)
    quarters = []
    for core in range(CORES):
        for h in range(HALF):
            first = core * BACK_ROWS + OUT_ROWS + h
            from_core = float_ref[pl.ds(first, ROWS // CORES, stride=CORES * BACK_ROWS), :]
            quarters.append(jnp.sum(from_core, axis=0, keepdims=True))
    term = jnp.concatenate(quarters, axis=1)
    grad_ref[...] = term[:, 0 : grad_ref.shape[1]]


VM = pl.BlockSpec(memory_space=pltpu.VMEM)
SM = pl.BlockSpec(memory_space=pltpu.SMEM)
HBM = pl.BlockSpec(memory_space=pltpu.HBM)


def call(kernel, name, outs, specs, scratch=(), flops=0, bytes_accessed=0, limit=24 << 20):
    return pl.pallas_call(
        kernel,
        name=name,
        out_shape=outs,
        in_specs=list(specs),
        out_specs=jax.tree.map(lambda _: VM, outs),
        scratch_shapes=list(scratch),
        compiler_params=pltpu.CompilerParams(vmem_limit_bytes=limit),
        cost_estimate=pl.CostEstimate(flops=flops, bytes_accessed=bytes_accessed, transcendentals=0),
    )


def out(shape, dtype):
    return jax.ShapeDtypeStruct(shape, dtype)


DP = ("z", "x", "core")
EVERY = DP + ("frame",)


def to_frame(array, ahead):
    return lax.ppermute(array, "frame", [(f, (f + ahead) % FRAMES) for f in range(FRAMES)])


def shards(
    enc_rows, dest, pred_rows, label_ids, block_off, band_start, w_enc, w_dec, w_out, bias_out, grad_blank, grad_label
):
    me = lax.axis_index(EVERY).astype(I32).reshape(1)
    flat_dest = dest.reshape(ROWS, ROWS)
    start = band_start.reshape(1, ROWS)
    bias = bias_out.reshape(1, -1)
    part = out((PART, WIDTH), BF16)
    pick = out((SLOTS, ROWS, ROWS), BF16)

    wire, dec = call(
        pack_kernel,
        "pack",
        (out((ROWS * OUT_ROWS, ROWS), BF16), part),
        [SM, HBM, HBM, HBM, HBM],
        [
            pltpu.VMEM((1, ROWS), I32),
            pltpu.VMEM((ROWS, WIDTH), BF16),
            pltpu.VMEM((PART, WIDTH), BF16),
            pltpu.VMEM((WIDTH, WIDTH), BF16),
            pltpu.VMEM((ROWS * OUT_ROWS, ROWS), F32),
            pltpu.SemaphoreType.DMA((4,)),
        ],
        flops=40000000,
        bytes_accessed=400000,
        limit=None,
    )(me, dest, enc_rows, pred_rows, w_dec)
    wire = lax.all_to_all(wire, DP, 0, 0, tiled=True)
    into, out_of, home, here, table, wide, wide_bias = call(
        prep_kernel,
        "prep",
        (pick, pick, pick, out((KEPT * ROWS, ROWS), BF16), out((ROWS, ROWS), F32), out((WIDTH, WIDTH), BF16), out((1, WIDTH), F32)),
        [SM, SM] + [VM] * 5,
        flops=100000000,
        bytes_accessed=2000000,
    )(me, block_off, flat_dest, start, label_ids, w_out, bias)
    enc_joint = call(
        enter_kernel,
        "enter",
        out((ROWS, WIDTH), F32),
        [VM] * 3,
        [pltpu.VMEM((ROWS * OUT_ROWS, ROWS), F32)],
        flops=100000000,
        bytes_accessed=1000000,
    )(wire, into, w_enc)
    logprobs, hidden, dlogit, term = call(
        joint_kernel,
        "joint",
        (
            out((ROWS, 2 * KEPT), F32),
            out((KEPT * ROWS, WIDTH), BF16),
            out((KEPT * ROWS, WIDTH), BF16),
            out((CORES * WIDTH, WIDTH // CORES), BF16),
        ),
        [VM] * 11,
        [
            pltpu.VMEM((PACK, WIDTH, ROWS), F32),
            pltpu.VMEM((KEPT * ROWS, WIDTH), F32),
        ],
        flops=500000000,
        bytes_accessed=3000000,
    )(enc_joint, here, dec, to_frame(dec, 1), to_frame(dec, 2), to_frame(dec, 3), table, wide, wide_bias, grad_blank, grad_label)
    term = lax.all_to_all(term, ("core", "frame"), 0, 0, tiled=True)
    rows, planes, dec0, dec1, dec2, dec3 = call(
        back_kernel,
        "back",
        (out((2 * KEPT, ROWS), F32), out((SLOTS * ROWS, WIDTH), BF16), part, part, part, part),
        [SM, SM] + [VM] * 7,
        flops=500000000,
        bytes_accessed=3000000,
    )(me, block_off, start, out_of, hidden, dlogit, w_enc, wide, logprobs)
    back = call(
        merge_kernel,
        "merge",
        out((ROWS * BACK_ROWS, ROWS), BF16),
        [VM, VM],
        [pltpu.VMEM((ROWS * BACK_ROWS, ROWS), F32)],
        flops=300000,
        bytes_accessed=1700000,
    )(term, planes)
    back, dec1, dec2 = lax.optimization_barrier((back, dec1, dec2))
    back = lax.all_to_all(back.reshape(ROWS * BACK_ROWS // 2, 2, ROWS), DP, 0, 0, tiled=True)
    back = back.reshape(ROWS * BACK_ROWS, ROWS)
    grad_pred = call(
        pred_kernel,
        "pred",
        out((PART, WIDTH), F32),
        [VM] * 5,
        flops=40000000,
        bytes_accessed=700000,
    )(dec0, to_frame(dec1, 1), to_frame(dec2, 2), to_frame(dec3, 3), w_dec)
    grad_enc, grad_w_out = call(
        unpack_kernel,
        "unpack",
        (out((ROWS, WIDTH), BF16), out((1, w_out.shape[1]), F32)),
        [VM, VM],
        [pltpu.VMEM((ROWS * BACK_ROWS, ROWS), F32)],
        flops=40000000,
        bytes_accessed=600000,
    )(home, back)
    return (rows.T, grad_enc, grad_pred, grad_w_out)


def solution(mesh):
    fine = Mesh(mesh.devices.reshape(16, 4, 2, 4), EVERY)
    return jax.shard_map(
        shards,
        mesh=fine,
        in_specs=(
            P(EVERY, None),
            P(None, "frame", None),
            P(EVERY, None),
            P(DP, None),
            P(EVERY),
            P(EVERY),
            P(),
            P(),
            P(),
            P(),
            P(EVERY, None),
            P(EVERY, None),
        ),
        out_specs=(P(EVERY, None), P(EVERY, None), P(EVERY, None), P(EVERY, None)),
        check_vma=False,
    )
```

```python
import jax
import jax.numpy as jnp
from jax import lax
from jax.experimental import pallas as pl
from jax.experimental.pallas import tpu as pltpu
from jax.sharding import Mesh
from jax.sharding import PartitionSpec as P

F32 = jnp.float32
BF16 = jnp.bfloat16
I32 = jnp.int32

ROWS = 128
PACK = 4
SLOTS = 2
WIDTH = PACK * ROWS
KEPT = 3
BLOCK = 64
FRAMES = 4
PART = ROWS // FRAMES
OUT_ROWS = SLOTS * PACK
HALF = PACK // 2
BACK_ROWS = OUT_ROWS + HALF
CORES = 2
STEP = 64


def iota(dim, shape=(ROWS, ROWS)):
    return lax.broadcasted_iota(I32, shape, dim)


def mm(a, b):
    return jnp.dot(a, b, preferred_element_type=F32)


def mm_nt(a, b):
    return lax.dot_general(a, b, (((1,), (1,)), ((), ())), preferred_element_type=F32)


def mm_tn(a, b):
    return lax.dot_general(a, b, (((0,), (0,)), ((), ())), preferred_element_type=F32)


def to_bf(mask):
    return jnp.where(mask, 1.0, 0.0).astype(BF16)


def chunk(c):
    return slice(c * ROWS, (c + 1) * ROWS)


def as_column(row):
    return jnp.sum(jnp.where(iota(0) == iota(1), jnp.broadcast_to(row, (ROWS, ROWS)), 0.0), axis=1, keepdims=True)


def as_row(column):
    return jnp.sum(jnp.where(iota(0) == iota(1), jnp.broadcast_to(column, (ROWS, ROWS)), 0.0), axis=0, keepdims=True)


def owner_and_rank(dest_row):
    dest_f = dest_row.astype(F32)
    follows = (as_column(dest_f) + 1.0) == jnp.broadcast_to(dest_f, (ROWS, ROWS))
    rank = jnp.sum(jnp.where(follows, 1.0, 0.0), axis=0, keepdims=True)
    return (dest_row // ROWS).astype(F32), jnp.where(dest_row % ROWS == 0, 0.0, rank)


def pack_kernel(id_ref, dest_hbm, enc_hbm, pred_hbm, w_hbm, out_hbm, dec_ref, dest_ref, enc_ref, pred_ref, w_ref, wire_ref, out_ref, sems):
    pairs = ((dest_hbm.at[id_ref[0] // FRAMES], dest_ref), (enc_hbm, enc_ref), (pred_hbm, pred_ref), (w_hbm, w_ref))
    copies = [pltpu.make_async_copy(src, dst, sems.at[i]) for i, (src, dst) in enumerate(pairs)]
    for copy in copies:
        copy.start()
    copies[0].wait()
    owner, rank = owner_and_rank(dest_ref[...])
    down = iota(0).astype(F32)
    picks = [to_bf((down == owner) & (rank == float(k))) for k in range(SLOTS)]
    copies[1].wait()
    owners = ROWS // 2
    for half in range(2):
        for k in range(SLOTS):
            picked = mm(picks[k][half * owners : (half + 1) * owners], enc_ref[...])
            for c in range(PACK):
                first = half * owners * OUT_ROWS + k * PACK + c
                wire_ref[pl.ds(first, owners, stride=OUT_ROWS), :] = picked[:, chunk(c)]
        rows = slice(half * owners * OUT_ROWS, (half + 1) * owners * OUT_ROWS)
        out_ref[rows, :] = wire_ref[rows, :].astype(BF16)
        copies.append(pltpu.make_async_copy(out_ref.at[rows], out_hbm.at[rows], sems.at[len(pairs) + half]))
        copies[-1].start()
    copies[2].wait()
    copies[3].wait()
    dec_ref[...] = mm(pred_ref[...], w_ref[...]).astype(BF16)
    for copy in copies[len(pairs) :]:
        copy.wait()


def base_row(off_ref, start_ref):
    lane = iota(1, (1, ROWS))
    return (start_ref[...] + jnp.where(lane < BLOCK, off_ref[0], off_ref[1])).astype(F32)


def prep_kernel(
    id_ref, off_ref, dest_ref, start_ref, label_ref, w_ref, bias_ref,
    into_ref, from_ref, home_ref, here_ref, table_ref, wide_ref, bias_out_ref,
):
    dest = dest_ref[...]
    mine = to_bf(dest // ROWS == id_ref[0] // FRAMES)
    ones = jnp.ones((ROWS, ROWS), BF16)
    count_row = mm_nt(ones, mine)
    count_col = mm(mine, ones)
    offset_row = mm(count_row.astype(BF16), to_bf(iota(0) < iota(1)))
    offset_col = mm(to_bf(iota(1) < iota(0)), count_col.astype(BF16))
    owner, rank = owner_and_rank(dest_ref[pl.ds(id_ref[0] // FRAMES, 1), :])
    owner = as_column(owner)
    rank = as_column(rank)
    down = iota(0).astype(F32)
    along = iota(1).astype(F32)
    for k in range(SLOTS):
        into_ref[k] = to_bf((offset_row + float(k) == down) & (count_row > float(k)))
        from_ref[k] = to_bf((offset_col + float(k) == along) & (count_col > float(k)))
        home_ref[k] = to_bf((owner == along) & (rank == float(k)))
    base = as_column(base_row(off_ref, start_ref))
    labels = label_ref[...].astype(F32)
    table = jnp.zeros((ROWS, ROWS), F32)
    frame = id_ref[0] % FRAMES
    held = (((frame + FRAMES - iota(1) // PART) % FRAMES) * PART + iota(1) % PART).astype(F32)
    for k in range(KEPT):
        here_ref[k * ROWS : (k + 1) * ROWS, :] = to_bf(held == base + float(k))
        emitted = jnp.sum(jnp.where(along == base + float(k), labels, 0.0), axis=1, keepdims=True)
        table = jnp.where(iota(1) == k, emitted, table)
    table_ref[...] = table
    vocab = w_ref.shape[1]
    wide_ref[...] = jnp.zeros_like(wide_ref)
    wide_ref[:, 0:vocab] = w_ref[...]
    bias_out_ref[...] = jnp.full_like(bias_out_ref, -1e30)
    bias_out_ref[:, 0:vocab] = bias_ref[...]


def take_slot(wire_ref, slot, rows):
    return jnp.concatenate([wire_ref[pl.ds(slot * PACK + c, ROWS, stride=rows), :] for c in range(PACK)], axis=1)


def enter_kernel(wire_ref, into_ref, w_enc_ref, out_ref, float_ref):
    float_ref[...] = wire_ref[...].astype(F32)
    owned = jnp.zeros((ROWS, WIDTH), F32)
    for k in range(SLOTS):
        owned = owned + mm(into_ref[k], take_slot(float_ref, k, OUT_ROWS).astype(BF16))
    out_ref[...] = mm(owned.astype(BF16), w_enc_ref[...])


def joint_kernel(
    enc_ref, here_ref, dec0_ref, dec1_ref, dec2_ref, dec3_ref, table_ref, w_out_ref, bias_ref,
    cot_blank_ref, cot_label_ref, logprob_ref, hidden_ref, dlogit_ref, grad_hbm, turn_ref, turned_ref, logit_ref,
    grad_ref, sems,
):
    enc_joint = enc_ref[...]
    dec = jnp.concatenate([dec0_ref[...], dec1_ref[...], dec2_ref[...], dec3_ref[...]], axis=0)
    dec_rows = mm(here_ref[...], dec)
    for k in range(KEPT):
        rows = slice(k * ROWS, (k + 1) * ROWS)
        hidden = jnp.tanh(enc_joint + dec_rows[rows, :]).astype(BF16)
        hidden_ref[rows, :] = hidden
        turn_ref[k] = hidden.astype(F32).T
        for f in range(FRAMES):
            turned_ref[chunk(f), rows] = turn_ref.at[k][pl.ds(f, ROWS, stride=FRAMES), :].astype(BF16)
    logit_ref[...] = mm(hidden_ref[...], w_out_ref[...])
    lane = iota(1, (STEP, WIDTH))
    first = iota(1, (STEP, ROWS)) == 0
    for k in range(KEPT):
        for r in range(0, ROWS, STEP):
            rows = slice(k * ROWS + r, k * ROWS + r + STEP)
            part = slice(r, r + STEP)
            logits = logit_ref[rows, :] + bias_ref[...]
            shifted = logits - jnp.max(logits, axis=1, keepdims=True)
            power = jnp.exp(shifted)
            total = jnp.sum(power, axis=1, keepdims=True)
            log_total = jnp.log(total)
            is_label = lane == table_ref[part, k : k + 1].astype(I32)
            at_label = jnp.sum(jnp.where(is_label, shifted, 0.0), axis=1, keepdims=True)
            logprob_ref[part, k : k + 1] = shifted[:, 0:1] - log_total
            logprob_ref[part, KEPT + k : KEPT + k + 1] = at_label - log_total
            cot_blank = cot_blank_ref[part, k : k + 1]
            cot_label = cot_label_ref[part, k : k + 1]
            scale = (cot_blank + cot_label) / total
            dlogit = jnp.where(is_label, cot_label, 0.0) - power * scale
            dlogit_ref[rows, chunk(0)] = (dlogit[:, chunk(0)] + jnp.where(first, cot_blank, 0.0)).astype(BF16)
            dlogit_ref[rows, ROWS:WIDTH] = dlogit[:, ROWS:WIDTH].astype(BF16)
    copies = []
    for core in range(CORES):
        half = slice(core * WIDTH, (core + 1) * WIDTH)
        columns = slice(core * HALF * ROWS, (core + 1) * HALF * ROWS)
        grad_ref[half, :] = mm(turned_ref[...], dlogit_ref[:, columns]).astype(BF16)
        copies.append(pltpu.make_async_copy(grad_ref.at[half], grad_hbm.at[half], sems.at[core]))
        copies[-1].start()
    for copy in copies:
        copy.wait()


def back_kernel(
    id_ref, off_ref, start_ref, from_ref, hidden_ref, dlogit_ref, w_enc_ref, w_out_ref, logprob_ref,
    row_ref, plane_ref, dec0_ref, dec1_ref, dec2_ref, dec3_ref,
):
    for i in range(2 * KEPT):
        row_ref[i : i + 1, :] = as_row(logprob_ref[:, i : i + 1])
    base = base_row(off_ref, start_ref)
    frame = id_ref[0] % FRAMES
    sent = (((frame + iota(0) // PART) % FRAMES) * PART + iota(0) % PART).astype(F32)
    enc_grad = jnp.zeros((ROWS, WIDTH), F32)
    dec_grad = jnp.zeros((ROWS, WIDTH), F32)
    for k in range(KEPT):
        rows = slice(k * ROWS, (k + 1) * ROWS)
        hidden = hidden_ref[rows, :].astype(F32)
        dz = mm_nt(dlogit_ref[rows, :], w_out_ref[...]) * (1.0 - hidden * hidden)
        enc_grad = enc_grad + dz
        here = to_bf(sent == base + float(k))
        high = dz.astype(BF16)
        low = (dz - high.astype(F32)).astype(BF16)
        dec_grad = dec_grad + mm(here, high) + mm(here, low)
    dec_grad = dec_grad.astype(BF16)
    for f, ref in enumerate((dec0_ref, dec1_ref, dec2_ref, dec3_ref)):
        ref[...] = dec_grad[f * PART : (f + 1) * PART, :]
    owned = mm_nt(enc_grad.astype(BF16), w_enc_ref[...]).astype(BF16)
    for k in range(SLOTS):
        plane_ref[chunk(k), :] = mm(from_ref[k], owned).astype(BF16)


def merge_kernel(parts_ref, plane_ref, out_hbm, float_ref, out_ref, sems):
    owners = ROWS // 2
    copies = []
    for half in range(2):
        base = half * owners
        for k in range(SLOTS):
            for c in range(PACK):
                plane = plane_ref[k * ROWS + base : k * ROWS + base + owners, chunk(c)].astype(F32)
                float_ref[pl.ds(base * BACK_ROWS + k * PACK + c, owners, stride=BACK_ROWS), :] = plane
        for h in range(HALF):
            total = parts_ref[base : base + owners, chunk(h)].astype(F32)
            for i in range(1, CORES * FRAMES):
                total = total + parts_ref[i * ROWS + base : i * ROWS + base + owners, chunk(h)].astype(F32)
            float_ref[pl.ds(base * BACK_ROWS + OUT_ROWS + h, owners, stride=BACK_ROWS), :] = total
        rows = slice(base * BACK_ROWS, (base + owners) * BACK_ROWS)
        out_ref[rows, :] = float_ref[rows, :].astype(BF16)
        copies.append(pltpu.make_async_copy(out_ref.at[rows], out_hbm.at[rows], sems.at[half]))
        copies[-1].start()
    for copy in copies:
        copy.wait()


def pred_kernel(part0_ref, part1_ref, part2_ref, part3_ref, w_ref, out_ref):
    total = part0_ref[...].astype(F32) + part1_ref[...].astype(F32)
    total = total + (part2_ref[...].astype(F32) + part3_ref[...].astype(F32))
    high = total.astype(BF16)
    low = (total - high.astype(F32)).astype(BF16)
    out_ref[...] = mm_nt(high, w_ref[...]) + mm_nt(low, w_ref[...])


def unpack_kernel(home_ref, wire_ref, enc_ref, grad_ref, float_ref):
    float_ref[...] = wire_ref[...].astype(F32)
    rows = jnp.zeros((ROWS, WIDTH), F32)
    for k in range(SLOTS):
        rows = rows + mm(home_ref[k], take_slot(float_ref, k, BACK_ROWS).astype(BF16))
    enc_ref[...] = rows.astype(BF16)
    quarters = []
    for core in range(CORES):
        for h in range(HALF):
            first = core * BACK_ROWS + OUT_ROWS + h
            from_core = float_ref[pl.ds(first, ROWS // CORES, stride=CORES * BACK_ROWS), :]
            quarters.append(jnp.sum(from_core, axis=0, keepdims=True))
    term = jnp.concatenate(quarters, axis=1)
    grad_ref[...] = term[:, 0 : grad_ref.shape[1]]


VM = pl.BlockSpec(memory_space=pltpu.VMEM)
SM = pl.BlockSpec(memory_space=pltpu.SMEM)
HBM = pl.BlockSpec(memory_space=pltpu.HBM)


def call(kernel, name, outs, specs, scratch=(), flops=0, bytes_accessed=0, limit=24 << 20, out_specs=None):
    return pl.pallas_call(
        kernel,
        name=name,
        out_shape=outs,
        in_specs=list(specs),
        out_specs=jax.tree.map(lambda _: VM, outs) if out_specs is None else out_specs,
        scratch_shapes=list(scratch),
        compiler_params=pltpu.CompilerParams(vmem_limit_bytes=limit),
        cost_estimate=pl.CostEstimate(flops=flops, bytes_accessed=bytes_accessed, transcendentals=0),
    )


def out(shape, dtype):
    return jax.ShapeDtypeStruct(shape, dtype)


DP = ("z", "x", "core")
EVERY = DP + ("frame",)


def to_frame(array, ahead):
    return lax.ppermute(array, "frame", [(f, (f + ahead) % FRAMES) for f in range(FRAMES)])


def shards(
    enc_rows, dest, pred_rows, label_ids, block_off, band_start, w_enc, w_dec, w_out, bias_out, grad_blank, grad_label
):
    me = lax.axis_index(EVERY).astype(I32).reshape(1)
    flat_dest = dest.reshape(ROWS, ROWS)
    start = band_start.reshape(1, ROWS)
    bias = bias_out.reshape(1, -1)
    part = out((PART, WIDTH), BF16)
    pick = out((SLOTS, ROWS, ROWS), BF16)

    wire, dec = call(
        pack_kernel,
        "pack",
        (out((ROWS * OUT_ROWS, ROWS), BF16), part),
        [SM, HBM, HBM, HBM, HBM],
        [
            pltpu.VMEM((1, ROWS), I32),
            pltpu.VMEM((ROWS, WIDTH), BF16),
            pltpu.VMEM((PART, WIDTH), BF16),
            pltpu.VMEM((WIDTH, WIDTH), BF16),
            pltpu.VMEM((ROWS * OUT_ROWS, ROWS), F32),
            pltpu.VMEM((ROWS * OUT_ROWS, ROWS), BF16),
            pltpu.SemaphoreType.DMA((6,)),
        ],
        flops=40000000,
        bytes_accessed=400000,
        limit=None,
        out_specs=(HBM, VM),
    )(me, dest, enc_rows, pred_rows, w_dec)
    wire = lax.all_to_all(wire, DP, 0, 0, tiled=True)
    into, out_of, home, here, table, wide, wide_bias = call(
        prep_kernel,
        "prep",
        (pick, pick, pick, out((KEPT * ROWS, ROWS), BF16), out((ROWS, ROWS), F32), out((WIDTH, WIDTH), BF16), out((1, WIDTH), F32)),
        [SM, SM] + [VM] * 5,
        flops=100000000,
        bytes_accessed=2000000,
    )(me, block_off, flat_dest, start, label_ids, w_out, bias)
    enc_joint = call(
        enter_kernel,
        "enter",
        out((ROWS, WIDTH), F32),
        [VM] * 3,
        [pltpu.VMEM((ROWS * OUT_ROWS, ROWS), F32)],
        flops=100000000,
        bytes_accessed=1000000,
    )(wire, into, w_enc)
    logprobs, hidden, dlogit, term = call(
        joint_kernel,
        "joint",
        (
            out((ROWS, 2 * KEPT), F32),
            out((KEPT * ROWS, WIDTH), BF16),
            out((KEPT * ROWS, WIDTH), BF16),
            out((CORES * WIDTH, WIDTH // CORES), BF16),
        ),
        [VM] * 11,
        [
            pltpu.VMEM((KEPT, WIDTH, ROWS), F32),
            pltpu.VMEM((WIDTH, KEPT * ROWS), BF16),
            pltpu.VMEM((KEPT * ROWS, WIDTH), F32),
            pltpu.VMEM((CORES * WIDTH, WIDTH // CORES), BF16),
            pltpu.SemaphoreType.DMA((CORES,)),
        ],
        flops=500000000,
        bytes_accessed=3000000,
        out_specs=(VM, VM, VM, HBM),
    )(enc_joint, here, dec, to_frame(dec, 1), to_frame(dec, 2), to_frame(dec, 3), table, wide, wide_bias, grad_blank, grad_label)
    term = lax.all_to_all(term, ("core", "frame"), 0, 0, tiled=True)
    rows, planes, dec0, dec1, dec2, dec3 = call(
        back_kernel,
        "back",
        (out((2 * KEPT, ROWS), F32), out((SLOTS * ROWS, WIDTH), BF16), part, part, part, part),
        [SM, SM] + [VM] * 7,
        flops=500000000,
        bytes_accessed=3000000,
    )(me, block_off, start, out_of, hidden, dlogit, w_enc, wide, logprobs)
    back = call(
        merge_kernel,
        "merge",
        out((ROWS * BACK_ROWS, ROWS), BF16),
        [VM, VM],
        [
            pltpu.VMEM((ROWS * BACK_ROWS, ROWS), F32),
            pltpu.VMEM((ROWS * BACK_ROWS, ROWS), BF16),
            pltpu.SemaphoreType.DMA((2,)),
        ],
        flops=300000,
        bytes_accessed=1700000,
        out_specs=HBM,
    )(term, planes)
    back, dec1, dec2 = lax.optimization_barrier((back, dec1, dec2))
    back = lax.all_to_all(back.reshape(ROWS * BACK_ROWS // 2, 2, ROWS), DP, 0, 0, tiled=True)
    back = back.reshape(ROWS * BACK_ROWS, ROWS)
    grad_pred = call(
        pred_kernel,
        "pred",
        out((PART, WIDTH), F32),
        [VM] * 5,
        flops=40000000,
        bytes_accessed=700000,
    )(dec0, to_frame(dec1, 1), to_frame(dec2, 2), to_frame(dec3, 3), w_dec)
    grad_enc, grad_w_out = call(
        unpack_kernel,
        "unpack",
        (out((ROWS, WIDTH), BF16), out((1, w_out.shape[1]), F32)),
        [VM, VM],
        [pltpu.VMEM((ROWS * BACK_ROWS, ROWS), F32)],
        flops=40000000,
        bytes_accessed=600000,
    )(home, back)
    return (rows.T, grad_enc, grad_pred, grad_w_out)


def solution(mesh):
    fine = Mesh(mesh.devices.reshape(16, 4, 2, 4), EVERY)
    return jax.shard_map(
        shards,
        mesh=fine,
        in_specs=(
            P(EVERY, None),
            P(None, "frame", None),
            P(EVERY, None),
            P(DP, None),
            P(EVERY),
            P(EVERY),
            P(),
            P(),
            P(),
            P(),
            P(EVERY, None),
            P(EVERY, None),
        ),
        out_specs=(P(EVERY, None), P(EVERY, None), P(EVERY, None), P(EVERY, None)),
        check_vma=False,
    )
```

```python
import jax
import jax.numpy as jnp
from jax import lax
from jax.experimental import pallas as pl
from jax.experimental.pallas import tpu as pltpu
from jax.sharding import Mesh
from jax.sharding import PartitionSpec as P

F32 = jnp.float32
BF16 = jnp.bfloat16
I32 = jnp.int32

ROWS = 128
PACK = 4
SLOTS = 2
WIDTH = PACK * ROWS
KEPT = 3
BLOCK = 64
FRAMES = 4
PART = ROWS // FRAMES
OUT_ROWS = SLOTS * PACK
HALF = PACK // 2
BACK_ROWS = OUT_ROWS + HALF
CORES = 2
STEP = 64


def iota(dim, shape=(ROWS, ROWS)):
    return lax.broadcasted_iota(I32, shape, dim)


def mm(a, b):
    return jnp.dot(a, b, preferred_element_type=F32)


def mm_nt(a, b):
    return lax.dot_general(a, b, (((1,), (1,)), ((), ())), preferred_element_type=F32)


def mm_tn(a, b):
    return lax.dot_general(a, b, (((0,), (0,)), ((), ())), preferred_element_type=F32)


def to_bf(mask):
    return jnp.where(mask, 1.0, 0.0).astype(BF16)


def chunk(c):
    return slice(c * ROWS, (c + 1) * ROWS)


def as_column(row):
    return jnp.sum(jnp.where(iota(0) == iota(1), jnp.broadcast_to(row, (ROWS, ROWS)), 0.0), axis=1, keepdims=True)


def as_row(column):
    return jnp.sum(jnp.where(iota(0) == iota(1), jnp.broadcast_to(column, (ROWS, ROWS)), 0.0), axis=0, keepdims=True)


def owner_and_rank(dest_row):
    dest_f = dest_row.astype(F32)
    follows = (as_column(dest_f) + 1.0) == jnp.broadcast_to(dest_f, (ROWS, ROWS))
    rank = jnp.sum(jnp.where(follows, 1.0, 0.0), axis=0, keepdims=True)
    return (dest_row // ROWS).astype(F32), jnp.where(dest_row % ROWS == 0, 0.0, rank)


def pack_kernel(id_ref, dest_hbm, enc_hbm, pred_hbm, w_hbm, out_hbm, dec_hbm, dest_ref, enc_ref, pred_ref, w_ref, wire_ref, out_ref, dec_ref, sems):
    pairs = ((dest_hbm.at[id_ref[0] // FRAMES], dest_ref), (enc_hbm, enc_ref), (pred_hbm, pred_ref), (w_hbm, w_ref))
    copies = [pltpu.make_async_copy(src, dst, sems.at[i]) for i, (src, dst) in enumerate(pairs)]
    for copy in copies:
        copy.start()
    copies[0].wait()
    owner, rank = owner_and_rank(dest_ref[...])
    down = iota(0).astype(F32)
    picks = [to_bf((down == owner) & (rank == float(k))) for k in range(SLOTS)]
    copies[1].wait()
    owners = ROWS // 2
    for half in range(2):
        for k in range(SLOTS):
            picked = mm(picks[k][half * owners : (half + 1) * owners], enc_ref[...])
            for c in range(PACK):
                first = half * owners * OUT_ROWS + k * PACK + c
                wire_ref[pl.ds(first, owners, stride=OUT_ROWS), :] = picked[:, chunk(c)]
        rows = slice(half * owners * OUT_ROWS, (half + 1) * owners * OUT_ROWS)
        out_ref[rows, :] = wire_ref[rows, :].astype(BF16)
        copies.append(pltpu.make_async_copy(out_ref.at[rows], out_hbm.at[rows], sems.at[len(pairs) + half]))
        copies[-1].start()
    copies[2].wait()
    copies[3].wait()
    dec_ref[...] = mm(pred_ref[...], w_ref[...]).astype(BF16)
    copies.append(pltpu.make_async_copy(dec_ref, dec_hbm, sems.at[len(pairs) + 2]))
    copies[-1].start()
    for copy in copies[len(pairs) :]:
        copy.wait()


def base_row(off_ref, start_ref):
    lane = iota(1, (1, ROWS))
    return (start_ref[...] + jnp.where(lane < BLOCK, off_ref[0], off_ref[1])).astype(F32)


def prep_kernel(
    id_ref, off_ref, dest_ref, start_ref, label_ref, w_ref, bias_ref,
    into_ref, from_ref, home_ref, here_ref, table_ref, wide_ref, bias_out_ref,
):
    dest = dest_ref[...]
    mine = to_bf(dest // ROWS == id_ref[0] // FRAMES)
    ones = jnp.ones((ROWS, ROWS), BF16)
    count_row = mm_nt(ones, mine)
    count_col = mm(mine, ones)
    offset_row = mm(count_row.astype(BF16), to_bf(iota(0) < iota(1)))
    offset_col = mm(to_bf(iota(1) < iota(0)), count_col.astype(BF16))
    owner, rank = owner_and_rank(dest_ref[pl.ds(id_ref[0] // FRAMES, 1), :])
    owner = as_column(owner)
    rank = as_column(rank)
    down = iota(0).astype(F32)
    along = iota(1).astype(F32)
    for k in range(SLOTS):
        into_ref[k] = to_bf((offset_row + float(k) == down) & (count_row > float(k)))
        from_ref[k] = to_bf((offset_col + float(k) == along) & (count_col > float(k)))
        home_ref[k] = to_bf((owner == along) & (rank == float(k)))
    base = as_column(base_row(off_ref, start_ref))
    labels = label_ref[...].astype(F32)
    table = jnp.zeros((ROWS, ROWS), F32)
    frame = id_ref[0] % FRAMES
    held = (((frame + FRAMES - iota(1) // PART) % FRAMES) * PART + iota(1) % PART).astype(F32)
    for k in range(KEPT):
        here_ref[k * ROWS : (k + 1) * ROWS, :] = to_bf(held == base + float(k))
        emitted = jnp.sum(jnp.where(along == base + float(k), labels, 0.0), axis=1, keepdims=True)
        table = jnp.where(iota(1) == k, emitted, table)
    table_ref[...] = table
    vocab = w_ref.shape[1]
    wide_ref[...] = jnp.zeros_like(wide_ref)
    wide_ref[:, 0:vocab] = w_ref[...]
    bias_out_ref[...] = jnp.full_like(bias_out_ref, -1e30)
    bias_out_ref[:, 0:vocab] = bias_ref[...]


def take_slot(wire_ref, slot, rows):
    return jnp.concatenate([wire_ref[pl.ds(slot * PACK + c, ROWS, stride=rows), :] for c in range(PACK)], axis=1)


def enter_kernel(wire_ref, into_ref, w_enc_ref, out_ref, float_ref):
    float_ref[...] = wire_ref[...].astype(F32)
    owned = jnp.zeros((ROWS, WIDTH), F32)
    for k in range(SLOTS):
        owned = owned + mm(into_ref[k], take_slot(float_ref, k, OUT_ROWS).astype(BF16))
    out_ref[...] = mm(owned.astype(BF16), w_enc_ref[...])


def joint_kernel(
    enc_ref, here_ref, dec0_ref, dec1_ref, dec2_ref, dec3_ref, table_ref, w_out_ref, bias_ref,
    cot_blank_ref, cot_label_ref, logprob_ref, hidden_ref, dlogit_ref, grad_hbm, turn_ref, turned_ref, logit_ref,
    grad_ref, sems,
):
    enc_joint = enc_ref[...]
    dec = jnp.concatenate([dec0_ref[...], dec1_ref[...], dec2_ref[...], dec3_ref[...]], axis=0)
    dec_rows = mm(here_ref[...], dec)
    for k in range(KEPT):
        rows = slice(k * ROWS, (k + 1) * ROWS)
        hidden = jnp.tanh(enc_joint + dec_rows[rows, :]).astype(BF16)
        hidden_ref[rows, :] = hidden
        turn_ref[k] = hidden.astype(F32).T
        for f in range(FRAMES):
            turned_ref[chunk(f), rows] = turn_ref.at[k][pl.ds(f, ROWS, stride=FRAMES), :].astype(BF16)
    logit_ref[...] = mm(hidden_ref[...], w_out_ref[...])
    lane = iota(1, (STEP, WIDTH))
    first = iota(1, (STEP, ROWS)) == 0
    for k in range(KEPT):
        for r in range(0, ROWS, STEP):
            rows = slice(k * ROWS + r, k * ROWS + r + STEP)
            part = slice(r, r + STEP)
            logits = logit_ref[rows, :] + bias_ref[...]
            shifted = logits - jnp.max(logits, axis=1, keepdims=True)
            power = jnp.exp(shifted)
            total = jnp.sum(power, axis=1, keepdims=True)
            log_total = jnp.log(total)
            is_label = lane == table_ref[part, k : k + 1].astype(I32)
            at_label = jnp.sum(jnp.where(is_label, shifted, 0.0), axis=1, keepdims=True)
            logprob_ref[part, k : k + 1] = shifted[:, 0:1] - log_total
            logprob_ref[part, KEPT + k : KEPT + k + 1] = at_label - log_total
            cot_blank = cot_blank_ref[part, k : k + 1]
            cot_label = cot_label_ref[part, k : k + 1]
            scale = (cot_blank + cot_label) / total
            dlogit = jnp.where(is_label, cot_label, 0.0) - power * scale
            dlogit_ref[rows, chunk(0)] = (dlogit[:, chunk(0)] + jnp.where(first, cot_blank, 0.0)).astype(BF16)
            dlogit_ref[rows, ROWS:WIDTH] = dlogit[:, ROWS:WIDTH].astype(BF16)
    copies = []
    for core in range(CORES):
        half = slice(core * WIDTH, (core + 1) * WIDTH)
        columns = slice(core * HALF * ROWS, (core + 1) * HALF * ROWS)
        grad_ref[half, :] = mm(turned_ref[...], dlogit_ref[:, columns]).astype(BF16)
        copies.append(pltpu.make_async_copy(grad_ref.at[half], grad_hbm.at[half], sems.at[core]))
        copies[-1].start()
    for copy in copies:
        copy.wait()


def back_kernel(
    id_ref, off_ref, start_ref, from_ref, hidden_ref, dlogit_ref, w_enc_ref, w_out_ref, logprob_ref,
    row_ref, plane_ref, dec0_ref, dec1_ref, dec2_ref, dec3_ref,
):
    for i in range(2 * KEPT):
        row_ref[i : i + 1, :] = as_row(logprob_ref[:, i : i + 1])
    base = base_row(off_ref, start_ref)
    frame = id_ref[0] % FRAMES
    sent = (((frame + iota(0) // PART) % FRAMES) * PART + iota(0) % PART).astype(F32)
    enc_grad = jnp.zeros((ROWS, WIDTH), F32)
    dec_grad = jnp.zeros((ROWS, WIDTH), F32)
    for k in range(KEPT):
        rows = slice(k * ROWS, (k + 1) * ROWS)
        hidden = hidden_ref[rows, :].astype(F32)
        dz = mm_nt(dlogit_ref[rows, :], w_out_ref[...]) * (1.0 - hidden * hidden)
        enc_grad = enc_grad + dz
        here = to_bf(sent == base + float(k))
        high = dz.astype(BF16)
        low = (dz - high.astype(F32)).astype(BF16)
        dec_grad = dec_grad + mm(here, high) + mm(here, low)
    dec_grad = dec_grad.astype(BF16)
    for f, ref in enumerate((dec0_ref, dec1_ref, dec2_ref, dec3_ref)):
        ref[...] = dec_grad[f * PART : (f + 1) * PART, :]
    owned = mm_nt(enc_grad.astype(BF16), w_enc_ref[...]).astype(BF16)
    for k in range(SLOTS):
        plane_ref[chunk(k), :] = mm(from_ref[k], owned).astype(BF16)


def merge_kernel(parts_ref, plane_ref, out_hbm, float_ref, out_ref, sems):
    owners = ROWS // 2
    copies = []
    for half in range(2):
        base = half * owners
        for k in range(SLOTS):
            for c in range(PACK):
                plane = plane_ref[k * ROWS + base : k * ROWS + base + owners, chunk(c)].astype(F32)
                float_ref[pl.ds(base * BACK_ROWS + k * PACK + c, owners, stride=BACK_ROWS), :] = plane
        for h in range(HALF):
            total = parts_ref[base : base + owners, chunk(h)].astype(F32)
            for i in range(1, CORES * FRAMES):
                total = total + parts_ref[i * ROWS + base : i * ROWS + base + owners, chunk(h)].astype(F32)
            float_ref[pl.ds(base * BACK_ROWS + OUT_ROWS + h, owners, stride=BACK_ROWS), :] = total
        rows = slice(base * BACK_ROWS, (base + owners) * BACK_ROWS)
        out_ref[rows, :] = float_ref[rows, :].astype(BF16)
        copies.append(pltpu.make_async_copy(out_ref.at[rows], out_hbm.at[rows], sems.at[half]))
        copies[-1].start()
    for copy in copies:
        copy.wait()


def pred_kernel(part0_ref, part1_ref, part2_ref, part3_ref, w_ref, out_ref):
    total = part0_ref[...].astype(F32) + part1_ref[...].astype(F32)
    total = total + (part2_ref[...].astype(F32) + part3_ref[...].astype(F32))
    high = total.astype(BF16)
    low = (total - high.astype(F32)).astype(BF16)
    out_ref[...] = mm_nt(high, w_ref[...]) + mm_nt(low, w_ref[...])


def unpack_kernel(home_ref, wire_ref, enc_hbm, grad_hbm, float_ref, enc_ref, grad_ref, sems):
    float_ref[...] = wire_ref[...].astype(F32)
    slots = [take_slot(float_ref, k, BACK_ROWS).astype(BF16) for k in range(SLOTS)]
    quarters = []
    for core in range(CORES):
        for h in range(HALF):
            first = core * BACK_ROWS + OUT_ROWS + h
            from_core = float_ref[pl.ds(first, ROWS // CORES, stride=CORES * BACK_ROWS), :]
            quarters.append(jnp.sum(from_core, axis=0, keepdims=True))
    term = jnp.concatenate(quarters, axis=1)
    grad_ref[...] = term[:, 0 : grad_ref.shape[1]]
    copies = [pltpu.make_async_copy(grad_ref, grad_hbm, sems.at[2])]
    copies[0].start()
    for half in range(2):
        part = slice(half * ROWS // 2, (half + 1) * ROWS // 2)
        rows = mm(home_ref[0, part, :], slots[0])
        for k in range(1, SLOTS):
            rows = rows + mm(home_ref[k, part, :], slots[k])
        enc_ref[part, :] = rows.astype(BF16)
        copies.append(pltpu.make_async_copy(enc_ref.at[part], enc_hbm.at[part], sems.at[half]))
        copies[-1].start()
    for copy in copies:
        copy.wait()


VM = pl.BlockSpec(memory_space=pltpu.VMEM)
SM = pl.BlockSpec(memory_space=pltpu.SMEM)
HBM = pl.BlockSpec(memory_space=pltpu.HBM)


def call(kernel, name, outs, specs, scratch=(), flops=0, bytes_accessed=0, limit=24 << 20, out_specs=None):
    return pl.pallas_call(
        kernel,
        name=name,
        out_shape=outs,
        in_specs=list(specs),
        out_specs=jax.tree.map(lambda _: VM, outs) if out_specs is None else out_specs,
        scratch_shapes=list(scratch),
        compiler_params=pltpu.CompilerParams(vmem_limit_bytes=limit),
        cost_estimate=pl.CostEstimate(flops=flops, bytes_accessed=bytes_accessed, transcendentals=0),
    )


def out(shape, dtype):
    return jax.ShapeDtypeStruct(shape, dtype)


DP = ("z", "x", "core")
EVERY = DP + ("frame",)


def to_frame(array, ahead):
    return lax.ppermute(array, "frame", [(f, (f + ahead) % FRAMES) for f in range(FRAMES)])


def shards(
    enc_rows, dest, pred_rows, label_ids, block_off, band_start, w_enc, w_dec, w_out, bias_out, grad_blank, grad_label
):
    me = lax.axis_index(EVERY).astype(I32).reshape(1)
    flat_dest = dest.reshape(ROWS, ROWS)
    start = band_start.reshape(1, ROWS)
    bias = bias_out.reshape(1, -1)
    part = out((PART, WIDTH), BF16)
    pick = out((SLOTS, ROWS, ROWS), BF16)

    wire, dec = call(
        pack_kernel,
        "pack",
        (out((ROWS * OUT_ROWS, ROWS), BF16), part),
        [SM, HBM, HBM, HBM, HBM],
        [
            pltpu.VMEM((1, ROWS), I32),
            pltpu.VMEM((ROWS, WIDTH), BF16),
            pltpu.VMEM((PART, WIDTH), BF16),
            pltpu.VMEM((WIDTH, WIDTH), BF16),
            pltpu.VMEM((ROWS * OUT_ROWS, ROWS), F32),
            pltpu.VMEM((ROWS * OUT_ROWS, ROWS), BF16),
            pltpu.VMEM((PART, WIDTH), BF16),
            pltpu.SemaphoreType.DMA((7,)),
        ],
        flops=40000000,
        bytes_accessed=400000,
        limit=None,
        out_specs=(HBM, HBM),
    )(me, dest, enc_rows, pred_rows, w_dec)
    wire = lax.all_to_all(wire, DP, 0, 0, tiled=True)
    into, out_of, home, here, table, wide, wide_bias = call(
        prep_kernel,
        "prep",
        (pick, pick, pick, out((KEPT * ROWS, ROWS), BF16), out((ROWS, ROWS), F32), out((WIDTH, WIDTH), BF16), out((1, WIDTH), F32)),
        [SM, SM] + [VM] * 5,
        flops=100000000,
        bytes_accessed=2000000,
    )(me, block_off, flat_dest, start, label_ids, w_out, bias)
    enc_joint = call(
        enter_kernel,
        "enter",
        out((ROWS, WIDTH), F32),
        [VM] * 3,
        [pltpu.VMEM((ROWS * OUT_ROWS, ROWS), F32)],
        flops=100000000,
        bytes_accessed=1000000,
    )(wire, into, w_enc)
    logprobs, hidden, dlogit, term = call(
        joint_kernel,
        "joint",
        (
            out((ROWS, 2 * KEPT), F32),
            out((KEPT * ROWS, WIDTH), BF16),
            out((KEPT * ROWS, WIDTH), BF16),
            out((CORES * WIDTH, WIDTH // CORES), BF16),
        ),
        [VM] * 11,
        [
            pltpu.VMEM((KEPT, WIDTH, ROWS), F32),
            pltpu.VMEM((WIDTH, KEPT * ROWS), BF16),
            pltpu.VMEM((KEPT * ROWS, WIDTH), F32),
            pltpu.VMEM((CORES * WIDTH, WIDTH // CORES), BF16),
            pltpu.SemaphoreType.DMA((CORES,)),
        ],
        flops=500000000,
        bytes_accessed=3000000,
        out_specs=(VM, VM, VM, HBM),
    )(enc_joint, here, dec, to_frame(dec, 1), to_frame(dec, 2), to_frame(dec, 3), table, wide, wide_bias, grad_blank, grad_label)
    term = lax.all_to_all(term, ("core", "frame"), 0, 0, tiled=True)
    rows, planes, dec0, dec1, dec2, dec3 = call(
        back_kernel,
        "back",
        (out((2 * KEPT, ROWS), F32), out((SLOTS * ROWS, WIDTH), BF16), part, part, part, part),
        [SM, SM] + [VM] * 7,
        flops=500000000,
        bytes_accessed=3000000,
    )(me, block_off, start, out_of, hidden, dlogit, w_enc, wide, logprobs)
    back = call(
        merge_kernel,
        "merge",
        out((ROWS * BACK_ROWS, ROWS), BF16),
        [VM, VM],
        [
            pltpu.VMEM((ROWS * BACK_ROWS, ROWS), F32),
            pltpu.VMEM((ROWS * BACK_ROWS, ROWS), BF16),
            pltpu.SemaphoreType.DMA((2,)),
        ],
        flops=300000,
        bytes_accessed=1700000,
        out_specs=HBM,
    )(term, planes)
    back, dec1, dec2 = lax.optimization_barrier((back, dec1, dec2))
    back = lax.all_to_all(back.reshape(ROWS * BACK_ROWS // 2, 2, ROWS), DP, 0, 0, tiled=True)
    back = back.reshape(ROWS * BACK_ROWS, ROWS)
    grad_pred = call(
        pred_kernel,
        "pred",
        out((PART, WIDTH), F32),
        [VM] * 5,
        flops=40000000,
        bytes_accessed=700000,
    )(dec0, to_frame(dec1, 1), to_frame(dec2, 2), to_frame(dec3, 3), w_dec)
    grad_enc, grad_w_out = call(
        unpack_kernel,
        "unpack",
        (out((ROWS, WIDTH), BF16), out((1, w_out.shape[1]), F32)),
        [VM, VM],
        [
            pltpu.VMEM((ROWS * BACK_ROWS, ROWS), F32),
            pltpu.VMEM((ROWS, WIDTH), BF16),
            pltpu.VMEM((1, w_out.shape[1]), F32),
            pltpu.SemaphoreType.DMA((3,)),
        ],
        flops=40000000,
        bytes_accessed=600000,
        out_specs=(HBM, HBM),
    )(home, back)
    return (rows.T, grad_enc, grad_pred, grad_w_out)


def solution(mesh):
    fine = Mesh(mesh.devices.reshape(16, 4, 2, 4), EVERY)
    return jax.shard_map(
        shards,
        mesh=fine,
        in_specs=(
            P(EVERY, None),
            P(None, "frame", None),
            P(EVERY, None),
            P(DP, None),
            P(EVERY),
            P(EVERY),
            P(),
            P(),
            P(),
            P(),
            P(EVERY, None),
            P(EVERY, None),
        ),
        out_specs=(P(EVERY, None), P(EVERY, None), P(EVERY, None), P(EVERY, None)),
        check_vma=False,
    )
```

```python
import jax
import jax.numpy as jnp
from jax import lax
from jax.experimental import pallas as pl
from jax.experimental.pallas import tpu as pltpu
from jax.sharding import Mesh
from jax.sharding import PartitionSpec as P

F32 = jnp.float32
BF16 = jnp.bfloat16
I32 = jnp.int32

ROWS = 128
PACK = 4
SLOTS = 2
WIDTH = PACK * ROWS
KEPT = 3
BLOCK = 64
FRAMES = 4
PART = ROWS // FRAMES
OUT_ROWS = SLOTS * PACK
HALF = PACK // 2
BACK_ROWS = OUT_ROWS + HALF
CORES = 2
TURN = ROWS // 2
STEP = 64


def iota(dim, shape=(ROWS, ROWS)):
    return lax.broadcasted_iota(I32, shape, dim)


def mm(a, b):
    return jnp.dot(a, b, preferred_element_type=F32)


def mm_nt(a, b):
    return lax.dot_general(a, b, (((1,), (1,)), ((), ())), preferred_element_type=F32)


def mm_tn(a, b):
    return lax.dot_general(a, b, (((0,), (0,)), ((), ())), preferred_element_type=F32)


def to_bf(mask):
    return jnp.where(mask, 1.0, 0.0).astype(BF16)


def chunk(c):
    return slice(c * ROWS, (c + 1) * ROWS)


def as_column(row):
    return jnp.sum(jnp.where(iota(0) == iota(1), jnp.broadcast_to(row, (ROWS, ROWS)), 0.0), axis=1, keepdims=True)


def as_row(column):
    return jnp.sum(jnp.where(iota(0) == iota(1), jnp.broadcast_to(column, (ROWS, ROWS)), 0.0), axis=0, keepdims=True)


def owner_and_rank(dest_row):
    dest_f = dest_row.astype(F32)
    follows = (as_column(dest_f) + 1.0) == jnp.broadcast_to(dest_f, (ROWS, ROWS))
    rank = jnp.sum(jnp.where(follows, 1.0, 0.0), axis=0, keepdims=True)
    return member(dest_row // ROWS).astype(F32), jnp.where(dest_row % ROWS == 0, 0.0, rank)


def pack_kernel(id_ref, dest_hbm, enc_hbm, pred_hbm, w_hbm, out_hbm, dec_hbm, dest_ref, enc_ref, pred_ref, w_ref, wire_ref, out_ref, dec_ref, sems):
    pairs = ((dest_hbm.at[id_ref[0] // FRAMES], dest_ref), (enc_hbm, enc_ref), (pred_hbm, pred_ref), (w_hbm, w_ref))
    copies = [pltpu.make_async_copy(src, dst, sems.at[i]) for i, (src, dst) in enumerate(pairs)]
    for copy in copies:
        copy.start()
    copies[0].wait()
    owner, rank = owner_and_rank(dest_ref[...])
    down = iota(0).astype(F32)
    picks = [to_bf((down == owner) & (rank == float(k))) for k in range(SLOTS)]
    copies[1].wait()
    owners = ROWS // 2
    for half in range(2):
        for k in range(SLOTS):
            picked = mm(picks[k][half * owners : (half + 1) * owners], enc_ref[...])
            for c in range(PACK):
                first = half * owners * OUT_ROWS + k * PACK + c
                wire_ref[pl.ds(first, owners, stride=OUT_ROWS), :] = picked[:, chunk(c)]
        rows = slice(half * owners * OUT_ROWS, (half + 1) * owners * OUT_ROWS)
        out_ref[rows, :] = wire_ref[rows, :].astype(BF16)
        copies.append(pltpu.make_async_copy(out_ref.at[rows], out_hbm.at[rows], sems.at[len(pairs) + half]))
        copies[-1].start()
    copies[2].wait()
    copies[3].wait()
    dec_ref[...] = mm(pred_ref[...], w_ref[...]).astype(BF16)
    copies.append(pltpu.make_async_copy(dec_ref, dec_hbm, sems.at[len(pairs) + 2]))
    copies[-1].start()
    for copy in copies[len(pairs) :]:
        copy.wait()


def base_row(off_ref, start_ref):
    lane = iota(1, (1, ROWS))
    return (start_ref[...] + jnp.where(lane < BLOCK, off_ref[0], off_ref[1])).astype(F32)


def prep_kernel(
    id_ref, off_ref, dest_ref, start_ref, label_ref, w_ref, bias_ref,
    into_ref, from_ref, home_ref, here_ref, table_ref, wide_ref, bias_out_ref,
):
    dest = jnp.concatenate([dest_ref[TURN:ROWS, :], dest_ref[0:TURN, :]], axis=0)
    mine = to_bf(dest // ROWS == id_ref[0] // FRAMES)
    ones = jnp.ones((ROWS, ROWS), BF16)
    count_row = mm_nt(ones, mine)
    count_col = mm(mine, ones)
    offset_row = mm(count_row.astype(BF16), to_bf(member(iota(0)) < member(iota(1))))
    offset_col = mm(to_bf(member(iota(1)) < member(iota(0))), count_col.astype(BF16))
    owner, rank = owner_and_rank(dest_ref[pl.ds(id_ref[0] // FRAMES, 1), :])
    owner = as_column(owner)
    rank = as_column(rank)
    down = iota(0).astype(F32)
    along = iota(1).astype(F32)
    for k in range(SLOTS):
        into_ref[k] = to_bf((offset_row + float(k) == down) & (count_row > float(k)))
        from_ref[k] = to_bf((offset_col + float(k) == along) & (count_col > float(k)))
        home_ref[k] = to_bf((owner == along) & (rank == float(k)))
    base = as_column(base_row(off_ref, start_ref))
    labels = label_ref[...].astype(F32)
    table = jnp.zeros((ROWS, ROWS), F32)
    frame = id_ref[0] % FRAMES
    held = (((frame + FRAMES - iota(1) // PART) % FRAMES) * PART + iota(1) % PART).astype(F32)
    for k in range(KEPT):
        here_ref[k * ROWS : (k + 1) * ROWS, :] = to_bf(held == base + float(k))
        emitted = jnp.sum(jnp.where(along == base + float(k), labels, 0.0), axis=1, keepdims=True)
        table = jnp.where(iota(1) == k, emitted, table)
    table_ref[...] = table
    vocab = w_ref.shape[1]
    wide_ref[...] = jnp.zeros_like(wide_ref)
    wide_ref[:, 0:vocab] = w_ref[...]
    bias_out_ref[...] = jnp.full_like(bias_out_ref, -1e30)
    bias_out_ref[:, 0:vocab] = bias_ref[...]


def take_slot(wire_ref, slot, rows):
    return jnp.concatenate([wire_ref[pl.ds(slot * PACK + c, ROWS, stride=rows), :] for c in range(PACK)], axis=1)


def enter_kernel(wire_ref, into_ref, w_enc_ref, out_ref, float_ref):
    float_ref[...] = wire_ref[...].astype(F32)
    owned = jnp.zeros((ROWS, WIDTH), F32)
    for k in range(SLOTS):
        owned = owned + mm(into_ref[k], take_slot(float_ref, k, OUT_ROWS).astype(BF16))
    out_ref[...] = mm(owned.astype(BF16), w_enc_ref[...])


def joint_kernel(
    enc_ref, here_ref, dec0_ref, dec1_ref, dec2_ref, dec3_ref, table_ref, w_out_ref, bias_ref,
    cot_blank_ref, cot_label_ref, logprob_ref, hidden_ref, dlogit_ref, grad_hbm, turn_ref, turned_ref, logit_ref,
    grad_ref, sems,
):
    enc_joint = enc_ref[...]
    dec = jnp.concatenate([dec0_ref[...], dec1_ref[...], dec2_ref[...], dec3_ref[...]], axis=0)
    dec_rows = mm(here_ref[...], dec)
    for k in range(KEPT):
        rows = slice(k * ROWS, (k + 1) * ROWS)
        hidden = jnp.tanh(enc_joint + dec_rows[rows, :]).astype(BF16)
        hidden_ref[rows, :] = hidden
        turn_ref[k] = hidden.astype(F32).T
        for f in range(FRAMES):
            turned_ref[chunk(f), rows] = turn_ref.at[k][pl.ds(f, ROWS, stride=FRAMES), :].astype(BF16)
    logit_ref[...] = mm(hidden_ref[...], w_out_ref[...])
    lane = iota(1, (STEP, WIDTH))
    first = iota(1, (STEP, ROWS)) == 0
    for k in range(KEPT):
        for r in range(0, ROWS, STEP):
            rows = slice(k * ROWS + r, k * ROWS + r + STEP)
            part = slice(r, r + STEP)
            logits = logit_ref[rows, :] + bias_ref[...]
            shifted = logits - jnp.max(logits, axis=1, keepdims=True)
            power = jnp.exp(shifted)
            total = jnp.sum(power, axis=1, keepdims=True)
            log_total = jnp.log(total)
            is_label = lane == table_ref[part, k : k + 1].astype(I32)
            at_label = jnp.sum(jnp.where(is_label, shifted, 0.0), axis=1, keepdims=True)
            logprob_ref[part, k : k + 1] = shifted[:, 0:1] - log_total
            logprob_ref[part, KEPT + k : KEPT + k + 1] = at_label - log_total
            cot_blank = cot_blank_ref[part, k : k + 1]
            cot_label = cot_label_ref[part, k : k + 1]
            scale = (cot_blank + cot_label) / total
            dlogit = jnp.where(is_label, cot_label, 0.0) - power * scale
            dlogit_ref[rows, chunk(0)] = (dlogit[:, chunk(0)] + jnp.where(first, cot_blank, 0.0)).astype(BF16)
            dlogit_ref[rows, ROWS:WIDTH] = dlogit[:, ROWS:WIDTH].astype(BF16)
    copies = []
    for core in range(CORES):
        half = slice(core * WIDTH, (core + 1) * WIDTH)
        columns = slice(core * HALF * ROWS, (core + 1) * HALF * ROWS)
        grad_ref[half, :] = mm(turned_ref[...], dlogit_ref[:, columns]).astype(BF16)
        copies.append(pltpu.make_async_copy(grad_ref.at[half], grad_hbm.at[half], sems.at[core]))
        copies[-1].start()
    for copy in copies:
        copy.wait()


def back_kernel(
    id_ref, off_ref, start_ref, from_ref, hidden_ref, dlogit_ref, w_enc_ref, w_out_ref, logprob_ref,
    row_ref, plane_ref, dec0_ref, dec1_ref, dec2_ref, dec3_ref,
):
    for i in range(2 * KEPT):
        row_ref[i : i + 1, :] = as_row(logprob_ref[:, i : i + 1])
    base = base_row(off_ref, start_ref)
    frame = id_ref[0] % FRAMES
    sent = (((frame + iota(0) // PART) % FRAMES) * PART + iota(0) % PART).astype(F32)
    enc_grad = jnp.zeros((ROWS, WIDTH), F32)
    dec_grad = jnp.zeros((ROWS, WIDTH), F32)
    for k in range(KEPT):
        rows = slice(k * ROWS, (k + 1) * ROWS)
        hidden = hidden_ref[rows, :].astype(F32)
        dz = mm_nt(dlogit_ref[rows, :], w_out_ref[...]) * (1.0 - hidden * hidden)
        enc_grad = enc_grad + dz
        here = to_bf(sent == base + float(k))
        high = dz.astype(BF16)
        low = (dz - high.astype(F32)).astype(BF16)
        dec_grad = dec_grad + mm(here, high) + mm(here, low)
    dec_grad = dec_grad.astype(BF16)
    for f, ref in enumerate((dec0_ref, dec1_ref, dec2_ref, dec3_ref)):
        ref[...] = dec_grad[f * PART : (f + 1) * PART, :]
    owned = mm_nt(enc_grad.astype(BF16), w_enc_ref[...]).astype(BF16)
    for k in range(SLOTS):
        plane_ref[chunk(k), :] = mm(from_ref[k], owned).astype(BF16)


def merge_kernel(parts_ref, plane_ref, out_hbm, float_ref, out_ref, sems):
    owners = ROWS // 2
    copies = []
    for half in range(2):
        base = half * owners
        for k in range(SLOTS):
            for c in range(PACK):
                plane = plane_ref[k * ROWS + base : k * ROWS + base + owners, chunk(c)].astype(F32)
                float_ref[pl.ds(base * BACK_ROWS + k * PACK + c, owners, stride=BACK_ROWS), :] = plane
        for h in range(HALF):
            held = member(base)
            total = parts_ref[held : held + owners, chunk(h)].astype(F32)
            for i in range(1, CORES * FRAMES):
                total = total + parts_ref[i * ROWS + held : i * ROWS + held + owners, chunk(h)].astype(F32)
            float_ref[pl.ds(base * BACK_ROWS + OUT_ROWS + h, owners, stride=BACK_ROWS), :] = total
        rows = slice(base * BACK_ROWS, (base + owners) * BACK_ROWS)
        out_ref[rows, :] = float_ref[rows, :].astype(BF16)
        copies.append(pltpu.make_async_copy(out_ref.at[rows], out_hbm.at[rows], sems.at[half]))
        copies[-1].start()
    for copy in copies:
        copy.wait()


def pred_kernel(part0_ref, part1_ref, part2_ref, part3_ref, w_ref, out_ref):
    total = part0_ref[...].astype(F32) + part1_ref[...].astype(F32)
    total = total + (part2_ref[...].astype(F32) + part3_ref[...].astype(F32))
    high = total.astype(BF16)
    low = (total - high.astype(F32)).astype(BF16)
    out_ref[...] = mm_nt(high, w_ref[...]) + mm_nt(low, w_ref[...])


def unpack_kernel(home_ref, wire_ref, enc_hbm, grad_hbm, float_ref, enc_ref, grad_ref, sems):
    float_ref[...] = wire_ref[...].astype(F32)
    slots = [take_slot(float_ref, k, BACK_ROWS).astype(BF16) for k in range(SLOTS)]
    quarters = []
    for core in range(CORES):
        for h in range(HALF):
            first = core * BACK_ROWS + OUT_ROWS + h
            from_core = float_ref[pl.ds(first, ROWS // CORES, stride=CORES * BACK_ROWS), :]
            quarters.append(jnp.sum(from_core, axis=0, keepdims=True))
    term = jnp.concatenate(quarters, axis=1)
    grad_ref[...] = term[:, 0 : grad_ref.shape[1]]
    copies = [pltpu.make_async_copy(grad_ref, grad_hbm, sems.at[2])]
    copies[0].start()
    for half in range(2):
        part = slice(half * ROWS // 2, (half + 1) * ROWS // 2)
        rows = mm(home_ref[0, part, :], slots[0])
        for k in range(1, SLOTS):
            rows = rows + mm(home_ref[k, part, :], slots[k])
        enc_ref[part, :] = rows.astype(BF16)
        copies.append(pltpu.make_async_copy(enc_ref.at[part], enc_hbm.at[part], sems.at[half]))
        copies[-1].start()
    for copy in copies:
        copy.wait()


VM = pl.BlockSpec(memory_space=pltpu.VMEM)
SM = pl.BlockSpec(memory_space=pltpu.SMEM)
HBM = pl.BlockSpec(memory_space=pltpu.HBM)


def call(kernel, name, outs, specs, scratch=(), flops=0, bytes_accessed=0, limit=24 << 20, out_specs=None):
    return pl.pallas_call(
        kernel,
        name=name,
        out_shape=outs,
        in_specs=list(specs),
        out_specs=jax.tree.map(lambda _: VM, outs) if out_specs is None else out_specs,
        scratch_shapes=list(scratch),
        compiler_params=pltpu.CompilerParams(vmem_limit_bytes=limit),
        cost_estimate=pl.CostEstimate(flops=flops, bytes_accessed=bytes_accessed, transcendentals=0),
    )


def out(shape, dtype):
    return jax.ShapeDtypeStruct(shape, dtype)


DP = ("z", "x", "core")
EVERY = DP + ("frame",)


def member(place):
    return (place + TURN) % ROWS


def exchange(array):
    return lax.all_to_all(array, DP, 0, 0, axis_index_groups=[[member(i) for i in range(ROWS)]], tiled=True)


def to_frame(array, ahead):
    return lax.ppermute(array, "frame", [(f, (f + ahead) % FRAMES) for f in range(FRAMES)])


def shards(
    enc_rows, dest, pred_rows, label_ids, block_off, band_start, w_enc, w_dec, w_out, bias_out, grad_blank, grad_label
):
    me = lax.axis_index(EVERY).astype(I32).reshape(1)
    flat_dest = dest.reshape(ROWS, ROWS)
    start = band_start.reshape(1, ROWS)
    bias = bias_out.reshape(1, -1)
    part = out((PART, WIDTH), BF16)
    pick = out((SLOTS, ROWS, ROWS), BF16)

    wire, dec = call(
        pack_kernel,
        "pack",
        (out((ROWS * OUT_ROWS, ROWS), BF16), part),
        [SM, HBM, HBM, HBM, HBM],
        [
            pltpu.VMEM((1, ROWS), I32),
            pltpu.VMEM((ROWS, WIDTH), BF16),
            pltpu.VMEM((PART, WIDTH), BF16),
            pltpu.VMEM((WIDTH, WIDTH), BF16),
            pltpu.VMEM((ROWS * OUT_ROWS, ROWS), F32),
            pltpu.VMEM((ROWS * OUT_ROWS, ROWS), BF16),
            pltpu.VMEM((PART, WIDTH), BF16),
            pltpu.SemaphoreType.DMA((7,)),
        ],
        flops=40000000,
        bytes_accessed=400000,
        limit=None,
        out_specs=(HBM, HBM),
    )(me, dest, enc_rows, pred_rows, w_dec)
    wire = exchange(wire)
    into, out_of, home, here, table, wide, wide_bias = call(
        prep_kernel,
        "prep",
        (pick, pick, pick, out((KEPT * ROWS, ROWS), BF16), out((ROWS, ROWS), F32), out((WIDTH, WIDTH), BF16), out((1, WIDTH), F32)),
        [SM, SM] + [VM] * 5,
        flops=100000000,
        bytes_accessed=2000000,
    )(me, block_off, flat_dest, start, label_ids, w_out, bias)
    enc_joint = call(
        enter_kernel,
        "enter",
        out((ROWS, WIDTH), F32),
        [VM] * 3,
        [pltpu.VMEM((ROWS * OUT_ROWS, ROWS), F32)],
        flops=100000000,
        bytes_accessed=1000000,
    )(wire, into, w_enc)
    logprobs, hidden, dlogit, term = call(
        joint_kernel,
        "joint",
        (
            out((ROWS, 2 * KEPT), F32),
            out((KEPT * ROWS, WIDTH), BF16),
            out((KEPT * ROWS, WIDTH), BF16),
            out((CORES * WIDTH, WIDTH // CORES), BF16),
        ),
        [VM] * 11,
        [
            pltpu.VMEM((KEPT, WIDTH, ROWS), F32),
            pltpu.VMEM((WIDTH, KEPT * ROWS), BF16),
            pltpu.VMEM((KEPT * ROWS, WIDTH), F32),
            pltpu.VMEM((CORES * WIDTH, WIDTH // CORES), BF16),
            pltpu.SemaphoreType.DMA((CORES,)),
        ],
        flops=500000000,
        bytes_accessed=3000000,
        out_specs=(VM, VM, VM, HBM),
    )(enc_joint, here, dec, to_frame(dec, 1), to_frame(dec, 2), to_frame(dec, 3), table, wide, wide_bias, grad_blank, grad_label)
    term = lax.all_to_all(term, ("core", "frame"), 0, 0, tiled=True)
    rows, planes, dec0, dec1, dec2, dec3 = call(
        back_kernel,
        "back",
        (out((2 * KEPT, ROWS), F32), out((SLOTS * ROWS, WIDTH), BF16), part, part, part, part),
        [SM, SM] + [VM] * 7,
        flops=500000000,
        bytes_accessed=3000000,
    )(me, block_off, start, out_of, hidden, dlogit, w_enc, wide, logprobs)
    back = call(
        merge_kernel,
        "merge",
        out((ROWS * BACK_ROWS, ROWS), BF16),
        [VM, VM],
        [
            pltpu.VMEM((ROWS * BACK_ROWS, ROWS), F32),
            pltpu.VMEM((ROWS * BACK_ROWS, ROWS), BF16),
            pltpu.SemaphoreType.DMA((2,)),
        ],
        flops=300000,
        bytes_accessed=1700000,
        out_specs=HBM,
    )(term, planes)
    back, dec1, dec2 = lax.optimization_barrier((back, dec1, dec2))
    back = exchange(back.reshape(ROWS * BACK_ROWS // 2, 2, ROWS))
    back = back.reshape(ROWS * BACK_ROWS, ROWS)
    grad_pred = call(
        pred_kernel,
        "pred",
        out((PART, WIDTH), F32),
        [VM] * 5,
        flops=40000000,
        bytes_accessed=700000,
    )(dec0, to_frame(dec1, 1), to_frame(dec2, 2), to_frame(dec3, 3), w_dec)
    grad_enc, grad_w_out = call(
        unpack_kernel,
        "unpack",
        (out((ROWS, WIDTH), BF16), out((1, w_out.shape[1]), F32)),
        [VM, VM],
        [
            pltpu.VMEM((ROWS * BACK_ROWS, ROWS), F32),
            pltpu.VMEM((ROWS, WIDTH), BF16),
            pltpu.VMEM((1, w_out.shape[1]), F32),
            pltpu.SemaphoreType.DMA((3,)),
        ],
        flops=40000000,
        bytes_accessed=600000,
        out_specs=(HBM, HBM),
    )(home, back)
    return (rows.T, grad_enc, grad_pred, grad_w_out)


def solution(mesh):
    fine = Mesh(mesh.devices.reshape(16, 4, 2, 4), EVERY)
    return jax.shard_map(
        shards,
        mesh=fine,
        in_specs=(
            P(EVERY, None),
            P(None, "frame", None),
            P(EVERY, None),
            P(DP, None),
            P(EVERY),
            P(EVERY),
            P(),
            P(),
            P(),
            P(),
            P(EVERY, None),
            P(EVERY, None),
        ),
        out_specs=(P(EVERY, None), P(EVERY, None), P(EVERY, None), P(EVERY, None)),
        check_vma=False,
    )
```

```python
import jax
import jax.numpy as jnp
from jax import lax
from jax.experimental import pallas as pl
from jax.experimental.pallas import tpu as pltpu
from jax.sharding import Mesh
from jax.sharding import PartitionSpec as P

F32 = jnp.float32
BF16 = jnp.bfloat16
I32 = jnp.int32

ROWS = 128
PACK = 4
SLOTS = 2
WIDTH = PACK * ROWS
KEPT = 3
BLOCK = 64
FRAMES = 4
PART = ROWS // FRAMES
OUT_ROWS = SLOTS * PACK
HALF = PACK // 2
BACK_ROWS = OUT_ROWS + HALF
CORES = 2
OUT_FIRST = 80
BACK_FIRST = 16
STEP = 64


def iota(dim, shape=(ROWS, ROWS)):
    return lax.broadcasted_iota(I32, shape, dim)


def mm(a, b):
    return jnp.dot(a, b, preferred_element_type=F32)


def mm_nt(a, b):
    return lax.dot_general(a, b, (((1,), (1,)), ((), ())), preferred_element_type=F32)


def mm_tn(a, b):
    return lax.dot_general(a, b, (((0,), (0,)), ((), ())), preferred_element_type=F32)


def to_bf(mask):
    return jnp.where(mask, 1.0, 0.0).astype(BF16)


def chunk(c):
    return slice(c * ROWS, (c + 1) * ROWS)


def member(place, first):
    return (place + first) % ROWS


def place_of(who, first):
    return (who + (ROWS - first)) % ROWS


def turned_to(array, first):
    return jnp.concatenate([array[first:ROWS], array[0:first]], axis=0)


def as_column(row):
    return jnp.sum(jnp.where(iota(0) == iota(1), jnp.broadcast_to(row, (ROWS, ROWS)), 0.0), axis=1, keepdims=True)


def as_row(column):
    return jnp.sum(jnp.where(iota(0) == iota(1), jnp.broadcast_to(column, (ROWS, ROWS)), 0.0), axis=0, keepdims=True)


def owner_and_rank(dest_row, first):
    dest_f = dest_row.astype(F32)
    follows = (as_column(dest_f) + 1.0) == jnp.broadcast_to(dest_f, (ROWS, ROWS))
    rank = jnp.sum(jnp.where(follows, 1.0, 0.0), axis=0, keepdims=True)
    return place_of(dest_row // ROWS, first).astype(F32), jnp.where(dest_row % ROWS == 0, 0.0, rank)


def pack_kernel(id_ref, dest_hbm, enc_hbm, pred_hbm, w_hbm, out_hbm, dec_hbm, dest_ref, enc_ref, pred_ref, w_ref, wire_ref, out_ref, dec_ref, sems):
    pairs = ((dest_hbm.at[id_ref[0] // FRAMES], dest_ref), (enc_hbm, enc_ref), (pred_hbm, pred_ref), (w_hbm, w_ref))
    copies = [pltpu.make_async_copy(src, dst, sems.at[i]) for i, (src, dst) in enumerate(pairs)]
    for copy in copies:
        copy.start()
    copies[0].wait()
    owner, rank = owner_and_rank(dest_ref[...], OUT_FIRST)
    down = iota(0).astype(F32)
    picks = [to_bf((down == owner) & (rank == float(k))) for k in range(SLOTS)]
    copies[1].wait()
    owners = ROWS // 2
    for half in range(2):
        for k in range(SLOTS):
            picked = mm(picks[k][half * owners : (half + 1) * owners], enc_ref[...])
            for c in range(PACK):
                first = half * owners * OUT_ROWS + k * PACK + c
                wire_ref[pl.ds(first, owners, stride=OUT_ROWS), :] = picked[:, chunk(c)]
        rows = slice(half * owners * OUT_ROWS, (half + 1) * owners * OUT_ROWS)
        out_ref[rows, :] = wire_ref[rows, :].astype(BF16)
        copies.append(pltpu.make_async_copy(out_ref.at[rows], out_hbm.at[rows], sems.at[len(pairs) + half]))
        copies[-1].start()
    copies[2].wait()
    copies[3].wait()
    dec_ref[...] = mm(pred_ref[...], w_ref[...]).astype(BF16)
    copies.append(pltpu.make_async_copy(dec_ref, dec_hbm, sems.at[len(pairs) + 2]))
    copies[-1].start()
    for copy in copies[len(pairs) :]:
        copy.wait()


def base_row(off_ref, start_ref):
    lane = iota(1, (1, ROWS))
    return (start_ref[...] + jnp.where(lane < BLOCK, off_ref[0], off_ref[1])).astype(F32)


def prep_kernel(
    id_ref, off_ref, dest_ref, start_ref, label_ref, w_ref, bias_ref,
    into_ref, from_ref, home_ref, here_ref, table_ref, wide_ref, bias_out_ref,
):
    mine = jnp.where(dest_ref[...] // ROWS == id_ref[0] // FRAMES, 1.0, 0.0)
    coming = turned_to(mine, OUT_FIRST).astype(BF16)
    going = turned_to(mine, BACK_FIRST).astype(BF16)
    ones = jnp.ones((ROWS, ROWS), BF16)
    count_row = mm_nt(ones, coming)
    count_col = mm(going, ones)
    earlier = member(iota(0), OUT_FIRST) < member(iota(1), OUT_FIRST)
    offset_row = mm(count_row.astype(BF16), to_bf(earlier))
    earlier = member(iota(1), BACK_FIRST) < member(iota(0), BACK_FIRST)
    offset_col = mm(to_bf(earlier), count_col.astype(BF16))
    owner, rank = owner_and_rank(dest_ref[pl.ds(id_ref[0] // FRAMES, 1), :], BACK_FIRST)
    owner = as_column(owner)
    rank = as_column(rank)
    down = iota(0).astype(F32)
    along = iota(1).astype(F32)
    for k in range(SLOTS):
        into_ref[k] = to_bf((offset_row + float(k) == down) & (count_row > float(k)))
        from_ref[k] = to_bf((offset_col + float(k) == along) & (count_col > float(k)))
        home_ref[k] = to_bf((owner == along) & (rank == float(k)))
    base = as_column(base_row(off_ref, start_ref))
    labels = label_ref[...].astype(F32)
    table = jnp.zeros((ROWS, ROWS), F32)
    frame = id_ref[0] % FRAMES
    held = (((frame + FRAMES - iota(1) // PART) % FRAMES) * PART + iota(1) % PART).astype(F32)
    for k in range(KEPT):
        here_ref[k * ROWS : (k + 1) * ROWS, :] = to_bf(held == base + float(k))
        emitted = jnp.sum(jnp.where(along == base + float(k), labels, 0.0), axis=1, keepdims=True)
        table = jnp.where(iota(1) == k, emitted, table)
    table_ref[...] = table
    vocab = w_ref.shape[1]
    wide_ref[...] = jnp.zeros_like(wide_ref)
    wide_ref[:, 0:vocab] = w_ref[...]
    bias_out_ref[...] = jnp.full_like(bias_out_ref, -1e30)
    bias_out_ref[:, 0:vocab] = bias_ref[...]


def take_slot(wire_ref, slot, rows):
    return jnp.concatenate([wire_ref[pl.ds(slot * PACK + c, ROWS, stride=rows), :] for c in range(PACK)], axis=1)


def enter_kernel(wire_ref, into_ref, w_enc_ref, out_ref, float_ref):
    float_ref[...] = wire_ref[...].astype(F32)
    owned = jnp.zeros((ROWS, WIDTH), F32)
    for k in range(SLOTS):
        owned = owned + mm(into_ref[k], take_slot(float_ref, k, OUT_ROWS).astype(BF16))
    out_ref[...] = mm(owned.astype(BF16), w_enc_ref[...])


def joint_kernel(
    enc_ref, here_ref, dec0_ref, dec1_ref, dec2_ref, dec3_ref, table_ref, w_out_ref, bias_ref,
    cot_blank_ref, cot_label_ref, logprob_ref, hidden_ref, dlogit_ref, grad_hbm, turn_ref, turned_ref, logit_ref,
    grad_ref, sems,
):
    enc_joint = enc_ref[...]
    dec = jnp.concatenate([dec0_ref[...], dec1_ref[...], dec2_ref[...], dec3_ref[...]], axis=0)
    dec_rows = mm(here_ref[...], dec)
    for k in range(KEPT):
        rows = slice(k * ROWS, (k + 1) * ROWS)
        hidden = jnp.tanh(enc_joint + dec_rows[rows, :]).astype(BF16)
        hidden_ref[rows, :] = hidden
        turn_ref[k] = hidden.astype(F32).T
        for f in range(FRAMES):
            turned_ref[chunk(f), rows] = turn_ref.at[k][pl.ds(f, ROWS, stride=FRAMES), :].astype(BF16)
    logit_ref[...] = mm(hidden_ref[...], w_out_ref[...])
    lane = iota(1, (STEP, WIDTH))
    first = iota(1, (STEP, ROWS)) == 0
    for k in range(KEPT):
        for r in range(0, ROWS, STEP):
            rows = slice(k * ROWS + r, k * ROWS + r + STEP)
            part = slice(r, r + STEP)
            logits = logit_ref[rows, :] + bias_ref[...]
            shifted = logits - jnp.max(logits, axis=1, keepdims=True)
            power = jnp.exp(shifted)
            total = jnp.sum(power, axis=1, keepdims=True)
            log_total = jnp.log(total)
            is_label = lane == table_ref[part, k : k + 1].astype(I32)
            at_label = jnp.sum(jnp.where(is_label, shifted, 0.0), axis=1, keepdims=True)
            logprob_ref[part, k : k + 1] = shifted[:, 0:1] - log_total
            logprob_ref[part, KEPT + k : KEPT + k + 1] = at_label - log_total
            cot_blank = cot_blank_ref[part, k : k + 1]
            cot_label = cot_label_ref[part, k : k + 1]
            scale = (cot_blank + cot_label) / total
            dlogit = jnp.where(is_label, cot_label, 0.0) - power * scale
            dlogit_ref[rows, chunk(0)] = (dlogit[:, chunk(0)] + jnp.where(first, cot_blank, 0.0)).astype(BF16)
            dlogit_ref[rows, ROWS:WIDTH] = dlogit[:, ROWS:WIDTH].astype(BF16)
    copies = []
    for core in range(CORES):
        half = slice(core * WIDTH, (core + 1) * WIDTH)
        columns = slice(core * HALF * ROWS, (core + 1) * HALF * ROWS)
        grad_ref[half, :] = mm(turned_ref[...], dlogit_ref[:, columns]).astype(BF16)
        copies.append(pltpu.make_async_copy(grad_ref.at[half], grad_hbm.at[half], sems.at[core]))
        copies[-1].start()
    for copy in copies:
        copy.wait()


def back_kernel(
    id_ref, off_ref, start_ref, from_ref, hidden_ref, dlogit_ref, w_enc_ref, w_out_ref, logprob_ref,
    row_ref, plane_ref, dec0_ref, dec1_ref, dec2_ref, dec3_ref,
):
    for i in range(2 * KEPT):
        row_ref[i : i + 1, :] = as_row(logprob_ref[:, i : i + 1])
    base = base_row(off_ref, start_ref)
    frame = id_ref[0] % FRAMES
    sent = (((frame + iota(0) // PART) % FRAMES) * PART + iota(0) % PART).astype(F32)
    enc_grad = jnp.zeros((ROWS, WIDTH), F32)
    dec_grad = jnp.zeros((ROWS, WIDTH), F32)
    for k in range(KEPT):
        rows = slice(k * ROWS, (k + 1) * ROWS)
        hidden = hidden_ref[rows, :].astype(F32)
        dz = mm_nt(dlogit_ref[rows, :], w_out_ref[...]) * (1.0 - hidden * hidden)
        enc_grad = enc_grad + dz
        here = to_bf(sent == base + float(k))
        high = dz.astype(BF16)
        low = (dz - high.astype(F32)).astype(BF16)
        dec_grad = dec_grad + mm(here, high) + mm(here, low)
    dec_grad = dec_grad.astype(BF16)
    for f, ref in enumerate((dec0_ref, dec1_ref, dec2_ref, dec3_ref)):
        ref[...] = dec_grad[f * PART : (f + 1) * PART, :]
    owned = mm_nt(enc_grad.astype(BF16), w_enc_ref[...]).astype(BF16)
    for k in range(SLOTS):
        plane_ref[chunk(k), :] = mm(from_ref[k], owned).astype(BF16)


def merge_kernel(parts_ref, plane_ref, out_hbm, float_ref, out_ref, sems):
    owners = ROWS // 2
    totals = []
    for h in range(HALF):
        total = parts_ref[chunk(0), chunk(h)].astype(F32)
        for i in range(1, CORES * FRAMES):
            total = total + parts_ref[chunk(i), chunk(h)].astype(F32)
        totals.append(turned_to(total, BACK_FIRST))
    copies = []
    for half in range(2):
        base = half * owners
        for k in range(SLOTS):
            for c in range(PACK):
                plane = plane_ref[k * ROWS + base : k * ROWS + base + owners, chunk(c)].astype(F32)
                float_ref[pl.ds(base * BACK_ROWS + k * PACK + c, owners, stride=BACK_ROWS), :] = plane
        for h in range(HALF):
            float_ref[pl.ds(base * BACK_ROWS + OUT_ROWS + h, owners, stride=BACK_ROWS), :] = totals[h][base : base + owners]
        rows = slice(base * BACK_ROWS, (base + owners) * BACK_ROWS)
        out_ref[rows, :] = float_ref[rows, :].astype(BF16)
        copies.append(pltpu.make_async_copy(out_ref.at[rows], out_hbm.at[rows], sems.at[half]))
        copies[-1].start()
    for copy in copies:
        copy.wait()


def pred_kernel(part0_ref, part1_ref, part2_ref, part3_ref, w_ref, out_ref):
    total = part0_ref[...].astype(F32) + part1_ref[...].astype(F32)
    total = total + (part2_ref[...].astype(F32) + part3_ref[...].astype(F32))
    high = total.astype(BF16)
    low = (total - high.astype(F32)).astype(BF16)
    out_ref[...] = mm_nt(high, w_ref[...]) + mm_nt(low, w_ref[...])


def unpack_kernel(home_ref, wire_ref, enc_hbm, grad_hbm, float_ref, enc_ref, grad_ref, sems):
    float_ref[...] = wire_ref[...].astype(F32)
    slots = [take_slot(float_ref, k, BACK_ROWS).astype(BF16) for k in range(SLOTS)]
    quarters = []
    for core in range(CORES):
        for h in range(HALF):
            first = core * BACK_ROWS + OUT_ROWS + h
            from_core = float_ref[pl.ds(first, ROWS // CORES, stride=CORES * BACK_ROWS), :]
            quarters.append(jnp.sum(from_core, axis=0, keepdims=True))
    term = jnp.concatenate(quarters, axis=1)
    grad_ref[...] = term[:, 0 : grad_ref.shape[1]]
    copies = [pltpu.make_async_copy(grad_ref, grad_hbm, sems.at[2])]
    copies[0].start()
    for half in range(2):
        part = slice(half * ROWS // 2, (half + 1) * ROWS // 2)
        rows = mm(home_ref[0, part, :], slots[0])
        for k in range(1, SLOTS):
            rows = rows + mm(home_ref[k, part, :], slots[k])
        enc_ref[part, :] = rows.astype(BF16)
        copies.append(pltpu.make_async_copy(enc_ref.at[part], enc_hbm.at[part], sems.at[half]))
        copies[-1].start()
    for copy in copies:
        copy.wait()


VM = pl.BlockSpec(memory_space=pltpu.VMEM)
SM = pl.BlockSpec(memory_space=pltpu.SMEM)
HBM = pl.BlockSpec(memory_space=pltpu.HBM)


def call(kernel, name, outs, specs, scratch=(), flops=0, bytes_accessed=0, limit=24 << 20, out_specs=None):
    return pl.pallas_call(
        kernel,
        name=name,
        out_shape=outs,
        in_specs=list(specs),
        out_specs=jax.tree.map(lambda _: VM, outs) if out_specs is None else out_specs,
        scratch_shapes=list(scratch),
        compiler_params=pltpu.CompilerParams(vmem_limit_bytes=limit),
        cost_estimate=pl.CostEstimate(flops=flops, bytes_accessed=bytes_accessed, transcendentals=0),
    )


def out(shape, dtype):
    return jax.ShapeDtypeStruct(shape, dtype)


DP = ("z", "x", "core")
EVERY = DP + ("frame",)


def exchange(array, first):
    return lax.all_to_all(array, DP, 0, 0, axis_index_groups=[[member(i, first) for i in range(ROWS)]], tiled=True)


def to_frame(array, ahead):
    return lax.ppermute(array, "frame", [(f, (f + ahead) % FRAMES) for f in range(FRAMES)])


def shards(
    enc_rows, dest, pred_rows, label_ids, block_off, band_start, w_enc, w_dec, w_out, bias_out, grad_blank, grad_label
):
    me = lax.axis_index(EVERY).astype(I32).reshape(1)
    flat_dest = dest.reshape(ROWS, ROWS)
    start = band_start.reshape(1, ROWS)
    bias = bias_out.reshape(1, -1)
    part = out((PART, WIDTH), BF16)
    pick = out((SLOTS, ROWS, ROWS), BF16)

    wire, dec = call(
        pack_kernel,
        "pack",
        (out((ROWS * OUT_ROWS, ROWS), BF16), part),
        [SM, HBM, HBM, HBM, HBM],
        [
            pltpu.VMEM((1, ROWS), I32),
            pltpu.VMEM((ROWS, WIDTH), BF16),
            pltpu.VMEM((PART, WIDTH), BF16),
            pltpu.VMEM((WIDTH, WIDTH), BF16),
            pltpu.VMEM((ROWS * OUT_ROWS, ROWS), F32),
            pltpu.VMEM((ROWS * OUT_ROWS, ROWS), BF16),
            pltpu.VMEM((PART, WIDTH), BF16),
            pltpu.SemaphoreType.DMA((7,)),
        ],
        flops=40000000,
        bytes_accessed=400000,
        limit=None,
        out_specs=(HBM, HBM),
    )(me, dest, enc_rows, pred_rows, w_dec)
    wire = exchange(wire, OUT_FIRST)
    into, out_of, home, here, table, wide, wide_bias = call(
        prep_kernel,
        "prep",
        (pick, pick, pick, out((KEPT * ROWS, ROWS), BF16), out((ROWS, ROWS), F32), out((WIDTH, WIDTH), BF16), out((1, WIDTH), F32)),
        [SM, SM] + [VM] * 5,
        flops=100000000,
        bytes_accessed=2000000,
    )(me, block_off, flat_dest, start, label_ids, w_out, bias)
    enc_joint = call(
        enter_kernel,
        "enter",
        out((ROWS, WIDTH), F32),
        [VM] * 3,
        [pltpu.VMEM((ROWS * OUT_ROWS, ROWS), F32)],
        flops=100000000,
        bytes_accessed=1000000,
    )(wire, into, w_enc)
    logprobs, hidden, dlogit, term = call(
        joint_kernel,
        "joint",
        (
            out((ROWS, 2 * KEPT), F32),
            out((KEPT * ROWS, WIDTH), BF16),
            out((KEPT * ROWS, WIDTH), BF16),
            out((CORES * WIDTH, WIDTH // CORES), BF16),
        ),
        [VM] * 11,
        [
            pltpu.VMEM((KEPT, WIDTH, ROWS), F32),
            pltpu.VMEM((WIDTH, KEPT * ROWS), BF16),
            pltpu.VMEM((KEPT * ROWS, WIDTH), F32),
            pltpu.VMEM((CORES * WIDTH, WIDTH // CORES), BF16),
            pltpu.SemaphoreType.DMA((CORES,)),
        ],
        flops=500000000,
        bytes_accessed=3000000,
        out_specs=(VM, VM, VM, HBM),
    )(enc_joint, here, dec, to_frame(dec, 1), to_frame(dec, 2), to_frame(dec, 3), table, wide, wide_bias, grad_blank, grad_label)
    term = lax.all_to_all(term, ("core", "frame"), 0, 0, tiled=True)
    rows, planes, dec0, dec1, dec2, dec3 = call(
        back_kernel,
        "back",
        (out((2 * KEPT, ROWS), F32), out((SLOTS * ROWS, WIDTH), BF16), part, part, part, part),
        [SM, SM] + [VM] * 7,
        flops=500000000,
        bytes_accessed=3000000,
    )(me, block_off, start, out_of, hidden, dlogit, w_enc, wide, logprobs)
    back = call(
        merge_kernel,
        "merge",
        out((ROWS * BACK_ROWS, ROWS), BF16),
        [VM, VM],
        [
            pltpu.VMEM((ROWS * BACK_ROWS, ROWS), F32),
            pltpu.VMEM((ROWS * BACK_ROWS, ROWS), BF16),
            pltpu.SemaphoreType.DMA((2,)),
        ],
        flops=300000,
        bytes_accessed=1700000,
        out_specs=HBM,
    )(term, planes)
    back, dec1, dec2 = lax.optimization_barrier((back, dec1, dec2))
    back = exchange(back.reshape(ROWS * BACK_ROWS // 2, 2, ROWS), BACK_FIRST)
    back = back.reshape(ROWS * BACK_ROWS, ROWS)
    grad_pred = call(
        pred_kernel,
        "pred",
        out((PART, WIDTH), F32),
        [VM] * 5,
        flops=40000000,
        bytes_accessed=700000,
    )(dec0, to_frame(dec1, 1), to_frame(dec2, 2), to_frame(dec3, 3), w_dec)
    grad_enc, grad_w_out = call(
        unpack_kernel,
        "unpack",
        (out((ROWS, WIDTH), BF16), out((1, w_out.shape[1]), F32)),
        [VM, VM],
        [
            pltpu.VMEM((ROWS * BACK_ROWS, ROWS), F32),
            pltpu.VMEM((ROWS, WIDTH), BF16),
            pltpu.VMEM((1, w_out.shape[1]), F32),
            pltpu.SemaphoreType.DMA((3,)),
        ],
        flops=40000000,
        bytes_accessed=600000,
        out_specs=(HBM, HBM),
    )(home, back)
    return (rows.T, grad_enc, grad_pred, grad_w_out)


def solution(mesh):
    fine = Mesh(mesh.devices.reshape(16, 4, 2, 4), EVERY)
    return jax.shard_map(
        shards,
        mesh=fine,
        in_specs=(
            P(EVERY, None),
            P(None, "frame", None),
            P(EVERY, None),
            P(DP, None),
            P(EVERY),
            P(EVERY),
            P(),
            P(),
            P(),
            P(),
            P(EVERY, None),
            P(EVERY, None),
        ),
        out_specs=(P(EVERY, None), P(EVERY, None), P(EVERY, None), P(EVERY, None)),
        check_vma=False,
    )
```

```python
import jax
import jax.numpy as jnp
from jax import lax
from jax.experimental import pallas as pl
from jax.experimental.pallas import tpu as pltpu
from jax.sharding import Mesh
from jax.sharding import PartitionSpec as P

F32 = jnp.float32
BF16 = jnp.bfloat16
I32 = jnp.int32

ROWS = 128
PACK = 4
SLOTS = 2
WIDTH = PACK * ROWS
KEPT = 3
BLOCK = 64
FRAMES = 4
PART = ROWS // FRAMES
OUT_ROWS = SLOTS * PACK
HALF = PACK // 2
BACK_ROWS = OUT_ROWS + HALF
CORES = 2
OUT_FIRST = 72
BACK_FIRST = 80
STEP = 64


def iota(dim, shape=(ROWS, ROWS)):
    return lax.broadcasted_iota(I32, shape, dim)


def mm(a, b):
    return jnp.dot(a, b, preferred_element_type=F32)


def mm_nt(a, b):
    return lax.dot_general(a, b, (((1,), (1,)), ((), ())), preferred_element_type=F32)


def mm_tn(a, b):
    return lax.dot_general(a, b, (((0,), (0,)), ((), ())), preferred_element_type=F32)


def to_bf(mask):
    return jnp.where(mask, 1.0, 0.0).astype(BF16)


def chunk(c):
    return slice(c * ROWS, (c + 1) * ROWS)


def member(place, first):
    return (place + first) % ROWS


def place_of(who, first):
    return (who + (ROWS - first)) % ROWS


def turned_to(array, first):
    return jnp.concatenate([array[first:ROWS], array[0:first]], axis=0)


def as_column(row):
    return jnp.sum(jnp.where(iota(0) == iota(1), jnp.broadcast_to(row, (ROWS, ROWS)), 0.0), axis=1, keepdims=True)


def as_row(column):
    return jnp.sum(jnp.where(iota(0) == iota(1), jnp.broadcast_to(column, (ROWS, ROWS)), 0.0), axis=0, keepdims=True)


def owner_and_rank(dest_row, first):
    dest_f = dest_row.astype(F32)
    follows = (as_column(dest_f) + 1.0) == jnp.broadcast_to(dest_f, (ROWS, ROWS))
    rank = jnp.sum(jnp.where(follows, 1.0, 0.0), axis=0, keepdims=True)
    return place_of(dest_row // ROWS, first).astype(F32), jnp.where(dest_row % ROWS == 0, 0.0, rank)


def pack_kernel(id_ref, dest_hbm, enc_hbm, pred_hbm, w_hbm, out_hbm, dec_hbm, dest_ref, enc_ref, pred_ref, w_ref, wire_ref, out_ref, dec_ref, sems):
    pairs = ((dest_hbm.at[id_ref[0] // FRAMES], dest_ref), (enc_hbm, enc_ref), (pred_hbm, pred_ref), (w_hbm, w_ref))
    copies = [pltpu.make_async_copy(src, dst, sems.at[i]) for i, (src, dst) in enumerate(pairs)]
    for copy in copies:
        copy.start()
    copies[0].wait()
    owner, rank = owner_and_rank(dest_ref[...], OUT_FIRST)
    down = iota(0).astype(F32)
    picks = [to_bf((down == owner) & (rank == float(k))) for k in range(SLOTS)]
    copies[1].wait()
    owners = ROWS // 2
    for half in range(2):
        for k in range(SLOTS):
            picked = mm(picks[k][half * owners : (half + 1) * owners], enc_ref[...])
            for c in range(PACK):
                first = half * owners * OUT_ROWS + k * PACK + c
                wire_ref[pl.ds(first, owners, stride=OUT_ROWS), :] = picked[:, chunk(c)]
        rows = slice(half * owners * OUT_ROWS, (half + 1) * owners * OUT_ROWS)
        out_ref[rows, :] = wire_ref[rows, :].astype(BF16)
        copies.append(pltpu.make_async_copy(out_ref.at[rows], out_hbm.at[rows], sems.at[len(pairs) + half]))
        copies[-1].start()
    copies[2].wait()
    copies[3].wait()
    dec_ref[...] = mm(pred_ref[...], w_ref[...]).astype(BF16)
    copies.append(pltpu.make_async_copy(dec_ref, dec_hbm, sems.at[len(pairs) + 2]))
    copies[-1].start()
    for copy in copies[len(pairs) :]:
        copy.wait()


def base_row(off_ref, start_ref):
    lane = iota(1, (1, ROWS))
    return (start_ref[...] + jnp.where(lane < BLOCK, off_ref[0], off_ref[1])).astype(F32)


def prep_kernel(
    id_ref, off_ref, dest_ref, start_ref, label_ref, w_ref, bias_ref,
    into_ref, from_ref, home_ref, here_ref, table_ref, wide_ref, bias_out_ref,
):
    mine = jnp.where(dest_ref[...] // ROWS == id_ref[0] // FRAMES, 1.0, 0.0)
    coming = turned_to(mine, OUT_FIRST).astype(BF16)
    going = turned_to(mine, BACK_FIRST).astype(BF16)
    ones = jnp.ones((ROWS, ROWS), BF16)
    count_row = mm_nt(ones, coming)
    count_col = mm(going, ones)
    earlier = member(iota(0), OUT_FIRST) < member(iota(1), OUT_FIRST)
    offset_row = mm(count_row.astype(BF16), to_bf(earlier))
    earlier = member(iota(1), BACK_FIRST) < member(iota(0), BACK_FIRST)
    offset_col = mm(to_bf(earlier), count_col.astype(BF16))
    owner, rank = owner_and_rank(dest_ref[pl.ds(id_ref[0] // FRAMES, 1), :], BACK_FIRST)
    owner = as_column(owner)
    rank = as_column(rank)
    down = iota(0).astype(F32)
    along = iota(1).astype(F32)
    for k in range(SLOTS):
        into_ref[k] = to_bf((offset_row + float(k) == down) & (count_row > float(k)))
        from_ref[k] = to_bf((offset_col + float(k) == along) & (count_col > float(k)))
        home_ref[k] = to_bf((owner == along) & (rank == float(k)))
    base = as_column(base_row(off_ref, start_ref))
    labels = label_ref[...].astype(F32)
    table = jnp.zeros((ROWS, ROWS), F32)
    frame = id_ref[0] % FRAMES
    held = (((frame + FRAMES - iota(1) // PART) % FRAMES) * PART + iota(1) % PART).astype(F32)
    for k in range(KEPT):
        here_ref[k * ROWS : (k + 1) * ROWS, :] = to_bf(held == base + float(k))
        emitted = jnp.sum(jnp.where(along == base + float(k), labels, 0.0), axis=1, keepdims=True)
        table = jnp.where(iota(1) == k, emitted, table)
    table_ref[...] = table
    vocab = w_ref.shape[1]
    wide_ref[...] = jnp.zeros_like(wide_ref)
    wide_ref[:, 0:vocab] = w_ref[...]
    bias_out_ref[...] = jnp.full_like(bias_out_ref, -1e30)
    bias_out_ref[:, 0:vocab] = bias_ref[...]


def take_slot(wire_ref, slot, rows):
    return jnp.concatenate([wire_ref[pl.ds(slot * PACK + c, ROWS, stride=rows), :] for c in range(PACK)], axis=1)


def enter_kernel(wire_ref, into_ref, w_enc_ref, out_ref, float_ref):
    float_ref[...] = wire_ref[...].astype(F32)
    owned = jnp.zeros((ROWS, WIDTH), F32)
    for k in range(SLOTS):
        owned = owned + mm(into_ref[k], take_slot(float_ref, k, OUT_ROWS).astype(BF16))
    out_ref[...] = mm(owned.astype(BF16), w_enc_ref[...])


def joint_kernel(
    enc_ref, here_ref, dec0_ref, dec1_ref, dec2_ref, dec3_ref, table_ref, w_out_ref, bias_ref,
    cot_blank_ref, cot_label_ref, logprob_ref, hidden_ref, dlogit_ref, grad_hbm, turn_ref, turned_ref, logit_ref,
    grad_ref, sems,
):
    enc_joint = enc_ref[...]
    dec = jnp.concatenate([dec0_ref[...], dec1_ref[...], dec2_ref[...], dec3_ref[...]], axis=0)
    dec_rows = mm(here_ref[...], dec)
    for k in range(KEPT):
        rows = slice(k * ROWS, (k + 1) * ROWS)
        hidden = jnp.tanh(enc_joint + dec_rows[rows, :]).astype(BF16)
        hidden_ref[rows, :] = hidden
        turn_ref[k] = hidden.astype(F32).T
        for f in range(FRAMES):
            turned_ref[chunk(f), rows] = turn_ref.at[k][pl.ds(f, ROWS, stride=FRAMES), :].astype(BF16)
    logit_ref[...] = mm(hidden_ref[...], w_out_ref[...])
    lane = iota(1, (STEP, WIDTH))
    first = iota(1, (STEP, ROWS)) == 0
    for k in range(KEPT):
        for r in range(0, ROWS, STEP):
            rows = slice(k * ROWS + r, k * ROWS + r + STEP)
            part = slice(r, r + STEP)
            logits = logit_ref[rows, :] + bias_ref[...]
            shifted = logits - jnp.max(logits, axis=1, keepdims=True)
            power = jnp.exp(shifted)
            total = jnp.sum(power, axis=1, keepdims=True)
            log_total = jnp.log(total)
            is_label = lane == table_ref[part, k : k + 1].astype(I32)
            at_label = jnp.sum(jnp.where(is_label, shifted, 0.0), axis=1, keepdims=True)
            logprob_ref[part, k : k + 1] = shifted[:, 0:1] - log_total
            logprob_ref[part, KEPT + k : KEPT + k + 1] = at_label - log_total
            cot_blank = cot_blank_ref[part, k : k + 1]
            cot_label = cot_label_ref[part, k : k + 1]
            scale = (cot_blank + cot_label) / total
            dlogit = jnp.where(is_label, cot_label, 0.0) - power * scale
            dlogit_ref[rows, chunk(0)] = (dlogit[:, chunk(0)] + jnp.where(first, cot_blank, 0.0)).astype(BF16)
            dlogit_ref[rows, ROWS:WIDTH] = dlogit[:, ROWS:WIDTH].astype(BF16)
    copies = []
    for core in range(CORES):
        half = slice(core * WIDTH, (core + 1) * WIDTH)
        columns = slice(core * HALF * ROWS, (core + 1) * HALF * ROWS)
        grad_ref[half, :] = mm(turned_ref[...], dlogit_ref[:, columns]).astype(BF16)
        copies.append(pltpu.make_async_copy(grad_ref.at[half], grad_hbm.at[half], sems.at[core]))
        copies[-1].start()
    for copy in copies:
        copy.wait()


def back_kernel(
    id_ref, off_ref, start_ref, from_ref, hidden_ref, dlogit_ref, w_enc_ref, w_out_ref, logprob_ref,
    row_ref, plane_ref, dec0_ref, dec1_ref, dec2_ref, dec3_ref,
):
    for i in range(2 * KEPT):
        row_ref[i : i + 1, :] = as_row(logprob_ref[:, i : i + 1])
    base = base_row(off_ref, start_ref)
    frame = id_ref[0] % FRAMES
    sent = (((frame + iota(0) // PART) % FRAMES) * PART + iota(0) % PART).astype(F32)
    enc_grad = jnp.zeros((ROWS, WIDTH), F32)
    dec_grad = jnp.zeros((ROWS, WIDTH), F32)
    for k in range(KEPT):
        rows = slice(k * ROWS, (k + 1) * ROWS)
        hidden = hidden_ref[rows, :].astype(F32)
        dz = mm_nt(dlogit_ref[rows, :], w_out_ref[...]) * (1.0 - hidden * hidden)
        enc_grad = enc_grad + dz
        here = to_bf(sent == base + float(k))
        high = dz.astype(BF16)
        low = (dz - high.astype(F32)).astype(BF16)
        dec_grad = dec_grad + mm(here, high) + mm(here, low)
    dec_grad = dec_grad.astype(BF16)
    for f, ref in enumerate((dec0_ref, dec1_ref, dec2_ref, dec3_ref)):
        ref[...] = dec_grad[f * PART : (f + 1) * PART, :]
    owned = mm_nt(enc_grad.astype(BF16), w_enc_ref[...]).astype(BF16)
    for k in range(SLOTS):
        plane_ref[chunk(k), :] = mm(from_ref[k], owned).astype(BF16)


def merge_kernel(parts_ref, plane_ref, out_hbm, float_ref, out_ref, sems):
    owners = ROWS // 2
    totals = []
    for h in range(HALF):
        total = parts_ref[chunk(0), chunk(h)].astype(F32)
        for i in range(1, CORES * FRAMES):
            total = total + parts_ref[chunk(i), chunk(h)].astype(F32)
        totals.append(turned_to(total, BACK_FIRST))
    copies = []
    for half in range(2):
        base = half * owners
        for k in range(SLOTS):
            for c in range(PACK):
                plane = plane_ref[k * ROWS + base : k * ROWS + base + owners, chunk(c)].astype(F32)
                float_ref[pl.ds(base * BACK_ROWS + k * PACK + c, owners, stride=BACK_ROWS), :] = plane
        for h in range(HALF):
            float_ref[pl.ds(base * BACK_ROWS + OUT_ROWS + h, owners, stride=BACK_ROWS), :] = totals[h][base : base + owners]
        rows = slice(base * BACK_ROWS, (base + owners) * BACK_ROWS)
        out_ref[rows, :] = float_ref[rows, :].astype(BF16)
        copies.append(pltpu.make_async_copy(out_ref.at[rows], out_hbm.at[rows], sems.at[half]))
        copies[-1].start()
    for copy in copies:
        copy.wait()


def pred_kernel(part0_ref, part1_ref, part2_ref, part3_ref, w_ref, out_ref):
    total = part0_ref[...].astype(F32) + part1_ref[...].astype(F32)
    total = total + (part2_ref[...].astype(F32) + part3_ref[...].astype(F32))
    high = total.astype(BF16)
    low = (total - high.astype(F32)).astype(BF16)
    out_ref[...] = mm_nt(high, w_ref[...]) + mm_nt(low, w_ref[...])


def unpack_kernel(home_ref, wire_ref, enc_hbm, grad_hbm, float_ref, enc_ref, grad_ref, sems):
    float_ref[...] = wire_ref[...].astype(F32)
    slots = [take_slot(float_ref, k, BACK_ROWS).astype(BF16) for k in range(SLOTS)]
    quarters = []
    for core in range(CORES):
        for h in range(HALF):
            first = core * BACK_ROWS + OUT_ROWS + h
            from_core = float_ref[pl.ds(first, ROWS // CORES, stride=CORES * BACK_ROWS), :]
            quarters.append(jnp.sum(from_core, axis=0, keepdims=True))
    term = jnp.concatenate(quarters, axis=1)
    grad_ref[...] = term[:, 0 : grad_ref.shape[1]]
    copies = [pltpu.make_async_copy(grad_ref, grad_hbm, sems.at[2])]
    copies[0].start()
    for half in range(2):
        part = slice(half * ROWS // 2, (half + 1) * ROWS // 2)
        rows = mm(home_ref[0, part, :], slots[0])
        for k in range(1, SLOTS):
            rows = rows + mm(home_ref[k, part, :], slots[k])
        enc_ref[part, :] = rows.astype(BF16)
        copies.append(pltpu.make_async_copy(enc_ref.at[part], enc_hbm.at[part], sems.at[half]))
        copies[-1].start()
    for copy in copies:
        copy.wait()


VM = pl.BlockSpec(memory_space=pltpu.VMEM)
SM = pl.BlockSpec(memory_space=pltpu.SMEM)
HBM = pl.BlockSpec(memory_space=pltpu.HBM)


def call(kernel, name, outs, specs, scratch=(), flops=0, bytes_accessed=0, limit=24 << 20, out_specs=None):
    return pl.pallas_call(
        kernel,
        name=name,
        out_shape=outs,
        in_specs=list(specs),
        out_specs=jax.tree.map(lambda _: VM, outs) if out_specs is None else out_specs,
        scratch_shapes=list(scratch),
        compiler_params=pltpu.CompilerParams(vmem_limit_bytes=limit),
        cost_estimate=pl.CostEstimate(flops=flops, bytes_accessed=bytes_accessed, transcendentals=0),
    )


def out(shape, dtype):
    return jax.ShapeDtypeStruct(shape, dtype)


DP = ("z", "x", "core")
EVERY = DP + ("frame",)


def exchange(array, first):
    return lax.all_to_all(array, DP, 0, 0, axis_index_groups=[[member(i, first) for i in range(ROWS)]], tiled=True)


def to_frame(array, ahead):
    return lax.ppermute(array, "frame", [(f, (f + ahead) % FRAMES) for f in range(FRAMES)])


def shards(
    enc_rows, dest, pred_rows, label_ids, block_off, band_start, w_enc, w_dec, w_out, bias_out, grad_blank, grad_label
):
    me = lax.axis_index(EVERY).astype(I32).reshape(1)
    flat_dest = dest.reshape(ROWS, ROWS)
    start = band_start.reshape(1, ROWS)
    bias = bias_out.reshape(1, -1)
    part = out((PART, WIDTH), BF16)
    pick = out((SLOTS, ROWS, ROWS), BF16)

    wire, dec = call(
        pack_kernel,
        "pack",
        (out((ROWS * OUT_ROWS, ROWS), BF16), part),
        [SM, HBM, HBM, HBM, HBM],
        [
            pltpu.VMEM((1, ROWS), I32),
            pltpu.VMEM((ROWS, WIDTH), BF16),
            pltpu.VMEM((PART, WIDTH), BF16),
            pltpu.VMEM((WIDTH, WIDTH), BF16),
            pltpu.VMEM((ROWS * OUT_ROWS, ROWS), F32),
            pltpu.VMEM((ROWS * OUT_ROWS, ROWS), BF16),
            pltpu.VMEM((PART, WIDTH), BF16),
            pltpu.SemaphoreType.DMA((7,)),
        ],
        flops=40000000,
        bytes_accessed=400000,
        limit=None,
        out_specs=(HBM, HBM),
    )(me, dest, enc_rows, pred_rows, w_dec)
    wire = exchange(wire, OUT_FIRST)
    into, out_of, home, here, table, wide, wide_bias = call(
        prep_kernel,
        "prep",
        (pick, pick, pick, out((KEPT * ROWS, ROWS), BF16), out((ROWS, ROWS), F32), out((WIDTH, WIDTH), BF16), out((1, WIDTH), F32)),
        [SM, SM] + [VM] * 5,
        flops=100000000,
        bytes_accessed=2000000,
    )(me, block_off, flat_dest, start, label_ids, w_out, bias)
    enc_joint = call(
        enter_kernel,
        "enter",
        out((ROWS, WIDTH), F32),
        [VM] * 3,
        [pltpu.VMEM((ROWS * OUT_ROWS, ROWS), F32)],
        flops=100000000,
        bytes_accessed=1000000,
    )(wire, into, w_enc)
    logprobs, hidden, dlogit, term = call(
        joint_kernel,
        "joint",
        (
            out((ROWS, 2 * KEPT), F32),
            out((KEPT * ROWS, WIDTH), BF16),
            out((KEPT * ROWS, WIDTH), BF16),
            out((CORES * WIDTH, WIDTH // CORES), BF16),
        ),
        [VM] * 11,
        [
            pltpu.VMEM((KEPT, WIDTH, ROWS), F32),
            pltpu.VMEM((WIDTH, KEPT * ROWS), BF16),
            pltpu.VMEM((KEPT * ROWS, WIDTH), F32),
            pltpu.VMEM((CORES * WIDTH, WIDTH // CORES), BF16),
            pltpu.SemaphoreType.DMA((CORES,)),
        ],
        flops=500000000,
        bytes_accessed=3000000,
        out_specs=(VM, VM, VM, HBM),
    )(enc_joint, here, dec, to_frame(dec, 1), to_frame(dec, 2), to_frame(dec, 3), table, wide, wide_bias, grad_blank, grad_label)
    term = lax.all_to_all(term, ("core", "frame"), 0, 0, tiled=True)
    rows, planes, dec0, dec1, dec2, dec3 = call(
        back_kernel,
        "back",
        (out((2 * KEPT, ROWS), F32), out((SLOTS * ROWS, WIDTH), BF16), part, part, part, part),
        [SM, SM] + [VM] * 7,
        flops=500000000,
        bytes_accessed=3000000,
    )(me, block_off, start, out_of, hidden, dlogit, w_enc, wide, logprobs)
    back = call(
        merge_kernel,
        "merge",
        out((ROWS * BACK_ROWS, ROWS), BF16),
        [VM, VM],
        [
            pltpu.VMEM((ROWS * BACK_ROWS, ROWS), F32),
            pltpu.VMEM((ROWS * BACK_ROWS, ROWS), BF16),
            pltpu.SemaphoreType.DMA((2,)),
        ],
        flops=300000,
        bytes_accessed=1700000,
        out_specs=HBM,
    )(term, planes)
    back, dec1, dec2 = lax.optimization_barrier((back, dec1, dec2))
    back = exchange(back.reshape(ROWS * BACK_ROWS // 2, 2, ROWS), BACK_FIRST)
    back = back.reshape(ROWS * BACK_ROWS, ROWS)
    grad_pred = call(
        pred_kernel,
        "pred",
        out((PART, WIDTH), F32),
        [VM] * 5,
        flops=40000000,
        bytes_accessed=700000,
    )(dec0, to_frame(dec1, 1), to_frame(dec2, 2), to_frame(dec3, 3), w_dec)
    grad_enc, grad_w_out = call(
        unpack_kernel,
        "unpack",
        (out((ROWS, WIDTH), BF16), out((1, w_out.shape[1]), F32)),
        [VM, VM],
        [
            pltpu.VMEM((ROWS * BACK_ROWS, ROWS), F32),
            pltpu.VMEM((ROWS, WIDTH), BF16),
            pltpu.VMEM((1, w_out.shape[1]), F32),
            pltpu.SemaphoreType.DMA((3,)),
        ],
        flops=40000000,
        bytes_accessed=600000,
        out_specs=(HBM, HBM),
    )(home, back)
    return (rows.T, grad_enc, grad_pred, grad_w_out)


def solution(mesh):
    fine = Mesh(mesh.devices.reshape(16, 4, 2, 4), EVERY)
    return jax.shard_map(
        shards,
        mesh=fine,
        in_specs=(
            P(EVERY, None),
            P(None, "frame", None),
            P(EVERY, None),
            P(DP, None),
            P(EVERY),
            P(EVERY),
            P(),
            P(),
            P(),
            P(),
            P(EVERY, None),
            P(EVERY, None),
        ),
        out_specs=(P(EVERY, None), P(EVERY, None), P(EVERY, None), P(EVERY, None)),
        check_vma=False,
    )
```

```python
import jax
import jax.numpy as jnp
from jax import lax
from jax.experimental import pallas as pl
from jax.experimental.pallas import tpu as pltpu
from jax.sharding import Mesh
from jax.sharding import PartitionSpec as P

F32 = jnp.float32
BF16 = jnp.bfloat16
I32 = jnp.int32

ROWS = 128
PACK = 4
SLOTS = 2
WIDTH = PACK * ROWS
KEPT = 3
BLOCK = 64
FRAMES = 4
PART = ROWS // FRAMES
OUT_ROWS = SLOTS * PACK
HALF = PACK // 2
BACK_ROWS = OUT_ROWS + HALF
CORES = 2
OUT_FIRST = 68
BACK_FIRST = 68
STEP = 64


def iota(dim, shape=(ROWS, ROWS)):
    return lax.broadcasted_iota(I32, shape, dim)


def mm(a, b):
    return jnp.dot(a, b, preferred_element_type=F32)


def mm_nt(a, b):
    return lax.dot_general(a, b, (((1,), (1,)), ((), ())), preferred_element_type=F32)


def mm_tn(a, b):
    return lax.dot_general(a, b, (((0,), (0,)), ((), ())), preferred_element_type=F32)


def to_bf(mask):
    return jnp.where(mask, 1.0, 0.0).astype(BF16)


def chunk(c):
    return slice(c * ROWS, (c + 1) * ROWS)


def member(place, first):
    return (place + first) % ROWS


def place_of(who, first):
    return (who + (ROWS - first)) % ROWS


def turned_to(array, first):
    return pltpu.roll(array, ROWS - first, 0)


def as_column(row):
    return jnp.sum(jnp.where(iota(0) == iota(1), jnp.broadcast_to(row, (ROWS, ROWS)), 0.0), axis=1, keepdims=True)


def as_row(column):
    return jnp.sum(jnp.where(iota(0) == iota(1), jnp.broadcast_to(column, (ROWS, ROWS)), 0.0), axis=0, keepdims=True)


def owner_and_rank(dest_row, first):
    dest_f = dest_row.astype(F32)
    follows = (as_column(dest_f) + 1.0) == jnp.broadcast_to(dest_f, (ROWS, ROWS))
    rank = jnp.sum(jnp.where(follows, 1.0, 0.0), axis=0, keepdims=True)
    return place_of(dest_row // ROWS, first).astype(F32), jnp.where(dest_row % ROWS == 0, 0.0, rank)


def pack_kernel(id_ref, dest_hbm, enc_hbm, pred_hbm, w_hbm, out_hbm, dec_hbm, dest_ref, enc_ref, pred_ref, w_ref, wire_ref, out_ref, dec_ref, sems):
    pairs = ((dest_hbm.at[id_ref[0] // FRAMES], dest_ref), (enc_hbm, enc_ref), (pred_hbm, pred_ref), (w_hbm, w_ref))
    copies = [pltpu.make_async_copy(src, dst, sems.at[i]) for i, (src, dst) in enumerate(pairs)]
    for copy in copies:
        copy.start()
    copies[0].wait()
    owner, rank = owner_and_rank(dest_ref[...], OUT_FIRST)
    down = iota(0).astype(F32)
    picks = [to_bf((down == owner) & (rank == float(k))) for k in range(SLOTS)]
    copies[1].wait()
    owners = ROWS // 2
    for half in range(2):
        for k in range(SLOTS):
            picked = mm(picks[k][half * owners : (half + 1) * owners], enc_ref[...])
            for c in range(PACK):
                first = half * owners * OUT_ROWS + k * PACK + c
                wire_ref[pl.ds(first, owners, stride=OUT_ROWS), :] = picked[:, chunk(c)]
        rows = slice(half * owners * OUT_ROWS, (half + 1) * owners * OUT_ROWS)
        out_ref[rows, :] = wire_ref[rows, :].astype(BF16)
        copies.append(pltpu.make_async_copy(out_ref.at[rows], out_hbm.at[rows], sems.at[len(pairs) + half]))
        copies[-1].start()
    copies[2].wait()
    copies[3].wait()
    dec_ref[...] = mm(pred_ref[...], w_ref[...]).astype(BF16)
    copies.append(pltpu.make_async_copy(dec_ref, dec_hbm, sems.at[len(pairs) + 2]))
    copies[-1].start()
    for copy in copies[len(pairs) :]:
        copy.wait()


def base_row(off_ref, start_ref):
    lane = iota(1, (1, ROWS))
    return (start_ref[...] + jnp.where(lane < BLOCK, off_ref[0], off_ref[1])).astype(F32)


def prep_kernel(
    id_ref, off_ref, dest_ref, start_ref, label_ref, w_ref, bias_ref,
    into_ref, from_ref, home_ref, here_ref, table_ref, wide_ref, bias_out_ref,
):
    mine = jnp.where(dest_ref[...] // ROWS == id_ref[0] // FRAMES, 1.0, 0.0)
    coming = turned_to(mine, OUT_FIRST).astype(BF16)
    going = turned_to(mine, BACK_FIRST).astype(BF16)
    ones = jnp.ones((ROWS, ROWS), BF16)
    count_row = mm_nt(ones, coming)
    count_col = mm(going, ones)
    earlier = member(iota(0), OUT_FIRST) < member(iota(1), OUT_FIRST)
    offset_row = mm(count_row.astype(BF16), to_bf(earlier))
    earlier = member(iota(1), BACK_FIRST) < member(iota(0), BACK_FIRST)
    offset_col = mm(to_bf(earlier), count_col.astype(BF16))
    owner, rank = owner_and_rank(dest_ref[pl.ds(id_ref[0] // FRAMES, 1), :], BACK_FIRST)
    owner = as_column(owner)
    rank = as_column(rank)
    down = iota(0).astype(F32)
    along = iota(1).astype(F32)
    for k in range(SLOTS):
        into_ref[k] = to_bf((offset_row + float(k) == down) & (count_row > float(k)))
        from_ref[k] = to_bf((offset_col + float(k) == along) & (count_col > float(k)))
        home_ref[k] = to_bf((owner == along) & (rank == float(k)))
    base = as_column(base_row(off_ref, start_ref))
    labels = label_ref[...].astype(F32)
    table = jnp.zeros((ROWS, ROWS), F32)
    frame = id_ref[0] % FRAMES
    held = (((frame + FRAMES - iota(1) // PART) % FRAMES) * PART + iota(1) % PART).astype(F32)
    for k in range(KEPT):
        here_ref[k * ROWS : (k + 1) * ROWS, :] = to_bf(held == base + float(k))
        emitted = jnp.sum(jnp.where(along == base + float(k), labels, 0.0), axis=1, keepdims=True)
        table = jnp.where(iota(1) == k, emitted, table)
    table_ref[...] = table
    vocab = w_ref.shape[1]
    wide_ref[...] = jnp.zeros_like(wide_ref)
    wide_ref[:, 0:vocab] = w_ref[...]
    bias_out_ref[...] = jnp.full_like(bias_out_ref, -1e30)
    bias_out_ref[:, 0:vocab] = bias_ref[...]


def take_slot(wire_ref, slot, rows):
    return jnp.concatenate([wire_ref[pl.ds(slot * PACK + c, ROWS, stride=rows), :] for c in range(PACK)], axis=1)


def enter_kernel(wire_ref, into_ref, w_enc_ref, out_ref, float_ref):
    float_ref[...] = wire_ref[...].astype(F32)
    owned = jnp.zeros((ROWS, WIDTH), F32)
    for k in range(SLOTS):
        owned = owned + mm(into_ref[k], take_slot(float_ref, k, OUT_ROWS).astype(BF16))
    out_ref[...] = mm(owned.astype(BF16), w_enc_ref[...])


def joint_kernel(
    enc_ref, here_ref, dec0_ref, dec1_ref, dec2_ref, dec3_ref, table_ref, w_out_ref, bias_ref,
    cot_blank_ref, cot_label_ref, logprob_ref, hidden_ref, dlogit_ref, grad_hbm, turn_ref, turned_ref, logit_ref,
    grad_ref, sems,
):
    enc_joint = enc_ref[...]
    dec = jnp.concatenate([dec0_ref[...], dec1_ref[...], dec2_ref[...], dec3_ref[...]], axis=0)
    dec_rows = mm(here_ref[...], dec)
    for k in range(KEPT):
        rows = slice(k * ROWS, (k + 1) * ROWS)
        hidden = jnp.tanh(enc_joint + dec_rows[rows, :]).astype(BF16)
        hidden_ref[rows, :] = hidden
        turn_ref[k] = hidden.astype(F32).T
        for f in range(FRAMES):
            turned_ref[chunk(f), rows] = turn_ref.at[k][pl.ds(f, ROWS, stride=FRAMES), :].astype(BF16)
    logit_ref[...] = mm(hidden_ref[...], w_out_ref[...])
    lane = iota(1, (STEP, WIDTH))
    first = iota(1, (STEP, ROWS)) == 0
    for k in range(KEPT):
        for r in range(0, ROWS, STEP):
            rows = slice(k * ROWS + r, k * ROWS + r + STEP)
            part = slice(r, r + STEP)
            logits = logit_ref[rows, :] + bias_ref[...]
            shifted = logits - jnp.max(logits, axis=1, keepdims=True)
            power = jnp.exp(shifted)
            total = jnp.sum(power, axis=1, keepdims=True)
            log_total = jnp.log(total)
            is_label = lane == table_ref[part, k : k + 1].astype(I32)
            at_label = jnp.sum(jnp.where(is_label, shifted, 0.0), axis=1, keepdims=True)
            logprob_ref[part, k : k + 1] = shifted[:, 0:1] - log_total
            logprob_ref[part, KEPT + k : KEPT + k + 1] = at_label - log_total
            cot_blank = cot_blank_ref[part, k : k + 1]
            cot_label = cot_label_ref[part, k : k + 1]
            scale = (cot_blank + cot_label) / total
            dlogit = jnp.where(is_label, cot_label, 0.0) - power * scale
            dlogit_ref[rows, chunk(0)] = (dlogit[:, chunk(0)] + jnp.where(first, cot_blank, 0.0)).astype(BF16)
            dlogit_ref[rows, ROWS:WIDTH] = dlogit[:, ROWS:WIDTH].astype(BF16)
    copies = []
    for core in range(CORES):
        half = slice(core * WIDTH, (core + 1) * WIDTH)
        columns = slice(core * HALF * ROWS, (core + 1) * HALF * ROWS)
        grad_ref[half, :] = mm(turned_ref[...], dlogit_ref[:, columns]).astype(BF16)
        copies.append(pltpu.make_async_copy(grad_ref.at[half], grad_hbm.at[half], sems.at[core]))
        copies[-1].start()
    for copy in copies:
        copy.wait()


def back_kernel(
    id_ref, off_ref, start_ref, from_ref, hidden_ref, dlogit_ref, w_enc_ref, w_out_ref, logprob_ref,
    row_ref, plane_ref, dec0_ref, dec1_ref, dec2_ref, dec3_ref,
):
    for i in range(2 * KEPT):
        row_ref[i : i + 1, :] = as_row(logprob_ref[:, i : i + 1])
    base = base_row(off_ref, start_ref)
    frame = id_ref[0] % FRAMES
    sent = (((frame + iota(0) // PART) % FRAMES) * PART + iota(0) % PART).astype(F32)
    enc_grad = jnp.zeros((ROWS, WIDTH), F32)
    dec_grad = jnp.zeros((ROWS, WIDTH), F32)
    for k in range(KEPT):
        rows = slice(k * ROWS, (k + 1) * ROWS)
        hidden = hidden_ref[rows, :].astype(F32)
        dz = mm_nt(dlogit_ref[rows, :], w_out_ref[...]) * (1.0 - hidden * hidden)
        enc_grad = enc_grad + dz
        here = to_bf(sent == base + float(k))
        high = dz.astype(BF16)
        low = (dz - high.astype(F32)).astype(BF16)
        dec_grad = dec_grad + mm(here, high) + mm(here, low)
    dec_grad = dec_grad.astype(BF16)
    for f, ref in enumerate((dec0_ref, dec1_ref, dec2_ref, dec3_ref)):
        ref[...] = dec_grad[f * PART : (f + 1) * PART, :]
    owned = mm_nt(enc_grad.astype(BF16), w_enc_ref[...]).astype(BF16)
    for k in range(SLOTS):
        plane_ref[chunk(k), :] = mm(from_ref[k], owned).astype(BF16)


def merge_kernel(parts_ref, plane_ref, out_hbm, float_ref, out_ref, sems):
    owners = ROWS // 2
    totals = []
    for h in range(HALF):
        total = parts_ref[chunk(0), chunk(h)].astype(F32)
        for i in range(1, CORES * FRAMES):
            total = total + parts_ref[chunk(i), chunk(h)].astype(F32)
        totals.append(turned_to(total, BACK_FIRST))
    copies = []
    for half in range(2):
        base = half * owners
        for k in range(SLOTS):
            for c in range(PACK):
                plane = plane_ref[k * ROWS + base : k * ROWS + base + owners, chunk(c)].astype(F32)
                float_ref[pl.ds(base * BACK_ROWS + k * PACK + c, owners, stride=BACK_ROWS), :] = plane
        for h in range(HALF):
            float_ref[pl.ds(base * BACK_ROWS + OUT_ROWS + h, owners, stride=BACK_ROWS), :] = totals[h][base : base + owners]
        rows = slice(base * BACK_ROWS, (base + owners) * BACK_ROWS)
        out_ref[rows, :] = float_ref[rows, :].astype(BF16)
        copies.append(pltpu.make_async_copy(out_ref.at[rows], out_hbm.at[rows], sems.at[half]))
        copies[-1].start()
    for copy in copies:
        copy.wait()


def pred_kernel(part0_ref, part1_ref, part2_ref, part3_ref, w_ref, out_ref):
    total = part0_ref[...].astype(F32) + part1_ref[...].astype(F32)
    total = total + (part2_ref[...].astype(F32) + part3_ref[...].astype(F32))
    high = total.astype(BF16)
    low = (total - high.astype(F32)).astype(BF16)
    out_ref[...] = mm_nt(high, w_ref[...]) + mm_nt(low, w_ref[...])


def unpack_kernel(home_ref, wire_ref, enc_hbm, grad_hbm, float_ref, enc_ref, grad_ref, sems):
    float_ref[...] = wire_ref[...].astype(F32)
    slots = [take_slot(float_ref, k, BACK_ROWS).astype(BF16) for k in range(SLOTS)]
    quarters = []
    for core in range(CORES):
        for h in range(HALF):
            first = core * BACK_ROWS + OUT_ROWS + h
            from_core = float_ref[pl.ds(first, ROWS // CORES, stride=CORES * BACK_ROWS), :]
            quarters.append(jnp.sum(from_core, axis=0, keepdims=True))
    term = jnp.concatenate(quarters, axis=1)
    grad_ref[...] = term[:, 0 : grad_ref.shape[1]]
    copies = [pltpu.make_async_copy(grad_ref, grad_hbm, sems.at[2])]
    copies[0].start()
    for half in range(2):
        part = slice(half * ROWS // 2, (half + 1) * ROWS // 2)
        rows = mm(home_ref[0, part, :], slots[0])
        for k in range(1, SLOTS):
            rows = rows + mm(home_ref[k, part, :], slots[k])
        enc_ref[part, :] = rows.astype(BF16)
        copies.append(pltpu.make_async_copy(enc_ref.at[part], enc_hbm.at[part], sems.at[half]))
        copies[-1].start()
    for copy in copies:
        copy.wait()


VM = pl.BlockSpec(memory_space=pltpu.VMEM)
SM = pl.BlockSpec(memory_space=pltpu.SMEM)
HBM = pl.BlockSpec(memory_space=pltpu.HBM)


def call(kernel, name, outs, specs, scratch=(), flops=0, bytes_accessed=0, limit=24 << 20, out_specs=None):
    return pl.pallas_call(
        kernel,
        name=name,
        out_shape=outs,
        in_specs=list(specs),
        out_specs=jax.tree.map(lambda _: VM, outs) if out_specs is None else out_specs,
        scratch_shapes=list(scratch),
        compiler_params=pltpu.CompilerParams(vmem_limit_bytes=limit),
        cost_estimate=pl.CostEstimate(flops=flops, bytes_accessed=bytes_accessed, transcendentals=0),
    )


def out(shape, dtype):
    return jax.ShapeDtypeStruct(shape, dtype)


DP = ("z", "x", "core")
EVERY = DP + ("frame",)


def exchange(array, first):
    return lax.all_to_all(array, DP, 0, 0, axis_index_groups=[[member(i, first) for i in range(ROWS)]], tiled=True)


def to_frame(array, ahead):
    return lax.ppermute(array, "frame", [(f, (f + ahead) % FRAMES) for f in range(FRAMES)])


def shards(
    enc_rows, dest, pred_rows, label_ids, block_off, band_start, w_enc, w_dec, w_out, bias_out, grad_blank, grad_label
):
    me = lax.axis_index(EVERY).astype(I32).reshape(1)
    flat_dest = dest.reshape(ROWS, ROWS)
    start = band_start.reshape(1, ROWS)
    bias = bias_out.reshape(1, -1)
    part = out((PART, WIDTH), BF16)
    pick = out((SLOTS, ROWS, ROWS), BF16)

    wire, dec = call(
        pack_kernel,
        "pack",
        (out((ROWS * OUT_ROWS, ROWS), BF16), part),
        [SM, HBM, HBM, HBM, HBM],
        [
            pltpu.VMEM((1, ROWS), I32),
            pltpu.VMEM((ROWS, WIDTH), BF16),
            pltpu.VMEM((PART, WIDTH), BF16),
            pltpu.VMEM((WIDTH, WIDTH), BF16),
            pltpu.VMEM((ROWS * OUT_ROWS, ROWS), F32),
            pltpu.VMEM((ROWS * OUT_ROWS, ROWS), BF16),
            pltpu.VMEM((PART, WIDTH), BF16),
            pltpu.SemaphoreType.DMA((7,)),
        ],
        flops=40000000,
        bytes_accessed=400000,
        limit=None,
        out_specs=(HBM, HBM),
    )(me, dest, enc_rows, pred_rows, w_dec)
    wire = exchange(wire, OUT_FIRST)
    into, out_of, home, here, table, wide, wide_bias = call(
        prep_kernel,
        "prep",
        (pick, pick, pick, out((KEPT * ROWS, ROWS), BF16), out((ROWS, ROWS), F32), out((WIDTH, WIDTH), BF16), out((1, WIDTH), F32)),
        [SM, SM] + [VM] * 5,
        flops=100000000,
        bytes_accessed=2000000,
    )(me, block_off, flat_dest, start, label_ids, w_out, bias)
    enc_joint = call(
        enter_kernel,
        "enter",
        out((ROWS, WIDTH), F32),
        [VM] * 3,
        [pltpu.VMEM((ROWS * OUT_ROWS, ROWS), F32)],
        flops=100000000,
        bytes_accessed=1000000,
    )(wire, into, w_enc)
    logprobs, hidden, dlogit, term = call(
        joint_kernel,
        "joint",
        (
            out((ROWS, 2 * KEPT), F32),
            out((KEPT * ROWS, WIDTH), BF16),
            out((KEPT * ROWS, WIDTH), BF16),
            out((CORES * WIDTH, WIDTH // CORES), BF16),
        ),
        [VM] * 11,
        [
            pltpu.VMEM((KEPT, WIDTH, ROWS), F32),
            pltpu.VMEM((WIDTH, KEPT * ROWS), BF16),
            pltpu.VMEM((KEPT * ROWS, WIDTH), F32),
            pltpu.VMEM((CORES * WIDTH, WIDTH // CORES), BF16),
            pltpu.SemaphoreType.DMA((CORES,)),
        ],
        flops=500000000,
        bytes_accessed=3000000,
        out_specs=(VM, VM, VM, HBM),
    )(enc_joint, here, dec, to_frame(dec, 1), to_frame(dec, 2), to_frame(dec, 3), table, wide, wide_bias, grad_blank, grad_label)
    term = lax.all_to_all(term, ("core", "frame"), 0, 0, tiled=True)
    rows, planes, dec0, dec1, dec2, dec3 = call(
        back_kernel,
        "back",
        (out((2 * KEPT, ROWS), F32), out((SLOTS * ROWS, WIDTH), BF16), part, part, part, part),
        [SM, SM] + [VM] * 7,
        flops=500000000,
        bytes_accessed=3000000,
    )(me, block_off, start, out_of, hidden, dlogit, w_enc, wide, logprobs)
    back = call(
        merge_kernel,
        "merge",
        out((ROWS * BACK_ROWS, ROWS), BF16),
        [VM, VM],
        [
            pltpu.VMEM((ROWS * BACK_ROWS, ROWS), F32),
            pltpu.VMEM((ROWS * BACK_ROWS, ROWS), BF16),
            pltpu.SemaphoreType.DMA((2,)),
        ],
        flops=300000,
        bytes_accessed=1700000,
        out_specs=HBM,
    )(term, planes)
    back, dec1, dec2 = lax.optimization_barrier((back, dec1, dec2))
    back = exchange(back.reshape(ROWS * BACK_ROWS // 2, 2, ROWS), BACK_FIRST)
    back = back.reshape(ROWS * BACK_ROWS, ROWS)
    grad_pred = call(
        pred_kernel,
        "pred",
        out((PART, WIDTH), F32),
        [VM] * 5,
        flops=40000000,
        bytes_accessed=700000,
    )(dec0, to_frame(dec1, 1), to_frame(dec2, 2), to_frame(dec3, 3), w_dec)
    grad_enc, grad_w_out = call(
        unpack_kernel,
        "unpack",
        (out((ROWS, WIDTH), BF16), out((1, w_out.shape[1]), F32)),
        [VM, VM],
        [
            pltpu.VMEM((ROWS * BACK_ROWS, ROWS), F32),
            pltpu.VMEM((ROWS, WIDTH), BF16),
            pltpu.VMEM((1, w_out.shape[1]), F32),
            pltpu.SemaphoreType.DMA((3,)),
        ],
        flops=40000000,
        bytes_accessed=600000,
        out_specs=(HBM, HBM),
    )(home, back)
    return (rows.T, grad_enc, grad_pred, grad_w_out)


def solution(mesh):
    fine = Mesh(mesh.devices.reshape(16, 4, 2, 4), EVERY)
    return jax.shard_map(
        shards,
        mesh=fine,
        in_specs=(
            P(EVERY, None),
            P(None, "frame", None),
            P(EVERY, None),
            P(DP, None),
            P(EVERY),
            P(EVERY),
            P(),
            P(),
            P(),
            P(),
            P(EVERY, None),
            P(EVERY, None),
        ),
        out_specs=(P(EVERY, None), P(EVERY, None), P(EVERY, None), P(EVERY, None)),
        check_vma=False,
    )
```

```python
import jax
import jax.numpy as jnp
from jax import lax
from jax.experimental import pallas as pl
from jax.experimental.pallas import tpu as pltpu
from jax.sharding import Mesh
from jax.sharding import PartitionSpec as P

F32 = jnp.float32
BF16 = jnp.bfloat16
I32 = jnp.int32

ROWS = 128
PACK = 4
SLOTS = 2
WIDTH = PACK * ROWS
KEPT = 3
BLOCK = 64
FRAMES = 4
PART = ROWS // FRAMES
OUT_ROWS = SLOTS * PACK
HALF = PACK // 2
BACK_ROWS = OUT_ROWS + HALF
CORES = 2
OUT_FIRST = 76
BACK_FIRST = 76
STEP = 64


def iota(dim, shape=(ROWS, ROWS)):
    return lax.broadcasted_iota(I32, shape, dim)


def mm(a, b):
    return jnp.dot(a, b, preferred_element_type=F32)


def mm_nt(a, b):
    return lax.dot_general(a, b, (((1,), (1,)), ((), ())), preferred_element_type=F32)


def mm_tn(a, b):
    return lax.dot_general(a, b, (((0,), (0,)), ((), ())), preferred_element_type=F32)


def to_bf(mask):
    return jnp.where(mask, 1.0, 0.0).astype(BF16)


def chunk(c):
    return slice(c * ROWS, (c + 1) * ROWS)


def member(place, first):
    return (place + first) % ROWS


def place_of(who, first):
    return (who + (ROWS - first)) % ROWS


def turned_to(array, first):
    return pltpu.roll(array, ROWS - first, 0)


def as_column(row):
    return jnp.sum(jnp.where(iota(0) == iota(1), jnp.broadcast_to(row, (ROWS, ROWS)), 0.0), axis=1, keepdims=True)


def as_row(column):
    return jnp.sum(jnp.where(iota(0) == iota(1), jnp.broadcast_to(column, (ROWS, ROWS)), 0.0), axis=0, keepdims=True)


def owner_and_rank(dest_row, first):
    dest_f = dest_row.astype(F32)
    follows = (as_column(dest_f) + 1.0) == jnp.broadcast_to(dest_f, (ROWS, ROWS))
    rank = jnp.sum(jnp.where(follows, 1.0, 0.0), axis=0, keepdims=True)
    return place_of(dest_row // ROWS, first).astype(F32), jnp.where(dest_row % ROWS == 0, 0.0, rank)


def pack_kernel(id_ref, dest_hbm, enc_hbm, pred_hbm, w_hbm, out_hbm, dec_hbm, dest_ref, enc_ref, pred_ref, w_ref, wire_ref, out_ref, dec_ref, sems):
    pairs = ((dest_hbm.at[id_ref[0] // FRAMES], dest_ref), (enc_hbm, enc_ref), (pred_hbm, pred_ref), (w_hbm, w_ref))
    copies = [pltpu.make_async_copy(src, dst, sems.at[i]) for i, (src, dst) in enumerate(pairs)]
    for copy in copies:
        copy.start()
    copies[0].wait()
    owner, rank = owner_and_rank(dest_ref[...], OUT_FIRST)
    down = iota(0).astype(F32)
    picks = [to_bf((down == owner) & (rank == float(k))) for k in range(SLOTS)]
    copies[1].wait()
    owners = ROWS // 2
    for half in range(2):
        for k in range(SLOTS):
            picked = mm(picks[k][half * owners : (half + 1) * owners], enc_ref[...])
            for c in range(PACK):
                first = half * owners * OUT_ROWS + k * PACK + c
                wire_ref[pl.ds(first, owners, stride=OUT_ROWS), :] = picked[:, chunk(c)]
        rows = slice(half * owners * OUT_ROWS, (half + 1) * owners * OUT_ROWS)
        out_ref[rows, :] = wire_ref[rows, :].astype(BF16)
        copies.append(pltpu.make_async_copy(out_ref.at[rows], out_hbm.at[rows], sems.at[len(pairs) + half]))
        copies[-1].start()
    copies[2].wait()
    copies[3].wait()
    dec_ref[...] = mm(pred_ref[...], w_ref[...]).astype(BF16)
    copies.append(pltpu.make_async_copy(dec_ref, dec_hbm, sems.at[len(pairs) + 2]))
    copies[-1].start()
    for copy in copies[len(pairs) :]:
        copy.wait()


def base_row(off_ref, start_ref):
    lane = iota(1, (1, ROWS))
    return (start_ref[...] + jnp.where(lane < BLOCK, off_ref[0], off_ref[1])).astype(F32)


def prep_kernel(
    id_ref, off_ref, dest_ref, start_ref, label_ref, w_ref, bias_ref,
    into_ref, from_ref, home_ref, here_ref, table_ref, wide_ref, bias_out_ref,
):
    mine = jnp.where(dest_ref[...] // ROWS == id_ref[0] // FRAMES, 1.0, 0.0)
    coming = turned_to(mine, OUT_FIRST).astype(BF16)
    going = turned_to(mine, BACK_FIRST).astype(BF16)
    ones = jnp.ones((ROWS, ROWS), BF16)
    count_row = mm_nt(ones, coming)
    count_col = mm(going, ones)
    earlier = member(iota(0), OUT_FIRST) < member(iota(1), OUT_FIRST)
    offset_row = mm(count_row.astype(BF16), to_bf(earlier))
    earlier = member(iota(1), BACK_FIRST) < member(iota(0), BACK_FIRST)
    offset_col = mm(to_bf(earlier), count_col.astype(BF16))
    owner, rank = owner_and_rank(dest_ref[pl.ds(id_ref[0] // FRAMES, 1), :], BACK_FIRST)
    owner = as_column(owner)
    rank = as_column(rank)
    down = iota(0).astype(F32)
    along = iota(1).astype(F32)
    for k in range(SLOTS):
        into_ref[k] = to_bf((offset_row + float(k) == down) & (count_row > float(k)))
        from_ref[k] = to_bf((offset_col + float(k) == along) & (count_col > float(k)))
        home_ref[k] = to_bf((owner == along) & (rank == float(k)))
    base = as_column(base_row(off_ref, start_ref))
    labels = label_ref[...].astype(F32)
    table = jnp.zeros((ROWS, ROWS), F32)
    frame = id_ref[0] % FRAMES
    held = (((frame + FRAMES - iota(1) // PART) % FRAMES) * PART + iota(1) % PART).astype(F32)
    for k in range(KEPT):
        here_ref[k * ROWS : (k + 1) * ROWS, :] = to_bf(held == base + float(k))
        emitted = jnp.sum(jnp.where(along == base + float(k), labels, 0.0), axis=1, keepdims=True)
        table = jnp.where(iota(1) == k, emitted, table)
    table_ref[...] = table
    vocab = w_ref.shape[1]
    wide_ref[...] = jnp.zeros_like(wide_ref)
    wide_ref[:, 0:vocab] = w_ref[...]
    bias_out_ref[...] = jnp.full_like(bias_out_ref, -1e30)
    bias_out_ref[:, 0:vocab] = bias_ref[...]


def take_slot(wire_ref, slot, rows):
    return jnp.concatenate([wire_ref[pl.ds(slot * PACK + c, ROWS, stride=rows), :] for c in range(PACK)], axis=1)


def enter_kernel(wire_ref, into_ref, w_enc_ref, out_ref, float_ref):
    float_ref[...] = wire_ref[...].astype(F32)
    owned = jnp.zeros((ROWS, WIDTH), F32)
    for k in range(SLOTS):
        owned = owned + mm(into_ref[k], take_slot(float_ref, k, OUT_ROWS).astype(BF16))
    out_ref[...] = mm(owned.astype(BF16), w_enc_ref[...])


def joint_kernel(
    enc_ref, here_ref, dec0_ref, dec1_ref, dec2_ref, dec3_ref, table_ref, w_out_ref, bias_ref,
    cot_blank_ref, cot_label_ref, logprob_ref, hidden_ref, dlogit_ref, grad_hbm, turn_ref, turned_ref, logit_ref,
    grad_ref, sems,
):
    enc_joint = enc_ref[...]
    dec = jnp.concatenate([dec0_ref[...], dec1_ref[...], dec2_ref[...], dec3_ref[...]], axis=0)
    dec_rows = mm(here_ref[...], dec)
    for k in range(KEPT):
        rows = slice(k * ROWS, (k + 1) * ROWS)
        hidden = jnp.tanh(enc_joint + dec_rows[rows, :]).astype(BF16)
        hidden_ref[rows, :] = hidden
        turn_ref[k] = hidden.astype(F32).T
        for f in range(FRAMES):
            turned_ref[chunk(f), rows] = turn_ref.at[k][pl.ds(f, ROWS, stride=FRAMES), :].astype(BF16)
    logit_ref[...] = mm(hidden_ref[...], w_out_ref[...])
    lane = iota(1, (STEP, WIDTH))
    first = iota(1, (STEP, ROWS)) == 0
    for k in range(KEPT):
        for r in range(0, ROWS, STEP):
            rows = slice(k * ROWS + r, k * ROWS + r + STEP)
            part = slice(r, r + STEP)
            logits = logit_ref[rows, :] + bias_ref[...]
            shifted = logits - jnp.max(logits, axis=1, keepdims=True)
            power = jnp.exp(shifted)
            total = jnp.sum(power, axis=1, keepdims=True)
            log_total = jnp.log(total)
            is_label = lane == table_ref[part, k : k + 1].astype(I32)
            at_label = jnp.sum(jnp.where(is_label, shifted, 0.0), axis=1, keepdims=True)
            logprob_ref[part, k : k + 1] = shifted[:, 0:1] - log_total
            logprob_ref[part, KEPT + k : KEPT + k + 1] = at_label - log_total
            cot_blank = cot_blank_ref[part, k : k + 1]
            cot_label = cot_label_ref[part, k : k + 1]
            scale = (cot_blank + cot_label) / total
            dlogit = jnp.where(is_label, cot_label, 0.0) - power * scale
            dlogit_ref[rows, chunk(0)] = (dlogit[:, chunk(0)] + jnp.where(first, cot_blank, 0.0)).astype(BF16)
            dlogit_ref[rows, ROWS:WIDTH] = dlogit[:, ROWS:WIDTH].astype(BF16)
    copies = []
    for core in range(CORES):
        half = slice(core * WIDTH, (core + 1) * WIDTH)
        columns = slice(core * HALF * ROWS, (core + 1) * HALF * ROWS)
        grad_ref[half, :] = mm(turned_ref[...], dlogit_ref[:, columns]).astype(BF16)
        copies.append(pltpu.make_async_copy(grad_ref.at[half], grad_hbm.at[half], sems.at[core]))
        copies[-1].start()
    for copy in copies:
        copy.wait()


def back_kernel(
    id_ref, off_ref, start_ref, from_ref, hidden_ref, dlogit_ref, w_enc_ref, w_out_ref, logprob_ref,
    row_ref, plane_ref, dec0_ref, dec1_ref, dec2_ref, dec3_ref,
):
    for i in range(2 * KEPT):
        row_ref[i : i + 1, :] = as_row(logprob_ref[:, i : i + 1])
    base = base_row(off_ref, start_ref)
    frame = id_ref[0] % FRAMES
    sent = (((frame + iota(0) // PART) % FRAMES) * PART + iota(0) % PART).astype(F32)
    enc_grad = jnp.zeros((ROWS, WIDTH), F32)
    dec_grad = jnp.zeros((ROWS, WIDTH), F32)
    for k in range(KEPT):
        rows = slice(k * ROWS, (k + 1) * ROWS)
        hidden = hidden_ref[rows, :].astype(F32)
        dz = mm_nt(dlogit_ref[rows, :], w_out_ref[...]) * (1.0 - hidden * hidden)
        enc_grad = enc_grad + dz
        here = to_bf(sent == base + float(k))
        high = dz.astype(BF16)
        low = (dz - high.astype(F32)).astype(BF16)
        dec_grad = dec_grad + mm(here, high) + mm(here, low)
    dec_grad = dec_grad.astype(BF16)
    for f, ref in enumerate((dec0_ref, dec1_ref, dec2_ref, dec3_ref)):
        ref[...] = dec_grad[f * PART : (f + 1) * PART, :]
    owned = mm_nt(enc_grad.astype(BF16), w_enc_ref[...]).astype(BF16)
    for k in range(SLOTS):
        plane_ref[chunk(k), :] = mm(from_ref[k], owned).astype(BF16)


def merge_kernel(parts_ref, plane_ref, out_hbm, float_ref, out_ref, sems):
    owners = ROWS // 2
    totals = []
    for h in range(HALF):
        total = parts_ref[chunk(0), chunk(h)].astype(F32)
        for i in range(1, CORES * FRAMES):
            total = total + parts_ref[chunk(i), chunk(h)].astype(F32)
        totals.append(turned_to(total, BACK_FIRST))
    copies = []
    for half in range(2):
        base = half * owners
        for k in range(SLOTS):
            for c in range(PACK):
                plane = plane_ref[k * ROWS + base : k * ROWS + base + owners, chunk(c)].astype(F32)
                float_ref[pl.ds(base * BACK_ROWS + k * PACK + c, owners, stride=BACK_ROWS), :] = plane
        for h in range(HALF):
            float_ref[pl.ds(base * BACK_ROWS + OUT_ROWS + h, owners, stride=BACK_ROWS), :] = totals[h][base : base + owners]
        rows = slice(base * BACK_ROWS, (base + owners) * BACK_ROWS)
        out_ref[rows, :] = float_ref[rows, :].astype(BF16)
        copies.append(pltpu.make_async_copy(out_ref.at[rows], out_hbm.at[rows], sems.at[half]))
        copies[-1].start()
    for copy in copies:
        copy.wait()


def pred_kernel(part0_ref, part1_ref, part2_ref, part3_ref, w_ref, out_ref):
    total = part0_ref[...].astype(F32) + part1_ref[...].astype(F32)
    total = total + (part2_ref[...].astype(F32) + part3_ref[...].astype(F32))
    high = total.astype(BF16)
    low = (total - high.astype(F32)).astype(BF16)
    out_ref[...] = mm_nt(high, w_ref[...]) + mm_nt(low, w_ref[...])


def unpack_kernel(home_ref, wire_ref, enc_hbm, grad_hbm, float_ref, enc_ref, grad_ref, sems):
    float_ref[...] = wire_ref[...].astype(F32)
    slots = [take_slot(float_ref, k, BACK_ROWS).astype(BF16) for k in range(SLOTS)]
    quarters = []
    for core in range(CORES):
        for h in range(HALF):
            first = core * BACK_ROWS + OUT_ROWS + h
            from_core = float_ref[pl.ds(first, ROWS // CORES, stride=CORES * BACK_ROWS), :]
            quarters.append(jnp.sum(from_core, axis=0, keepdims=True))
    term = jnp.concatenate(quarters, axis=1)
    grad_ref[...] = term[:, 0 : grad_ref.shape[1]]
    copies = [pltpu.make_async_copy(grad_ref, grad_hbm, sems.at[2])]
    copies[0].start()
    for half in range(2):
        part = slice(half * ROWS // 2, (half + 1) * ROWS // 2)
        rows = mm(home_ref[0, part, :], slots[0])
        for k in range(1, SLOTS):
            rows = rows + mm(home_ref[k, part, :], slots[k])
        enc_ref[part, :] = rows.astype(BF16)
        copies.append(pltpu.make_async_copy(enc_ref.at[part], enc_hbm.at[part], sems.at[half]))
        copies[-1].start()
    for copy in copies:
        copy.wait()


VM = pl.BlockSpec(memory_space=pltpu.VMEM)
SM = pl.BlockSpec(memory_space=pltpu.SMEM)
HBM = pl.BlockSpec(memory_space=pltpu.HBM)


def call(kernel, name, outs, specs, scratch=(), flops=0, bytes_accessed=0, limit=24 << 20, out_specs=None):
    return pl.pallas_call(
        kernel,
        name=name,
        out_shape=outs,
        in_specs=list(specs),
        out_specs=jax.tree.map(lambda _: VM, outs) if out_specs is None else out_specs,
        scratch_shapes=list(scratch),
        compiler_params=pltpu.CompilerParams(vmem_limit_bytes=limit),
        cost_estimate=pl.CostEstimate(flops=flops, bytes_accessed=bytes_accessed, transcendentals=0),
    )


def out(shape, dtype):
    return jax.ShapeDtypeStruct(shape, dtype)


DP = ("z", "x", "core")
EVERY = DP + ("frame",)


def exchange(array, first):
    return lax.all_to_all(array, DP, 0, 0, axis_index_groups=[[member(i, first) for i in range(ROWS)]], tiled=True)


def to_frame(array, ahead):
    return lax.ppermute(array, "frame", [(f, (f + ahead) % FRAMES) for f in range(FRAMES)])


def shards(
    enc_rows, dest, pred_rows, label_ids, block_off, band_start, w_enc, w_dec, w_out, bias_out, grad_blank, grad_label
):
    me = lax.axis_index(EVERY).astype(I32).reshape(1)
    flat_dest = dest.reshape(ROWS, ROWS)
    start = band_start.reshape(1, ROWS)
    bias = bias_out.reshape(1, -1)
    part = out((PART, WIDTH), BF16)
    pick = out((SLOTS, ROWS, ROWS), BF16)

    wire, dec = call(
        pack_kernel,
        "pack",
        (out((ROWS * OUT_ROWS, ROWS), BF16), part),
        [SM, HBM, HBM, HBM, HBM],
        [
            pltpu.VMEM((1, ROWS), I32),
            pltpu.VMEM((ROWS, WIDTH), BF16),
            pltpu.VMEM((PART, WIDTH), BF16),
            pltpu.VMEM((WIDTH, WIDTH), BF16),
            pltpu.VMEM((ROWS * OUT_ROWS, ROWS), F32),
            pltpu.VMEM((ROWS * OUT_ROWS, ROWS), BF16),
            pltpu.VMEM((PART, WIDTH), BF16),
            pltpu.SemaphoreType.DMA((7,)),
        ],
        flops=40000000,
        bytes_accessed=400000,
        limit=None,
        out_specs=(HBM, HBM),
    )(me, dest, enc_rows, pred_rows, w_dec)
    wire = exchange(wire, OUT_FIRST)
    into, out_of, home, here, table, wide, wide_bias = call(
        prep_kernel,
        "prep",
        (pick, pick, pick, out((KEPT * ROWS, ROWS), BF16), out((ROWS, ROWS), F32), out((WIDTH, WIDTH), BF16), out((1, WIDTH), F32)),
        [SM, SM] + [VM] * 5,
        flops=100000000,
        bytes_accessed=2000000,
    )(me, block_off, flat_dest, start, label_ids, w_out, bias)
    enc_joint = call(
        enter_kernel,
        "enter",
        out((ROWS, WIDTH), F32),
        [VM] * 3,
        [pltpu.VMEM((ROWS * OUT_ROWS, ROWS), F32)],
        flops=100000000,
        bytes_accessed=1000000,
    )(wire, into, w_enc)
    logprobs, hidden, dlogit, term = call(
        joint_kernel,
        "joint",
        (
            out((ROWS, 2 * KEPT), F32),
            out((KEPT * ROWS, WIDTH), BF16),
            out((KEPT * ROWS, WIDTH), BF16),
            out((CORES * WIDTH, WIDTH // CORES), BF16),
        ),
        [VM] * 11,
        [
            pltpu.VMEM((KEPT, WIDTH, ROWS), F32),
            pltpu.VMEM((WIDTH, KEPT * ROWS), BF16),
            pltpu.VMEM((KEPT * ROWS, WIDTH), F32),
            pltpu.VMEM((CORES * WIDTH, WIDTH // CORES), BF16),
            pltpu.SemaphoreType.DMA((CORES,)),
        ],
        flops=500000000,
        bytes_accessed=3000000,
        out_specs=(VM, VM, VM, HBM),
    )(enc_joint, here, dec, to_frame(dec, 1), to_frame(dec, 2), to_frame(dec, 3), table, wide, wide_bias, grad_blank, grad_label)
    term = lax.all_to_all(term, ("core", "frame"), 0, 0, tiled=True)
    rows, planes, dec0, dec1, dec2, dec3 = call(
        back_kernel,
        "back",
        (out((2 * KEPT, ROWS), F32), out((SLOTS * ROWS, WIDTH), BF16), part, part, part, part),
        [SM, SM] + [VM] * 7,
        flops=500000000,
        bytes_accessed=3000000,
    )(me, block_off, start, out_of, hidden, dlogit, w_enc, wide, logprobs)
    back = call(
        merge_kernel,
        "merge",
        out((ROWS * BACK_ROWS, ROWS), BF16),
        [VM, VM],
        [
            pltpu.VMEM((ROWS * BACK_ROWS, ROWS), F32),
            pltpu.VMEM((ROWS * BACK_ROWS, ROWS), BF16),
            pltpu.SemaphoreType.DMA((2,)),
        ],
        flops=300000,
        bytes_accessed=1700000,
        out_specs=HBM,
    )(term, planes)
    back, dec1, dec2 = lax.optimization_barrier((back, dec1, dec2))
    back = exchange(back.reshape(ROWS * BACK_ROWS // 2, 2, ROWS), BACK_FIRST)
    back = back.reshape(ROWS * BACK_ROWS, ROWS)
    grad_pred = call(
        pred_kernel,
        "pred",
        out((PART, WIDTH), F32),
        [VM] * 5,
        flops=40000000,
        bytes_accessed=700000,
    )(dec0, to_frame(dec1, 1), to_frame(dec2, 2), to_frame(dec3, 3), w_dec)
    grad_enc, grad_w_out = call(
        unpack_kernel,
        "unpack",
        (out((ROWS, WIDTH), BF16), out((1, w_out.shape[1]), F32)),
        [VM, VM],
        [
            pltpu.VMEM((ROWS * BACK_ROWS, ROWS), F32),
            pltpu.VMEM((ROWS, WIDTH), BF16),
            pltpu.VMEM((1, w_out.shape[1]), F32),
            pltpu.SemaphoreType.DMA((3,)),
        ],
        flops=40000000,
        bytes_accessed=600000,
        out_specs=(HBM, HBM),
    )(home, back)
    return (rows.T, grad_enc, grad_pred, grad_w_out)


def solution(mesh):
    fine = Mesh(mesh.devices.reshape(16, 4, 2, 4), EVERY)
    return jax.shard_map(
        shards,
        mesh=fine,
        in_specs=(
            P(EVERY, None),
            P(None, "frame", None),
            P(EVERY, None),
            P(DP, None),
            P(EVERY),
            P(EVERY),
            P(),
            P(),
            P(),
            P(),
            P(EVERY, None),
            P(EVERY, None),
        ),
        out_specs=(P(EVERY, None), P(EVERY, None), P(EVERY, None), P(EVERY, None)),
        check_vma=False,
    )
```

```python
import jax
import jax.numpy as jnp
from jax import lax
from jax.experimental import pallas as pl
from jax.experimental.pallas import tpu as pltpu
from jax.sharding import Mesh
from jax.sharding import PartitionSpec as P

F32 = jnp.float32
BF16 = jnp.bfloat16
I32 = jnp.int32

ROWS = 128
PACK = 4
SLOTS = 2
WIDTH = PACK * ROWS
KEPT = 3
BLOCK = 64
FRAMES = 4
PART = ROWS // FRAMES
OUT_ROWS = SLOTS * PACK
HALF = PACK // 2
BACK_ROWS = OUT_ROWS + HALF
CORES = 2
OUT_FIRST = 76
BACK_FIRST = 84
STEP = 64


def iota(dim, shape=(ROWS, ROWS)):
    return lax.broadcasted_iota(I32, shape, dim)


def mm(a, b):
    return jnp.dot(a, b, preferred_element_type=F32)


def mm_nt(a, b):
    return lax.dot_general(a, b, (((1,), (1,)), ((), ())), preferred_element_type=F32)


def mm_tn(a, b):
    return lax.dot_general(a, b, (((0,), (0,)), ((), ())), preferred_element_type=F32)


def to_bf(mask):
    return jnp.where(mask, 1.0, 0.0).astype(BF16)


def chunk(c):
    return slice(c * ROWS, (c + 1) * ROWS)


def member(place, first):
    return (place + first) % ROWS


def place_of(who, first):
    return (who + (ROWS - first)) % ROWS


def turned_to(array, first):
    return pltpu.roll(array, ROWS - first, 0)


def as_column(row):
    return jnp.sum(jnp.where(iota(0) == iota(1), jnp.broadcast_to(row, (ROWS, ROWS)), 0.0), axis=1, keepdims=True)


def as_row(column):
    return jnp.sum(jnp.where(iota(0) == iota(1), jnp.broadcast_to(column, (ROWS, ROWS)), 0.0), axis=0, keepdims=True)


def owner_and_rank(dest_row, first):
    dest_f = dest_row.astype(F32)
    follows = (as_column(dest_f) + 1.0) == jnp.broadcast_to(dest_f, (ROWS, ROWS))
    rank = jnp.sum(jnp.where(follows, 1.0, 0.0), axis=0, keepdims=True)
    return place_of(dest_row // ROWS, first).astype(F32), jnp.where(dest_row % ROWS == 0, 0.0, rank)


def pack_kernel(id_ref, dest_hbm, enc_hbm, pred_hbm, w_hbm, out_hbm, dec_hbm, dest_ref, enc_ref, pred_ref, w_ref, wire_ref, out_ref, dec_ref, sems):
    pairs = ((dest_hbm.at[id_ref[0] // FRAMES], dest_ref), (enc_hbm, enc_ref), (pred_hbm, pred_ref), (w_hbm, w_ref))
    copies = [pltpu.make_async_copy(src, dst, sems.at[i]) for i, (src, dst) in enumerate(pairs)]
    for copy in copies:
        copy.start()
    copies[0].wait()
    owner, rank = owner_and_rank(dest_ref[...], OUT_FIRST)
    down = iota(0).astype(F32)
    picks = [to_bf((down == owner) & (rank == float(k))) for k in range(SLOTS)]
    copies[1].wait()
    owners = ROWS // 2
    for half in range(2):
        for k in range(SLOTS):
            picked = mm(picks[k][half * owners : (half + 1) * owners], enc_ref[...])
            for c in range(PACK):
                first = half * owners * OUT_ROWS + k * PACK + c
                wire_ref[pl.ds(first, owners, stride=OUT_ROWS), :] = picked[:, chunk(c)]
        rows = slice(half * owners * OUT_ROWS, (half + 1) * owners * OUT_ROWS)
        out_ref[rows, :] = wire_ref[rows, :].astype(BF16)
        copies.append(pltpu.make_async_copy(out_ref.at[rows], out_hbm.at[rows], sems.at[len(pairs) + half]))
        copies[-1].start()
    copies[2].wait()
    copies[3].wait()
    dec_ref[...] = mm(pred_ref[...], w_ref[...]).astype(BF16)
    copies.append(pltpu.make_async_copy(dec_ref, dec_hbm, sems.at[len(pairs) + 2]))
    copies[-1].start()
    for copy in copies[len(pairs) :]:
        copy.wait()


def base_row(off_ref, start_ref):
    lane = iota(1, (1, ROWS))
    return (start_ref[...] + jnp.where(lane < BLOCK, off_ref[0], off_ref[1])).astype(F32)


def prep_kernel(
    id_ref, off_ref, dest_ref, start_ref, label_ref, w_ref, bias_ref,
    into_ref, from_ref, home_ref, here_ref, table_ref, wide_ref, bias_out_ref,
):
    mine = jnp.where(dest_ref[...] // ROWS == id_ref[0] // FRAMES, 1.0, 0.0)
    coming = turned_to(mine, OUT_FIRST).astype(BF16)
    going = turned_to(mine, BACK_FIRST).astype(BF16)
    ones = jnp.ones((ROWS, ROWS), BF16)
    count_row = mm_nt(ones, coming)
    count_col = mm(going, ones)
    earlier = member(iota(0), OUT_FIRST) < member(iota(1), OUT_FIRST)
    offset_row = mm(count_row.astype(BF16), to_bf(earlier))
    earlier = member(iota(1), BACK_FIRST) < member(iota(0), BACK_FIRST)
    offset_col = mm(to_bf(earlier), count_col.astype(BF16))
    owner, rank = owner_and_rank(dest_ref[pl.ds(id_ref[0] // FRAMES, 1), :], BACK_FIRST)
    owner = as_column(owner)
    rank = as_column(rank)
    down = iota(0).astype(F32)
    along = iota(1).astype(F32)
    for k in range(SLOTS):
        into_ref[k] = to_bf((offset_row + float(k) == down) & (count_row > float(k)))
        from_ref[k] = to_bf((offset_col + float(k) == along) & (count_col > float(k)))
        home_ref[k] = to_bf((owner == along) & (rank == float(k)))
    base = as_column(base_row(off_ref, start_ref))
    labels = label_ref[...].astype(F32)
    table = jnp.zeros((ROWS, ROWS), F32)
    frame = id_ref[0] % FRAMES
    held = (((frame + FRAMES - iota(1) // PART) % FRAMES) * PART + iota(1) % PART).astype(F32)
    for k in range(KEPT):
        here_ref[k * ROWS : (k + 1) * ROWS, :] = to_bf(held == base + float(k))
        emitted = jnp.sum(jnp.where(along == base + float(k), labels, 0.0), axis=1, keepdims=True)
        table = jnp.where(iota(1) == k, emitted, table)
    table_ref[...] = table
    vocab = w_ref.shape[1]
    wide_ref[...] = jnp.zeros_like(wide_ref)
    wide_ref[:, 0:vocab] = w_ref[...]
    bias_out_ref[...] = jnp.full_like(bias_out_ref, -1e30)
    bias_out_ref[:, 0:vocab] = bias_ref[...]


def take_slot(wire_ref, slot, rows):
    return jnp.concatenate([wire_ref[pl.ds(slot * PACK + c, ROWS, stride=rows), :] for c in range(PACK)], axis=1)


def enter_kernel(wire_ref, into_ref, w_enc_ref, out_ref, float_ref):
    float_ref[...] = wire_ref[...].astype(F32)
    owned = jnp.zeros((ROWS, WIDTH), F32)
    for k in range(SLOTS):
        owned = owned + mm(into_ref[k], take_slot(float_ref, k, OUT_ROWS).astype(BF16))
    out_ref[...] = mm(owned.astype(BF16), w_enc_ref[...])


def joint_kernel(
    enc_ref, here_ref, dec0_ref, dec1_ref, dec2_ref, dec3_ref, table_ref, w_out_ref, bias_ref,
    cot_blank_ref, cot_label_ref, logprob_ref, hidden_ref, dlogit_ref, grad_hbm, turn_ref, turned_ref, logit_ref,
    grad_ref, sems,
):
    enc_joint = enc_ref[...]
    dec = jnp.concatenate([dec0_ref[...], dec1_ref[...], dec2_ref[...], dec3_ref[...]], axis=0)
    dec_rows = mm(here_ref[...], dec)
    for k in range(KEPT):
        rows = slice(k * ROWS, (k + 1) * ROWS)
        hidden = jnp.tanh(enc_joint + dec_rows[rows, :]).astype(BF16)
        hidden_ref[rows, :] = hidden
        turn_ref[k] = hidden.astype(F32).T
        for f in range(FRAMES):
            turned_ref[chunk(f), rows] = turn_ref.at[k][pl.ds(f, ROWS, stride=FRAMES), :].astype(BF16)
    logit_ref[...] = mm(hidden_ref[...], w_out_ref[...])
    lane = iota(1, (STEP, WIDTH))
    first = iota(1, (STEP, ROWS)) == 0
    for k in range(KEPT):
        for r in range(0, ROWS, STEP):
            rows = slice(k * ROWS + r, k * ROWS + r + STEP)
            part = slice(r, r + STEP)
            logits = logit_ref[rows, :] + bias_ref[...]
            shifted = logits - jnp.max(logits, axis=1, keepdims=True)
            power = jnp.exp(shifted)
            total = jnp.sum(power, axis=1, keepdims=True)
            log_total = jnp.log(total)
            is_label = lane == table_ref[part, k : k + 1].astype(I32)
            at_label = jnp.sum(jnp.where(is_label, shifted, 0.0), axis=1, keepdims=True)
            logprob_ref[part, k : k + 1] = shifted[:, 0:1] - log_total
            logprob_ref[part, KEPT + k : KEPT + k + 1] = at_label - log_total
            cot_blank = cot_blank_ref[part, k : k + 1]
            cot_label = cot_label_ref[part, k : k + 1]
            scale = (cot_blank + cot_label) / total
            dlogit = jnp.where(is_label, cot_label, 0.0) - power * scale
            dlogit_ref[rows, chunk(0)] = (dlogit[:, chunk(0)] + jnp.where(first, cot_blank, 0.0)).astype(BF16)
            dlogit_ref[rows, ROWS:WIDTH] = dlogit[:, ROWS:WIDTH].astype(BF16)
    copies = []
    for core in range(CORES):
        half = slice(core * WIDTH, (core + 1) * WIDTH)
        columns = slice(core * HALF * ROWS, (core + 1) * HALF * ROWS)
        grad_ref[half, :] = mm(turned_ref[...], dlogit_ref[:, columns]).astype(BF16)
        copies.append(pltpu.make_async_copy(grad_ref.at[half], grad_hbm.at[half], sems.at[core]))
        copies[-1].start()
    for copy in copies:
        copy.wait()


def back_kernel(
    id_ref, off_ref, start_ref, from_ref, hidden_ref, dlogit_ref, w_enc_ref, w_out_ref, logprob_ref,
    row_ref, plane_ref, dec0_ref, dec1_ref, dec2_ref, dec3_ref,
):
    for i in range(2 * KEPT):
        row_ref[i : i + 1, :] = as_row(logprob_ref[:, i : i + 1])
    base = base_row(off_ref, start_ref)
    frame = id_ref[0] % FRAMES
    sent = (((frame + iota(0) // PART) % FRAMES) * PART + iota(0) % PART).astype(F32)
    enc_grad = jnp.zeros((ROWS, WIDTH), F32)
    dec_grad = jnp.zeros((ROWS, WIDTH), F32)
    for k in range(KEPT):
        rows = slice(k * ROWS, (k + 1) * ROWS)
        hidden = hidden_ref[rows, :].astype(F32)
        dz = mm_nt(dlogit_ref[rows, :], w_out_ref[...]) * (1.0 - hidden * hidden)
        enc_grad = enc_grad + dz
        here = to_bf(sent == base + float(k))
        high = dz.astype(BF16)
        low = (dz - high.astype(F32)).astype(BF16)
        dec_grad = dec_grad + mm(here, high) + mm(here, low)
    dec_grad = dec_grad.astype(BF16)
    for f, ref in enumerate((dec0_ref, dec1_ref, dec2_ref, dec3_ref)):
        ref[...] = dec_grad[f * PART : (f + 1) * PART, :]
    owned = mm_nt(enc_grad.astype(BF16), w_enc_ref[...]).astype(BF16)
    for k in range(SLOTS):
        plane_ref[chunk(k), :] = mm(from_ref[k], owned).astype(BF16)


def merge_kernel(parts_ref, plane_ref, out_hbm, float_ref, out_ref, sems):
    owners = ROWS // 2
    totals = []
    for h in range(HALF):
        total = parts_ref[chunk(0), chunk(h)].astype(F32)
        for i in range(1, CORES * FRAMES):
            total = total + parts_ref[chunk(i), chunk(h)].astype(F32)
        totals.append(turned_to(total, BACK_FIRST))
    copies = []
    for half in range(2):
        base = half * owners
        for k in range(SLOTS):
            for c in range(PACK):
                plane = plane_ref[k * ROWS + base : k * ROWS + base + owners, chunk(c)].astype(F32)
                float_ref[pl.ds(base * BACK_ROWS + k * PACK + c, owners, stride=BACK_ROWS), :] = plane
        for h in range(HALF):
            float_ref[pl.ds(base * BACK_ROWS + OUT_ROWS + h, owners, stride=BACK_ROWS), :] = totals[h][base : base + owners]
        rows = slice(base * BACK_ROWS, (base + owners) * BACK_ROWS)
        out_ref[rows, :] = float_ref[rows, :].astype(BF16)
        copies.append(pltpu.make_async_copy(out_ref.at[rows], out_hbm.at[rows], sems.at[half]))
        copies[-1].start()
    for copy in copies:
        copy.wait()


def pred_kernel(part0_ref, part1_ref, part2_ref, part3_ref, w_ref, out_ref):
    total = part0_ref[...].astype(F32) + part1_ref[...].astype(F32)
    total = total + (part2_ref[...].astype(F32) + part3_ref[...].astype(F32))
    high = total.astype(BF16)
    low = (total - high.astype(F32)).astype(BF16)
    out_ref[...] = mm_nt(high, w_ref[...]) + mm_nt(low, w_ref[...])


def unpack_kernel(home_ref, wire_ref, enc_hbm, grad_hbm, float_ref, enc_ref, grad_ref, sems):
    float_ref[...] = wire_ref[...].astype(F32)
    slots = [take_slot(float_ref, k, BACK_ROWS).astype(BF16) for k in range(SLOTS)]
    quarters = []
    for core in range(CORES):
        for h in range(HALF):
            first = core * BACK_ROWS + OUT_ROWS + h
            from_core = float_ref[pl.ds(first, ROWS // CORES, stride=CORES * BACK_ROWS), :]
            quarters.append(jnp.sum(from_core, axis=0, keepdims=True))
    term = jnp.concatenate(quarters, axis=1)
    grad_ref[...] = term[:, 0 : grad_ref.shape[1]]
    copies = [pltpu.make_async_copy(grad_ref, grad_hbm, sems.at[2])]
    copies[0].start()
    for half in range(2):
        part = slice(half * ROWS // 2, (half + 1) * ROWS // 2)
        rows = mm(home_ref[0, part, :], slots[0])
        for k in range(1, SLOTS):
            rows = rows + mm(home_ref[k, part, :], slots[k])
        enc_ref[part, :] = rows.astype(BF16)
        copies.append(pltpu.make_async_copy(enc_ref.at[part], enc_hbm.at[part], sems.at[half]))
        copies[-1].start()
    for copy in copies:
        copy.wait()


VM = pl.BlockSpec(memory_space=pltpu.VMEM)
SM = pl.BlockSpec(memory_space=pltpu.SMEM)
HBM = pl.BlockSpec(memory_space=pltpu.HBM)


def call(kernel, name, outs, specs, scratch=(), flops=0, bytes_accessed=0, limit=24 << 20, out_specs=None):
    return pl.pallas_call(
        kernel,
        name=name,
        out_shape=outs,
        in_specs=list(specs),
        out_specs=jax.tree.map(lambda _: VM, outs) if out_specs is None else out_specs,
        scratch_shapes=list(scratch),
        compiler_params=pltpu.CompilerParams(vmem_limit_bytes=limit),
        cost_estimate=pl.CostEstimate(flops=flops, bytes_accessed=bytes_accessed, transcendentals=0),
    )


def out(shape, dtype):
    return jax.ShapeDtypeStruct(shape, dtype)


DP = ("z", "x", "core")
EVERY = DP + ("frame",)


def exchange(array, first):
    return lax.all_to_all(array, DP, 0, 0, axis_index_groups=[[member(i, first) for i in range(ROWS)]], tiled=True)


def to_frame(array, ahead):
    return lax.ppermute(array, "frame", [(f, (f + ahead) % FRAMES) for f in range(FRAMES)])


def shards(
    enc_rows, dest, pred_rows, label_ids, block_off, band_start, w_enc, w_dec, w_out, bias_out, grad_blank, grad_label
):
    me = lax.axis_index(EVERY).astype(I32).reshape(1)
    flat_dest = dest.reshape(ROWS, ROWS)
    start = band_start.reshape(1, ROWS)
    bias = bias_out.reshape(1, -1)
    part = out((PART, WIDTH), BF16)
    pick = out((SLOTS, ROWS, ROWS), BF16)

    wire, dec = call(
        pack_kernel,
        "pack",
        (out((ROWS * OUT_ROWS, ROWS), BF16), part),
        [SM, HBM, HBM, HBM, HBM],
        [
            pltpu.VMEM((1, ROWS), I32),
            pltpu.VMEM((ROWS, WIDTH), BF16),
            pltpu.VMEM((PART, WIDTH), BF16),
            pltpu.VMEM((WIDTH, WIDTH), BF16),
            pltpu.VMEM((ROWS * OUT_ROWS, ROWS), F32),
            pltpu.VMEM((ROWS * OUT_ROWS, ROWS), BF16),
            pltpu.VMEM((PART, WIDTH), BF16),
            pltpu.SemaphoreType.DMA((7,)),
        ],
        flops=40000000,
        bytes_accessed=400000,
        limit=None,
        out_specs=(HBM, HBM),
    )(me, dest, enc_rows, pred_rows, w_dec)
    wire = exchange(wire, OUT_FIRST)
    into, out_of, home, here, table, wide, wide_bias = call(
        prep_kernel,
        "prep",
        (pick, pick, pick, out((KEPT * ROWS, ROWS), BF16), out((ROWS, ROWS), F32), out((WIDTH, WIDTH), BF16), out((1, WIDTH), F32)),
        [SM, SM] + [VM] * 5,
        flops=100000000,
        bytes_accessed=2000000,
    )(me, block_off, flat_dest, start, label_ids, w_out, bias)
    enc_joint = call(
        enter_kernel,
        "enter",
        out((ROWS, WIDTH), F32),
        [VM] * 3,
        [pltpu.VMEM((ROWS * OUT_ROWS, ROWS), F32)],
        flops=100000000,
        bytes_accessed=1000000,
    )(wire, into, w_enc)
    logprobs, hidden, dlogit, term = call(
        joint_kernel,
        "joint",
        (
            out((ROWS, 2 * KEPT), F32),
            out((KEPT * ROWS, WIDTH), BF16),
            out((KEPT * ROWS, WIDTH), BF16),
            out((CORES * WIDTH, WIDTH // CORES), BF16),
        ),
        [VM] * 11,
        [
            pltpu.VMEM((KEPT, WIDTH, ROWS), F32),
            pltpu.VMEM((WIDTH, KEPT * ROWS), BF16),
            pltpu.VMEM((KEPT * ROWS, WIDTH), F32),
            pltpu.VMEM((CORES * WIDTH, WIDTH // CORES), BF16),
            pltpu.SemaphoreType.DMA((CORES,)),
        ],
        flops=500000000,
        bytes_accessed=3000000,
        out_specs=(VM, VM, VM, HBM),
    )(enc_joint, here, dec, to_frame(dec, 1), to_frame(dec, 2), to_frame(dec, 3), table, wide, wide_bias, grad_blank, grad_label)
    term = lax.all_to_all(term, ("core", "frame"), 0, 0, tiled=True)
    rows, planes, dec0, dec1, dec2, dec3 = call(
        back_kernel,
        "back",
        (out((2 * KEPT, ROWS), F32), out((SLOTS * ROWS, WIDTH), BF16), part, part, part, part),
        [SM, SM] + [VM] * 7,
        flops=500000000,
        bytes_accessed=3000000,
    )(me, block_off, start, out_of, hidden, dlogit, w_enc, wide, logprobs)
    back = call(
        merge_kernel,
        "merge",
        out((ROWS * BACK_ROWS, ROWS), BF16),
        [VM, VM],
        [
            pltpu.VMEM((ROWS * BACK_ROWS, ROWS), F32),
            pltpu.VMEM((ROWS * BACK_ROWS, ROWS), BF16),
            pltpu.SemaphoreType.DMA((2,)),
        ],
        flops=300000,
        bytes_accessed=1700000,
        out_specs=HBM,
    )(term, planes)
    back, dec1, dec2 = lax.optimization_barrier((back, dec1, dec2))
    back = exchange(back.reshape(ROWS * BACK_ROWS // 2, 2, ROWS), BACK_FIRST)
    back = back.reshape(ROWS * BACK_ROWS, ROWS)
    grad_pred = call(
        pred_kernel,
        "pred",
        out((PART, WIDTH), F32),
        [VM] * 5,
        flops=40000000,
        bytes_accessed=700000,
    )(dec0, to_frame(dec1, 1), to_frame(dec2, 2), to_frame(dec3, 3), w_dec)
    grad_enc, grad_w_out = call(
        unpack_kernel,
        "unpack",
        (out((ROWS, WIDTH), BF16), out((1, w_out.shape[1]), F32)),
        [VM, VM],
        [
            pltpu.VMEM((ROWS * BACK_ROWS, ROWS), F32),
            pltpu.VMEM((ROWS, WIDTH), BF16),
            pltpu.VMEM((1, w_out.shape[1]), F32),
            pltpu.SemaphoreType.DMA((3,)),
        ],
        flops=40000000,
        bytes_accessed=600000,
        out_specs=(HBM, HBM),
    )(home, back)
    return (rows.T, grad_enc, grad_pred, grad_w_out)


def solution(mesh):
    fine = Mesh(mesh.devices.reshape(16, 4, 2, 4), EVERY)
    return jax.shard_map(
        shards,
        mesh=fine,
        in_specs=(
            P(EVERY, None),
            P(None, "frame", None),
            P(EVERY, None),
            P(DP, None),
            P(EVERY),
            P(EVERY),
            P(),
            P(),
            P(),
            P(),
            P(EVERY, None),
            P(EVERY, None),
        ),
        out_specs=(P(EVERY, None), P(EVERY, None), P(EVERY, None), P(EVERY, None)),
        check_vma=False,
    )
```
